32 devices in a mesh: groups: 2 (over x), seq: 16 (over z, y, core).
Axes of the slice: x: 2, y: 2, z: 4, core: 2. Of those that a mesh axis runs over, the one named last changes fastest.
Arguments:
- query_rows: bfloat16 [1536, 4096], P(('groups', 'seq')), parts along dimension 0, may hold values from -160 to 160
- key_rows: bfloat16 [1536, 4096], P(('groups', 'seq')), parts along dimension 0, may hold values from -8 to 8
- value_rows: bfloat16 [1536, 4096], P(('groups', 'seq')), parts along dimension 0, may hold values from -6 to 6
- proj_weight: bfloat16 [4096, 128], replicated, may hold values from -0.09375 to 0.09375
- in_weight: bfloat16 [3, 3, 3, 128, 512], replicated, may hold values from -0.109375 to 0.109375
- in_bias: float32 [512], replicated, may hold values from -3 to 3
- mid_weight: bfloat16 [3, 3, 3, 512, 512], P(None, None, None, None, 'seq'), may hold values from -0.0546875 to 0.0546875
- mid_bias: float32 [512], replicated, may hold values from -3 to 3
Outputs:
- upsampled: bfloat16 [32, 2, 2, 48, 128], P(('groups', 'seq')), parts along dimension 0
The draws below stay inside these ranges and needn't reach their ends.
There are 2 independent parts, one for each index of `groups`. The reference program is written for one: setup_inputs(seed, part) draws one part's arguments, and reference() takes and returns one part's arrays. A program takes and returns all parts, laid end to end along the dimension named above; an argument that names none is the same for every part. Nothing has to cross between parts.
All inputs are finite; a program needn't handle non-finite values.
Results may differ from the reference program's by a relative error of at most 0.01.
Values may be sent and summed in bfloat16 or wider, within the bound.
No kernel may reach another device: no remote copies, remote signals or barrier semaphores. Data moves between devices by JAX's collectives and lax.ppermute only.
A program may use at most 128 MiB of HBM per device.

```python
import math
import jax
import jax.numpy as jnp
from jax import lax

D = 4096
HEADS = 32
HD = 128
C_LAT = 128
CH = 512
W = 24
F = 2
HT = 1
TILES = 16
H = 16
TOKENS = 768


def paired_draw(key):
    key_part = jax.random.normal(jax.random.fold_in(key, 31), (TOKENS, D), jnp.float32)
    query_part = jax.random.normal(jax.random.fold_in(key, 37), (TOKENS, D), jnp.float32)
    return (jnp.clip(query_part, -160.0, 160.0), jnp.clip(key_part, -8.0, 8.0))


def draw_query_rows(key, part):
    return paired_draw(key)[0].astype(jnp.bfloat16)


def draw_key_rows(key, part):
    return paired_draw(key)[1].astype(jnp.bfloat16)


def block_levels(own_key, extent, cuts, smallest, high):
    gain = 1.0
    for dim, blocks in cuts:
        steps = jax.random.uniform(jax.random.fold_in(jax.random.fold_in(own_key, 6), dim), (blocks,), jnp.float32, smallest / len(cuts), high / len(cuts))
        gain = gain * jnp.repeat(jnp.exp(steps), extent[dim] // blocks).reshape((-1,) + (1,) * (len(extent) - 1 - dim))
    return gain


def scatter_about(key, dims, width, reach, cuts=(), kind=jnp.bfloat16):
    loudness = block_levels(key, dims, cuts, -0.22, 0.18) if cuts else 1.0
    values = jax.random.normal(key, dims, jnp.float32) * width * loudness
    return jnp.minimum(jnp.maximum(values, -reach), reach).astype(kind)


def setup_inputs(seed: int = 0, part: int = 0) -> dict:
    arg_keys = jax.random.split(jax.random.key(seed), 9)
    part_keys = jax.random.split(jax.random.fold_in(arg_keys[8], part), 9)
    query_rows = draw_query_rows(jax.random.fold_in(jax.random.fold_in(arg_keys[8], part), 71), part)
    key_rows = draw_key_rows(jax.random.fold_in(jax.random.fold_in(arg_keys[8], part), 71), part)
    value_rows = scatter_about(part_keys[2], (TOKENS, D), 1.0, 6.0, ((0, 16),))
    proj_weight = scatter_about(arg_keys[3], (D, C_LAT), D ** -0.5, 0.09375)
    in_weight = scatter_about(arg_keys[4], (3, 3, 3, C_LAT, CH), (27 * C_LAT) ** -0.5, 0.109375)
    in_bias = scatter_about(arg_keys[5], (CH,), 0.5, 3.0, (), jnp.float32)
    mid_weight = scatter_about(arg_keys[6], (3, 3, 3, CH, CH), (27 * CH) ** -0.5, 0.0546875, ((4, 16),))
    mid_bias = scatter_about(arg_keys[7], (CH,), 0.5, 3.0, (), jnp.float32)
    return dict(query_rows=query_rows, key_rows=key_rows, value_rows=value_rows, proj_weight=proj_weight, in_weight=in_weight, in_bias=in_bias, mid_weight=mid_weight, mid_bias=mid_bias)


def head_attention(operands):
    query_head, key_head, value_head = operands
    score_scale = 1.0 / math.sqrt(HD)
    scores = jnp.einsum('qd,kd->qk', query_head.astype(jnp.float32), key_head.astype(jnp.float32)) * score_scale
    largest = lax.optimization_barrier(jnp.max(scores, axis=1, keepdims=True))
    weights = jnp.exp(scores - largest)
    totals = lax.optimization_barrier(jnp.sum(weights, axis=1, keepdims=True))
    rounded = lax.optimization_barrier(weights.astype(jnp.bfloat16)).astype(jnp.float32)
    mixture = jnp.einsum('qk,kd->qd', rounded, value_head.astype(jnp.float32))
    return (mixture / totals).astype(jnp.bfloat16)

def unfold(padded, frames, height, columns):
    pieces = [padded[frame_off:frame_off + frames, row_off:row_off + height, col_off:col_off + columns] for frame_off in range(3) for row_off in range(3) for col_off in range(3)]
    return jnp.concatenate(pieces, axis=-1).reshape(frames * height * columns, -1)

def reference(query_rows, key_rows, value_rows, proj_weight, in_weight, in_bias, mid_weight, mid_bias):

    def split_heads(rows):
        return rows.reshape(TOKENS, HEADS, HD).transpose(1, 0, 2)
    attended = lax.map(head_attention, (split_heads(query_rows), split_heads(key_rows), split_heads(value_rows)))
    attended = attended.transpose(1, 0, 2).reshape(TOKENS, D).astype(jnp.float32)
    normed = (attended * lax.rsqrt(lax.optimization_barrier(jnp.mean(attended * attended, axis=1, keepdims=True)) + 1e-06)).astype(jnp.bfloat16)
    latents = jnp.dot(normed, proj_weight, preferred_element_type=jnp.float32).astype(jnp.bfloat16)
    grid_cells = latents.reshape(F, H, W, C_LAT)
    padded = jnp.pad(grid_cells, ((1, 1), (1, 1), (1, 1), (0, 0)))
    first = (jnp.dot(unfold(padded, F, H, W), in_weight.reshape(27 * C_LAT, CH), preferred_element_type=jnp.float32) + in_bias).astype(jnp.bfloat16)
    active = jax.nn.silu(first.astype(jnp.float32)).astype(jnp.bfloat16)
    padded_act = jnp.pad(active.reshape(F, H, W, CH), ((1, 1), (1, 1), (1, 1), (0, 0)))
    middle = (jnp.dot(unfold(padded_act, F, H, W), mid_weight.reshape(27 * CH, CH), preferred_element_type=jnp.float32) + mid_bias).astype(jnp.bfloat16)
    summed = first.astype(jnp.float32) + middle.astype(jnp.float32)
    shuffled = summed.reshape(F, H, W, C_LAT, 2, 2).transpose(0, 1, 4, 2, 5, 3).reshape(F, 2 * H, 2 * W, C_LAT)
    tiles = shuffled.reshape(F, TILES, 2 * HT, 2 * W, C_LAT).transpose(1, 0, 2, 3, 4)
    return tiles.astype(jnp.bfloat16)
```

```python
import math

import jax
import jax.numpy as jnp
from jax import lax
from jax.experimental import pallas as pl
from jax.experimental.pallas import tpu as pltpu
from jax.sharding import PartitionSpec as P

D = 4096
HEADS = 32
HD = 128
C_LAT = 128
CH = 512
W = 24
F = 2
HT = 1


def padded_2(block, sides, width):
    for axis, dim in sides:
        count = lax.axis_size(axis)
        forward = [(i, i + 1) for i in range(count - 1)]
        backward = [(target, source) for source, target in forward]
        low = lax.ppermute(
            lax.slice_in_dim(block, block.shape[dim] - width, None, axis=dim), axis, forward
        )
        high = lax.ppermute(lax.slice_in_dim(block, 0, width, axis=dim), axis, backward)
        block = jnp.concatenate([low, block, high], axis=dim)
    return block


def unfold(padded, frames, height, columns):
    pieces = [
        padded[
            frame_off : frame_off + frames, row_off : row_off + height, col_off : col_off + columns
        ]
        for frame_off in range(3)
        for row_off in range(3)
        for col_off in range(3)
    ]
    return jnp.concatenate(pieces, axis=-1).reshape(frames * height * columns, -1)


def normed_latents(token_rows, proj_weight):
    widened = token_rows.astype(jnp.float32)
    normed = (
        widened * lax.rsqrt(jnp.mean(widened * widened, axis=1, keepdims=True) + 1e-06)
    ).astype(jnp.bfloat16)
    return jnp.dot(normed, proj_weight, preferred_element_type=jnp.float32).astype(jnp.bfloat16)


def extend(tile_cells):
    bordered = padded_2(tile_cells, (("seq", 1),), 1)
    return jnp.pad(bordered, ((1, 1), (0, 0), (1, 1), (0, 0)))


def shuffle_tile(summed, frames, height, columns):
    channels = summed.shape[-1] // 4
    return (
        summed.reshape(frames, height, columns, channels, 2, 2)
        .transpose(0, 1, 4, 2, 5, 3)
        .reshape(frames, 2 * height, 2 * columns, channels)
    )


def shared_heads(
    query_rows, key_rows, value_rows, proj_weight, in_weight, in_bias, mid_weight, mid_bias
):
    devices = lax.axis_size("seq")
    halves = max(1, devices // HEADS)
    unit_count = HEADS * halves // devices
    local_tokens = query_rows.shape[0]
    shard_rows = local_tokens // W
    half_width = W // halves
    score_scale = 1.0 / math.sqrt(HD)

    def by_head(rows):
        shaped = rows.reshape(local_tokens, HEADS, HD).transpose(1, 0, 2)
        shaped = jnp.broadcast_to(shaped[:, None], (HEADS, halves, local_tokens, HD))
        return shaped.reshape(devices, unit_count, local_tokens, HD)

    shaped = query_rows.reshape(shard_rows, halves, half_width, HEADS, HD).transpose(3, 1, 0, 2, 4)
    query_units = lax.all_to_all(
        shaped.reshape(devices, unit_count, shard_rows, half_width, HD),
        "seq",
        split_axis=0,
        concat_axis=0,
        tiled=True,
    )
    key_units = lax.all_to_all(by_head(key_rows), "seq", split_axis=0, concat_axis=0, tiled=True)
    value_units = lax.all_to_all(
        by_head(value_rows), "seq", split_axis=0, concat_axis=0, tiled=True
    )
    key_heads = key_units.transpose(1, 0, 2, 3).reshape(unit_count, -1, HD)
    value_heads = value_units.transpose(1, 0, 2, 3).reshape(unit_count, -1, HD)
    query_total = devices * shard_rows * half_width
    block_rows = 512 if query_total % 512 == 0 else query_total
    query_heads = (
        query_units.transpose(1, 0, 2, 3, 4)
        .reshape(unit_count, query_total // block_rows, block_rows, HD)
        .transpose(1, 0, 2, 3)
    )

    def attend(query_block):
        scores = (
            jnp.einsum("uqd,ukd->uqk", query_block, key_heads, preferred_element_type=jnp.float32)
            * score_scale
        )
        largest = jnp.max(scores, axis=2, keepdims=True)
        weights = jnp.exp(scores - largest)
        totals = jnp.sum(weights, axis=2, keepdims=True)
        mixture = jnp.einsum(
            "uqk,ukd->uqd",
            weights.astype(jnp.bfloat16),
            value_heads,
            preferred_element_type=jnp.float32,
        )
        return (mixture / totals).astype(jnp.bfloat16)

    attended = lax.map(attend, query_heads)
    attended = attended.transpose(1, 0, 2, 3).reshape(
        unit_count, devices, shard_rows, half_width, HD
    )
    arranged = attended.reshape(unit_count, F, devices, HT, half_width, HD).transpose(
        2, 0, 1, 3, 4, 5
    )
    arrived = lax.all_to_all(arranged, "seq", split_axis=0, concat_axis=0, tiled=True)
    arrived = arrived.reshape(HEADS, halves, F, HT, half_width, HD).transpose(2, 3, 1, 4, 0, 5)
    latents = normed_latents(arrived.reshape(F * HT * W, D), proj_weight).reshape(F, HT, W, C_LAT)
    unfolded_in = unfold(extend(latents), F, HT, W)
    first = (
        jnp.dot(unfolded_in, in_weight.reshape(27 * C_LAT, CH), preferred_element_type=jnp.float32)
        + in_bias
    ).astype(jnp.bfloat16)
    active = jax.nn.silu(first.astype(jnp.float32)).astype(jnp.bfloat16)
    unfolded_mid = unfold(extend(active.reshape(F, HT, W, CH)), F, HT, W)
    piece = lax.all_gather(mid_weight, "seq", axis=4, tiled=True)
    column_span = piece.shape[4]
    middle = (
        jnp.dot(
            unfolded_mid, piece.reshape(27 * CH, column_span), preferred_element_type=jnp.float32
        )
        + mid_bias
    ).astype(jnp.bfloat16)
    summed = first.astype(jnp.float32) + middle.astype(jnp.float32)
    return shuffle_tile(summed, F, HT, W).astype(jnp.bfloat16)[None]


def dot_f32(left, right, left_dim=1, right_dim=0):
    return lax.dot_general(
        left, right, (((left_dim,), (right_dim,)), ((), ())), preferred_element_type=jnp.float32
    )


def pack_body(query_ref, key_ref, value_ref, out_ref):
    devices, _, _, span = out_ref.shape
    for which, ref in enumerate((query_ref, key_ref, value_ref)):
        for target in range(devices):
            out_ref[target, which] = ref[:, target * span : (target + 1) * span]


def attend_body(rank_ref, rows_ref, proj_ref, out_ref, proj_buf, proj_sem):
    devices, _, local, span = rows_ref.shape
    tokens = devices * local
    start = pl.multiple_of(rank_ref[0] * span, span)
    copy = pltpu.make_async_copy(proj_ref.at[pl.ds(start, span), :], proj_buf, proj_sem)
    copy.start()
    query = rows_ref[:, 0].reshape(tokens, span)
    key = rows_ref[:, 1].reshape(tokens, span)
    value = rows_ref[:, 2].reshape(tokens, span)
    score_scale = 1.0 / math.sqrt(HD)
    heads = []
    for unit in range(span // HD):
        lanes = slice(unit * HD, (unit + 1) * HD)
        scores = dot_f32(query[:, lanes], key[:, lanes], 1, 1) * score_scale
        largest = jnp.max(scores, axis=1, keepdims=True)
        weights = jnp.exp(scores - largest)
        totals = jnp.sum(weights, axis=1, keepdims=True)
        mixture = dot_f32(weights.astype(jnp.bfloat16), value[:, lanes])
        heads.append((mixture / totals).astype(jnp.bfloat16))
    attended = jnp.concatenate(heads, axis=1)
    widened = attended.astype(jnp.float32)
    squares = jnp.sum(widened * widened, axis=1, keepdims=True)
    copy.wait()
    partial = dot_f32(attended, proj_buf[...])
    out_ref[:, :local, :] = partial.reshape(devices, local, C_LAT).astype(jnp.bfloat16)
    lane = lax.broadcasted_iota(jnp.int32, (devices, local, C_LAT), 2)
    row = lax.broadcasted_iota(jnp.int32, (devices, local, C_LAT), 1)
    spread = jnp.broadcast_to(squares, (tokens, C_LAT)).reshape(devices, local, C_LAT)
    across = jnp.sum(jnp.where(lane == row, spread, 0.0), axis=1, keepdims=True)
    coarse = across.astype(jnp.bfloat16).astype(jnp.float32)
    extra = out_ref.shape[1] - local
    line = lax.broadcasted_iota(jnp.int32, (devices, extra, C_LAT), 1)
    tail = jnp.where(line == 0, coarse, jnp.where(line == 1, across - coarse, 0.0))
    out_ref[:, local:, :] = tail.astype(jnp.bfloat16)


def latents_body(parts_ref, out_ref):
    devices, local, _ = out_ref.shape
    total = jnp.sum(parts_ref[:, :local, :].astype(jnp.float32), axis=0)
    tail = jnp.sum(parts_ref[:, local:, :].astype(jnp.float32), axis=0)
    across = tail[0:1] + tail[1:2]
    lane = lax.broadcasted_iota(jnp.int32, (local, C_LAT), 1)
    row = lax.broadcasted_iota(jnp.int32, (local, C_LAT), 0)
    squares = jnp.sum(jnp.where(lane == row, across, 0.0), axis=1, keepdims=True)
    latents = (total * lax.rsqrt(squares / D + 1e-06)).astype(jnp.bfloat16)
    for target in range(devices):
        out_ref[target] = latents


def convolve_body(
    rank_ref, latents_ref, in_weight_ref, in_bias_ref, mid_weight_ref, mid_bias_ref, out_ref, cols
):
    frame = latents_ref.shape[0] // F
    own = mid_weight_ref.shape[1] // 9
    column = lax.broadcasted_iota(jnp.int32, (frame, C_LAT), 0) % W
    for index in range(F):
        cells = latents_ref[index * frame : (index + 1) * frame, :].astype(jnp.float32)
        shifted = (
            jnp.where(column == 0, 0.0, pltpu.roll(cells, 1, 0)),
            cells,
            jnp.where(column == W - 1, 0.0, pltpu.roll(cells, frame - 1, 0)),
        )
        blank = jnp.zeros((W, C_LAT), jnp.float32)
        for col_off, moved in enumerate(shifted):
            above = jnp.concatenate([blank, moved[:-W]], axis=0)
            below = jnp.concatenate([moved[W:], blank], axis=0)
            for row_off, piece in enumerate((above, moved, below)):
                at = ((index * 3 + row_off) * 3 + col_off) * C_LAT
                cols[:, at : at + C_LAT] = piece.astype(jnp.bfloat16)
    deep = 9 * C_LAT
    firsts = []
    actives = []
    for index in range(F):
        low = (F - 1 - index) * deep
        first = (
            dot_f32(cols[...], in_weight_ref[low : low + F * deep, :]) + in_bias_ref[...]
        ).astype(jnp.bfloat16)
        wide = first.astype(jnp.float32)
        firsts.append(first)
        actives.append((wide / (1.0 + jnp.exp(-wide))).astype(jnp.bfloat16))
    channel = lax.broadcasted_iota(jnp.int32, (own, CH), 1)
    mine = channel == lax.broadcasted_iota(jnp.int32, (own, CH), 0) + rank_ref[0] * own
    bias = jnp.sum(jnp.where(mine, mid_bias_ref[...], 0.0), axis=1, keepdims=True)
    chosen = jnp.where(mine, 1.0, 0.0).astype(jnp.bfloat16)
    spot = lax.broadcasted_iota(jnp.int32, (own, frame), 1)
    spot_column = spot % W
    outs = []
    for index in range(F):
        taps = sum(
            dot_f32(mid_weight_ref[source - index + 1], actives[source], 1, 1)
            for source in range(F)
        )
        total = None
        for col_off in range(3):
            merged = None
            for row_off in range(3):
                at = (row_off * 3 + col_off) * own
                piece = taps[at : at + own, :]
                if row_off == 0:
                    piece = jnp.where(spot < W, 0.0, pltpu.roll(piece, W, 1))
                elif row_off == 2:
                    piece = jnp.where(spot >= frame - W, 0.0, pltpu.roll(piece, frame - W, 1))
                merged = piece if merged is None else merged + piece
            if col_off == 0:
                merged = jnp.where(spot_column == 0, 0.0, pltpu.roll(merged, 1, 1))
            elif col_off == 2:
                merged = jnp.where(spot_column == W - 1, 0.0, pltpu.roll(merged, frame - 1, 1))
            total = merged if total is None else total + merged
        middle = (total + bias).astype(jnp.bfloat16).astype(jnp.float32)
        outs.append((dot_f32(chosen, firsts[index], 1, 1) + middle).astype(jnp.bfloat16))
    stacked = jnp.concatenate(outs, axis=0)
    source = lax.broadcasted_iota(jnp.int32, (F * own, 128), 0)
    target = lax.broadcasted_iota(jnp.int32, (F * own, 128), 1)
    inner = source % own
    place = (source // own) * own + (inner % 4) * (own // 4) + inner // 4
    moves = jnp.where(place == target, 1.0, 0.0).astype(jnp.bfloat16)
    out_ref[...] = dot_f32(stacked, moves, 0, 0).astype(jnp.bfloat16)


def shuffle_body(rows_ref, out_ref, wide):
    devices = rows_ref.shape[0] // W
    share = C_LAT // devices
    rows = rows_ref[...].astype(jnp.float32)
    lane = lax.broadcasted_iota(jnp.int32, (W, 128), 1) // share
    for index in range(F):
        for part in range(4):
            origin = (index * 4 + part) * share
            total = None
            for source in range(devices):
                block = rows[source * W : (source + 1) * W, :]
                moved = pltpu.roll(block, (source * share - origin) % 128, 1)
                total = moved if total is None else jnp.where(lane == source, moved, total)
            wide[index, part // 2, pl.ds(part % 2, W, stride=2), :] = total
    out_ref[0] = wide[...].astype(jnp.bfloat16)


def vmem(count):
    return [pl.BlockSpec(memory_space=pltpu.VMEM)] * count


def exchange(blocks):
    return lax.all_to_all(blocks, "seq", split_axis=0, concat_axis=0, tiled=True)


def whole_heads(
    query_rows, key_rows, value_rows, proj_weight, in_weight, in_bias, mid_weight, mid_bias
):
    devices = lax.axis_size("seq")
    local = query_rows.shape[0]
    span = D // devices
    frame = devices * local // F
    own = mid_weight.shape[4]
    rank = lax.axis_index("seq").reshape(1).astype(jnp.int32)
    scalar = pl.BlockSpec(memory_space=pltpu.SMEM)
    packed = pl.pallas_call(
        pack_body,
        out_shape=jax.ShapeDtypeStruct((devices, 3, local, span), jnp.bfloat16),
        in_specs=vmem(3),
        out_specs=vmem(1)[0],
        name="pack",
    )(query_rows, key_rows, value_rows)
    rows = exchange(packed)
    parts = pl.pallas_call(
        attend_body,
        out_shape=jax.ShapeDtypeStruct((devices, local + 16, C_LAT), jnp.bfloat16),
        in_specs=[scalar, vmem(1)[0], pl.BlockSpec(memory_space=pl.ANY)],
        out_specs=vmem(1)[0],
        scratch_shapes=[pltpu.VMEM((span, C_LAT), jnp.bfloat16), pltpu.SemaphoreType.DMA(())],
        name="attend",
    )(rank, rows, proj_weight)
    parts = exchange(parts)
    copies = pl.pallas_call(
        latents_body,
        out_shape=jax.ShapeDtypeStruct((devices, local, C_LAT), jnp.bfloat16),
        in_specs=vmem(1),
        out_specs=vmem(1)[0],
        name="latents",
    )(parts)
    latents = exchange(copies).reshape(devices * local, C_LAT)
    columns = pl.pallas_call(
        convolve_body,
        out_shape=jax.ShapeDtypeStruct((frame, 128), jnp.bfloat16),
        in_specs=[scalar] + vmem(5),
        out_specs=vmem(1)[0],
        scratch_shapes=[pltpu.VMEM((frame, F * 9 * C_LAT), jnp.bfloat16)],
        name="convolve",
    )(
        rank,
        latents,
        in_weight.reshape(27 * C_LAT, CH),
        in_bias.reshape(1, CH),
        mid_weight.transpose(0, 1, 2, 4, 3).reshape(3, 9 * own, CH),
        mid_bias.reshape(1, CH),
    )
    landed = exchange(columns.reshape(devices, W, 128)).reshape(frame, 128)
    return pl.pallas_call(
        shuffle_body,
        out_shape=jax.ShapeDtypeStruct((1, F, 2, 2 * W, C_LAT), jnp.bfloat16),
        in_specs=vmem(1),
        out_specs=vmem(1)[0],
        scratch_shapes=[pltpu.VMEM((F, 2, 2 * W, C_LAT), jnp.float32)],
        name="shuffle",
    )(landed)


def on_device(*operands):
    if lax.axis_size("seq") > HEADS:
        return shared_heads(*operands)
    return whole_heads(*operands)


def solution(mesh):
    return jax.shard_map(
        on_device,
        mesh=mesh,
        in_specs=(
            P(("groups", "seq"), None),
            P(("groups", "seq"), None),
            P(("groups", "seq"), None),
            P(),
            P(),
            P(),
            P(None, None, None, None, "seq"),
            P(),
        ),
        out_specs=P(("groups", "seq"), None, None, None, None),
        check_vma=False,
    )
```

```python
import math

import jax
import jax.numpy as jnp
from jax import lax
from jax.experimental import pallas as pl
from jax.experimental.pallas import tpu as pltpu
from jax.sharding import PartitionSpec as P

D = 4096
HEADS = 32
HD = 128
C_LAT = 128
CH = 512
W = 24
F = 2
HT = 1


def padded_2(block, sides, width):
    for axis, dim in sides:
        count = lax.axis_size(axis)
        forward = [(i, i + 1) for i in range(count - 1)]
        backward = [(target, source) for source, target in forward]
        low = lax.ppermute(
            lax.slice_in_dim(block, block.shape[dim] - width, None, axis=dim), axis, forward
        )
        high = lax.ppermute(lax.slice_in_dim(block, 0, width, axis=dim), axis, backward)
        block = jnp.concatenate([low, block, high], axis=dim)
    return block


def unfold(padded, frames, height, columns):
    pieces = [
        padded[
            frame_off : frame_off + frames, row_off : row_off + height, col_off : col_off + columns
        ]
        for frame_off in range(3)
        for row_off in range(3)
        for col_off in range(3)
    ]
    return jnp.concatenate(pieces, axis=-1).reshape(frames * height * columns, -1)


def normed_latents(token_rows, proj_weight):
    widened = token_rows.astype(jnp.float32)
    normed = (
        widened * lax.rsqrt(jnp.mean(widened * widened, axis=1, keepdims=True) + 1e-06)
    ).astype(jnp.bfloat16)
    return jnp.dot(normed, proj_weight, preferred_element_type=jnp.float32).astype(jnp.bfloat16)


def extend(tile_cells):
    bordered = padded_2(tile_cells, (("seq", 1),), 1)
    return jnp.pad(bordered, ((1, 1), (0, 0), (1, 1), (0, 0)))


def shuffle_tile(summed, frames, height, columns):
    channels = summed.shape[-1] // 4
    return (
        summed.reshape(frames, height, columns, channels, 2, 2)
        .transpose(0, 1, 4, 2, 5, 3)
        .reshape(frames, 2 * height, 2 * columns, channels)
    )


def shared_heads(
    query_rows, key_rows, value_rows, proj_weight, in_weight, in_bias, mid_weight, mid_bias
):
    devices = lax.axis_size("seq")
    halves = max(1, devices // HEADS)
    unit_count = HEADS * halves // devices
    local_tokens = query_rows.shape[0]
    shard_rows = local_tokens // W
    half_width = W // halves
    score_scale = 1.0 / math.sqrt(HD)

    def by_head(rows):
        shaped = rows.reshape(local_tokens, HEADS, HD).transpose(1, 0, 2)
        shaped = jnp.broadcast_to(shaped[:, None], (HEADS, halves, local_tokens, HD))
        return shaped.reshape(devices, unit_count, local_tokens, HD)

    shaped = query_rows.reshape(shard_rows, halves, half_width, HEADS, HD).transpose(3, 1, 0, 2, 4)
    query_units = lax.all_to_all(
        shaped.reshape(devices, unit_count, shard_rows, half_width, HD),
        "seq",
        split_axis=0,
        concat_axis=0,
        tiled=True,
    )
    key_units = lax.all_to_all(by_head(key_rows), "seq", split_axis=0, concat_axis=0, tiled=True)
    value_units = lax.all_to_all(
        by_head(value_rows), "seq", split_axis=0, concat_axis=0, tiled=True
    )
    key_heads = key_units.transpose(1, 0, 2, 3).reshape(unit_count, -1, HD)
    value_heads = value_units.transpose(1, 0, 2, 3).reshape(unit_count, -1, HD)
    query_total = devices * shard_rows * half_width
    block_rows = 512 if query_total % 512 == 0 else query_total
    query_heads = (
        query_units.transpose(1, 0, 2, 3, 4)
        .reshape(unit_count, query_total // block_rows, block_rows, HD)
        .transpose(1, 0, 2, 3)
    )

    def attend(query_block):
        scores = (
            jnp.einsum("uqd,ukd->uqk", query_block, key_heads, preferred_element_type=jnp.float32)
            * score_scale
        )
        largest = jnp.max(scores, axis=2, keepdims=True)
        weights = jnp.exp(scores - largest)
        totals = jnp.sum(weights, axis=2, keepdims=True)
        mixture = jnp.einsum(
            "uqk,ukd->uqd",
            weights.astype(jnp.bfloat16),
            value_heads,
            preferred_element_type=jnp.float32,
        )
        return (mixture / totals).astype(jnp.bfloat16)

    attended = lax.map(attend, query_heads)
    attended = attended.transpose(1, 0, 2, 3).reshape(
        unit_count, devices, shard_rows, half_width, HD
    )
    arranged = attended.reshape(unit_count, F, devices, HT, half_width, HD).transpose(
        2, 0, 1, 3, 4, 5
    )
    arrived = lax.all_to_all(arranged, "seq", split_axis=0, concat_axis=0, tiled=True)
    arrived = arrived.reshape(HEADS, halves, F, HT, half_width, HD).transpose(2, 3, 1, 4, 0, 5)
    latents = normed_latents(arrived.reshape(F * HT * W, D), proj_weight).reshape(F, HT, W, C_LAT)
    unfolded_in = unfold(extend(latents), F, HT, W)
    first = (
        jnp.dot(unfolded_in, in_weight.reshape(27 * C_LAT, CH), preferred_element_type=jnp.float32)
        + in_bias
    ).astype(jnp.bfloat16)
    active = jax.nn.silu(first.astype(jnp.float32)).astype(jnp.bfloat16)
    unfolded_mid = unfold(extend(active.reshape(F, HT, W, CH)), F, HT, W)
    piece = lax.all_gather(mid_weight, "seq", axis=4, tiled=True)
    column_span = piece.shape[4]
    middle = (
        jnp.dot(
            unfolded_mid, piece.reshape(27 * CH, column_span), preferred_element_type=jnp.float32
        )
        + mid_bias
    ).astype(jnp.bfloat16)
    summed = first.astype(jnp.float32) + middle.astype(jnp.float32)
    return shuffle_tile(summed, F, HT, W).astype(jnp.bfloat16)[None]


def dot_f32(left, right, left_dim=1, right_dim=0):
    return lax.dot_general(
        left, right, (((left_dim,), (right_dim,)), ((), ())), preferred_element_type=jnp.float32
    )


def pack_body(query_ref, key_ref, value_ref, out_ref, sems):
    devices, _, _, span = out_ref.shape
    copies = []
    for target in range(devices):
        for which, ref in enumerate((query_ref, key_ref, value_ref)):
            copies.append(
                pltpu.make_async_copy(
                    ref.at[:, target * span : (target + 1) * span],
                    out_ref.at[target, which],
                    sems.at[target, which],
                )
            )
    for copy in copies:
        copy.start()
    for copy in copies:
        copy.wait()


def attend_body(rank_ref, rows_ref, proj_ref, out_ref, proj_buf, proj_sem):
    devices, _, local, span = rows_ref.shape
    tokens = devices * local
    start = pl.multiple_of(rank_ref[0] * span, span)
    copy = pltpu.make_async_copy(proj_ref.at[pl.ds(start, span), :], proj_buf, proj_sem)
    copy.start()
    query = rows_ref[:, 0].reshape(tokens, span)
    key = rows_ref[:, 1].reshape(tokens, span)
    value = rows_ref[:, 2].reshape(tokens, span)
    score_scale = 1.0 / math.sqrt(HD)
    heads = []
    for unit in range(span // HD):
        lanes = slice(unit * HD, (unit + 1) * HD)
        scores = dot_f32(query[:, lanes], key[:, lanes], 1, 1) * score_scale
        largest = jnp.max(scores, axis=1, keepdims=True)
        weights = jnp.exp(scores - largest)
        totals = jnp.sum(weights, axis=1, keepdims=True)
        mixture = dot_f32(weights.astype(jnp.bfloat16), value[:, lanes])
        heads.append((mixture / totals).astype(jnp.bfloat16))
    attended = jnp.concatenate(heads, axis=1)
    widened = attended.astype(jnp.float32)
    squares = jnp.sum(widened * widened, axis=1, keepdims=True)
    copy.wait()
    partial = dot_f32(attended, proj_buf[...])
    out_ref[:, :local, :] = partial.reshape(devices, local, C_LAT).astype(jnp.bfloat16)
    lane = lax.broadcasted_iota(jnp.int32, (devices, local, C_LAT), 2)
    row = lax.broadcasted_iota(jnp.int32, (devices, local, C_LAT), 1)
    spread = jnp.broadcast_to(squares, (tokens, C_LAT)).reshape(devices, local, C_LAT)
    across = jnp.sum(jnp.where(lane == row, spread, 0.0), axis=1, keepdims=True)
    coarse = across.astype(jnp.bfloat16).astype(jnp.float32)
    extra = out_ref.shape[1] - local
    line = lax.broadcasted_iota(jnp.int32, (devices, extra, C_LAT), 1)
    tail = jnp.where(line == 0, coarse, jnp.where(line == 1, across - coarse, 0.0))
    out_ref[:, local:, :] = tail.astype(jnp.bfloat16)


def latents_body(parts_ref, out_ref):
    devices, local, _ = out_ref.shape
    total = jnp.sum(parts_ref[:, :local, :].astype(jnp.float32), axis=0)
    tail = jnp.sum(parts_ref[:, local:, :].astype(jnp.float32), axis=0)
    across = tail[0:1] + tail[1:2]
    lane = lax.broadcasted_iota(jnp.int32, (local, C_LAT), 1)
    row = lax.broadcasted_iota(jnp.int32, (local, C_LAT), 0)
    squares = jnp.sum(jnp.where(lane == row, across, 0.0), axis=1, keepdims=True)
    latents = (total * lax.rsqrt(squares / D + 1e-06)).astype(jnp.bfloat16)
    for target in range(devices):
        out_ref[target] = latents


def convolve_body(
    rank_ref, latents_ref, in_weight_ref, in_bias_ref, mid_weight_ref, mid_bias_ref, out_ref, cols
):
    frame = latents_ref.shape[0] // F
    own = mid_weight_ref.shape[1] // 9
    column = lax.broadcasted_iota(jnp.int32, (frame, C_LAT), 0) % W
    for index in range(F):
        cells = latents_ref[index * frame : (index + 1) * frame, :].astype(jnp.float32)
        shifted = (
            jnp.where(column == 0, 0.0, pltpu.roll(cells, 1, 0)),
            cells,
            jnp.where(column == W - 1, 0.0, pltpu.roll(cells, frame - 1, 0)),
        )
        blank = jnp.zeros((W, C_LAT), jnp.float32)
        for col_off, moved in enumerate(shifted):
            above = jnp.concatenate([blank, moved[:-W]], axis=0)
            below = jnp.concatenate([moved[W:], blank], axis=0)
            for row_off, piece in enumerate((above, moved, below)):
                at = ((index * 3 + row_off) * 3 + col_off) * C_LAT
                cols[:, at : at + C_LAT] = piece.astype(jnp.bfloat16)
    deep = 9 * C_LAT
    firsts = []
    actives = []
    for index in range(F):
        low = (F - 1 - index) * deep
        first = (
            dot_f32(cols[...], in_weight_ref[low : low + F * deep, :]) + in_bias_ref[...]
        ).astype(jnp.bfloat16)
        wide = first.astype(jnp.float32)
        firsts.append(first)
        actives.append((wide / (1.0 + jnp.exp(-wide))).astype(jnp.bfloat16))
    channel = lax.broadcasted_iota(jnp.int32, (own, CH), 1)
    mine = channel == lax.broadcasted_iota(jnp.int32, (own, CH), 0) + rank_ref[0] * own
    bias = jnp.sum(jnp.where(mine, mid_bias_ref[...], 0.0), axis=1, keepdims=True)
    chosen = jnp.where(mine, 1.0, 0.0).astype(jnp.bfloat16)
    spot = lax.broadcasted_iota(jnp.int32, (own, frame), 1)
    spot_column = spot % W
    outs = []
    for index in range(F):
        taps = sum(
            dot_f32(mid_weight_ref[source - index + 1], actives[source], 1, 1)
            for source in range(F)
        )
        total = None
        for col_off in range(3):
            merged = None
            for row_off in range(3):
                at = (row_off * 3 + col_off) * own
                piece = taps[at : at + own, :]
                if row_off == 0:
                    piece = jnp.where(spot < W, 0.0, pltpu.roll(piece, W, 1))
                elif row_off == 2:
                    piece = jnp.where(spot >= frame - W, 0.0, pltpu.roll(piece, frame - W, 1))
                merged = piece if merged is None else merged + piece
            if col_off == 0:
                merged = jnp.where(spot_column == 0, 0.0, pltpu.roll(merged, 1, 1))
            elif col_off == 2:
                merged = jnp.where(spot_column == W - 1, 0.0, pltpu.roll(merged, frame - 1, 1))
            total = merged if total is None else total + merged
        middle = (total + bias).astype(jnp.bfloat16).astype(jnp.float32)
        outs.append((dot_f32(chosen, firsts[index], 1, 1) + middle).astype(jnp.bfloat16))
    stacked = jnp.concatenate(outs, axis=0)
    source = lax.broadcasted_iota(jnp.int32, (F * own, 128), 0)
    target = lax.broadcasted_iota(jnp.int32, (F * own, 128), 1)
    inner = source % own
    place = (source // own) * own + (inner % 4) * (own // 4) + inner // 4
    moves = jnp.where(place == target, 1.0, 0.0).astype(jnp.bfloat16)
    out_ref[...] = dot_f32(stacked, moves, 0, 0).astype(jnp.bfloat16)


def shuffle_body(rows_ref, out_ref, wide):
    devices = rows_ref.shape[0] // W
    share = C_LAT // devices
    rows = rows_ref[...].astype(jnp.float32)
    lane = lax.broadcasted_iota(jnp.int32, (W, 128), 1) // share
    for index in range(F):
        for part in range(4):
            origin = (index * 4 + part) * share
            total = None
            for source in range(devices):
                block = rows[source * W : (source + 1) * W, :]
                moved = pltpu.roll(block, (source * share - origin) % 128, 1)
                total = moved if total is None else jnp.where(lane == source, moved, total)
            wide[index, part // 2, pl.ds(part % 2, W, stride=2), :] = total
    out_ref[0] = wide[...].astype(jnp.bfloat16)


def near(array):
    return pltpu.with_memory_space_constraint(array, pltpu.VMEM)


def vmem(count):
    return [pl.BlockSpec(memory_space=pltpu.VMEM)] * count


def exchange(blocks):
    return lax.all_to_all(blocks, "seq", split_axis=0, concat_axis=0, tiled=True)


def whole_heads(
    query_rows, key_rows, value_rows, proj_weight, in_weight, in_bias, mid_weight, mid_bias
):
    devices = lax.axis_size("seq")
    local = query_rows.shape[0]
    span = D // devices
    frame = devices * local // F
    own = mid_weight.shape[4]
    rank = lax.axis_index("seq").reshape(1).astype(jnp.int32)
    scalar = pl.BlockSpec(memory_space=pltpu.SMEM)
    packed = pl.pallas_call(
        pack_body,
        out_shape=pltpu.VMEM((devices, 3, local, span), jnp.bfloat16),
        in_specs=[pl.BlockSpec(memory_space=pl.ANY)] * 3,
        out_specs=vmem(1)[0],
        scratch_shapes=[pltpu.SemaphoreType.DMA((devices, 3))],
        compiler_params=pltpu.CompilerParams(vmem_limit_bytes=8 << 20),
        name="pack",
    )(query_rows, key_rows, value_rows)
    rows = exchange(packed)
    parts = pl.pallas_call(
        attend_body,
        out_shape=pltpu.VMEM((devices, local + 8, C_LAT), jnp.bfloat16),
        in_specs=[scalar, vmem(1)[0], pl.BlockSpec(memory_space=pl.ANY)],
        out_specs=vmem(1)[0],
        scratch_shapes=[pltpu.VMEM((span, C_LAT), jnp.bfloat16), pltpu.SemaphoreType.DMA(())],
        compiler_params=pltpu.CompilerParams(vmem_limit_bytes=32 << 20),
        name="attend",
    )(rank, near(rows), proj_weight)
    parts = exchange(parts)
    copies = pl.pallas_call(
        latents_body,
        out_shape=pltpu.VMEM((devices, local, C_LAT), jnp.bfloat16),
        in_specs=vmem(1),
        out_specs=vmem(1)[0],
        compiler_params=pltpu.CompilerParams(vmem_limit_bytes=8 << 20),
        name="latents",
    )(near(parts))
    latents = exchange(copies).reshape(devices * local, C_LAT)
    columns = pl.pallas_call(
        convolve_body,
        out_shape=pltpu.VMEM((frame, 128), jnp.bfloat16),
        in_specs=[scalar] + vmem(5),
        out_specs=vmem(1)[0],
        scratch_shapes=[pltpu.VMEM((frame, F * 9 * C_LAT), jnp.bfloat16)],
        compiler_params=pltpu.CompilerParams(vmem_limit_bytes=32 << 20),
        name="convolve",
    )(
        rank,
        near(latents),
        near(in_weight.reshape(27 * C_LAT, CH)),
        in_bias.reshape(1, CH),
        near(mid_weight.transpose(0, 1, 2, 4, 3).reshape(3, 9 * own, CH)),
        mid_bias.reshape(1, CH),
    )
    landed = exchange(columns.reshape(devices, W, 128)).reshape(frame, 128)
    return pl.pallas_call(
        shuffle_body,
        out_shape=jax.ShapeDtypeStruct((1, F, 2, 2 * W, C_LAT), jnp.bfloat16),
        in_specs=vmem(1),
        out_specs=vmem(1)[0],
        scratch_shapes=[pltpu.VMEM((F, 2, 2 * W, C_LAT), jnp.float32)],
        compiler_params=pltpu.CompilerParams(vmem_limit_bytes=8 << 20),
        name="shuffle",
    )(near(landed))


def on_device(*operands):
    if lax.axis_size("seq") > HEADS:
        return shared_heads(*operands)
    return whole_heads(*operands)


def solution(mesh):
    return jax.shard_map(
        on_device,
        mesh=mesh,
        in_specs=(
            P(("groups", "seq"), None),
            P(("groups", "seq"), None),
            P(("groups", "seq"), None),
            P(),
            P(),
            P(),
            P(None, None, None, None, "seq"),
            P(),
        ),
        out_specs=P(("groups", "seq"), None, None, None, None),
        check_vma=False,
    )
```

```python
import functools
import math

import jax
import jax.numpy as jnp
from jax import lax
from jax.experimental import pallas as pl
from jax.experimental.pallas import tpu as pltpu
from jax.sharding import PartitionSpec as P


D = 4096
HEADS = 32
HD = 128
C_LAT = 128
CH = 512
W = 24
F = 2
HT = 1


def padded_2(block, sides, width):
    for axis, dim in sides:
        count = lax.axis_size(axis)
        forward = [(i, i + 1) for i in range(count - 1)]
        backward = [(target, source) for source, target in forward]
        low = lax.ppermute(
            lax.slice_in_dim(block, block.shape[dim] - width, None, axis=dim), axis, forward
        )
        high = lax.ppermute(lax.slice_in_dim(block, 0, width, axis=dim), axis, backward)
        block = jnp.concatenate([low, block, high], axis=dim)
    return block


def unfold(padded, frames, height, columns):
    pieces = [
        padded[
            frame_off : frame_off + frames, row_off : row_off + height, col_off : col_off + columns
        ]
        for frame_off in range(3)
        for row_off in range(3)
        for col_off in range(3)
    ]
    return jnp.concatenate(pieces, axis=-1).reshape(frames * height * columns, -1)


def normed_latents(token_rows, proj_weight):
    widened = token_rows.astype(jnp.float32)
    normed = (
        widened * lax.rsqrt(jnp.mean(widened * widened, axis=1, keepdims=True) + 1e-06)
    ).astype(jnp.bfloat16)
    return jnp.dot(normed, proj_weight, preferred_element_type=jnp.float32).astype(jnp.bfloat16)


def extend(tile_cells):
    bordered = padded_2(tile_cells, (("seq", 1),), 1)
    return jnp.pad(bordered, ((1, 1), (0, 0), (1, 1), (0, 0)))


def shuffle_tile(summed, frames, height, columns):
    channels = summed.shape[-1] // 4
    return (
        summed.reshape(frames, height, columns, channels, 2, 2)
        .transpose(0, 1, 4, 2, 5, 3)
        .reshape(frames, 2 * height, 2 * columns, channels)
    )


def shared_heads(
    query_rows, key_rows, value_rows, proj_weight, in_weight, in_bias, mid_weight, mid_bias
):
    devices = lax.axis_size("seq")
    halves = max(1, devices // HEADS)
    unit_count = HEADS * halves // devices
    local_tokens = query_rows.shape[0]
    shard_rows = local_tokens // W
    half_width = W // halves
    score_scale = 1.0 / math.sqrt(HD)

    def by_head(rows):
        shaped = rows.reshape(local_tokens, HEADS, HD).transpose(1, 0, 2)
        shaped = jnp.broadcast_to(shaped[:, None], (HEADS, halves, local_tokens, HD))
        return shaped.reshape(devices, unit_count, local_tokens, HD)

    shaped = query_rows.reshape(shard_rows, halves, half_width, HEADS, HD).transpose(3, 1, 0, 2, 4)
    query_units = lax.all_to_all(
        shaped.reshape(devices, unit_count, shard_rows, half_width, HD),
        "seq",
        split_axis=0,
        concat_axis=0,
        tiled=True,
    )
    key_units = lax.all_to_all(by_head(key_rows), "seq", split_axis=0, concat_axis=0, tiled=True)
    value_units = lax.all_to_all(
        by_head(value_rows), "seq", split_axis=0, concat_axis=0, tiled=True
    )
    key_heads = key_units.transpose(1, 0, 2, 3).reshape(unit_count, -1, HD)
    value_heads = value_units.transpose(1, 0, 2, 3).reshape(unit_count, -1, HD)
    query_total = devices * shard_rows * half_width
    block_rows = 512 if query_total % 512 == 0 else query_total
    query_heads = (
        query_units.transpose(1, 0, 2, 3, 4)
        .reshape(unit_count, query_total // block_rows, block_rows, HD)
        .transpose(1, 0, 2, 3)
    )

    def attend(query_block):
        scores = (
            jnp.einsum("uqd,ukd->uqk", query_block, key_heads, preferred_element_type=jnp.float32)
            * score_scale
        )
        largest = jnp.max(scores, axis=2, keepdims=True)
        weights = jnp.exp(scores - largest)
        totals = jnp.sum(weights, axis=2, keepdims=True)
        mixture = jnp.einsum(
            "uqk,ukd->uqd",
            weights.astype(jnp.bfloat16),
            value_heads,
            preferred_element_type=jnp.float32,
        )
        return (mixture / totals).astype(jnp.bfloat16)

    attended = lax.map(attend, query_heads)
    attended = attended.transpose(1, 0, 2, 3).reshape(
        unit_count, devices, shard_rows, half_width, HD
    )
    arranged = attended.reshape(unit_count, F, devices, HT, half_width, HD).transpose(
        2, 0, 1, 3, 4, 5
    )
    arrived = lax.all_to_all(arranged, "seq", split_axis=0, concat_axis=0, tiled=True)
    arrived = arrived.reshape(HEADS, halves, F, HT, half_width, HD).transpose(2, 3, 1, 4, 0, 5)
    latents = normed_latents(arrived.reshape(F * HT * W, D), proj_weight).reshape(F, HT, W, C_LAT)
    unfolded_in = unfold(extend(latents), F, HT, W)
    first = (
        jnp.dot(unfolded_in, in_weight.reshape(27 * C_LAT, CH), preferred_element_type=jnp.float32)
        + in_bias
    ).astype(jnp.bfloat16)
    active = jax.nn.silu(first.astype(jnp.float32)).astype(jnp.bfloat16)
    unfolded_mid = unfold(extend(active.reshape(F, HT, W, CH)), F, HT, W)
    piece = lax.all_gather(mid_weight, "seq", axis=4, tiled=True)
    column_span = piece.shape[4]
    middle = (
        jnp.dot(
            unfolded_mid, piece.reshape(27 * CH, column_span), preferred_element_type=jnp.float32
        )
        + mid_bias
    ).astype(jnp.bfloat16)
    summed = first.astype(jnp.float32) + middle.astype(jnp.float32)
    return shuffle_tile(summed, F, HT, W).astype(jnp.bfloat16)[None]


def dot_f32(left, right, left_dim=1, right_dim=0):
    return lax.dot_general(
        left, right, (((left_dim,), (right_dim,)), ((), ())), preferred_element_type=jnp.float32
    )


def pack_body(rank_ref, query_ref, key_ref, value_ref, *rest):
    blocks, sems = rest[:-1], rest[-1]
    span = blocks[0].shape[2]
    copies = []
    for place, step in enumerate(exchange_order(len(blocks))):
        start = pl.multiple_of((rank_ref[0] ^ step) * span, span)
        for which, ref in enumerate((query_ref, key_ref, value_ref)):
            copies.append(
                pltpu.make_async_copy(
                    ref.at[:, pl.ds(start, span)], blocks[place].at[which], sems.at[place, which]
                )
            )
    for copy in copies:
        copy.start()
    for copy in copies:
        copy.wait()


def read_sums(ref, count):
    cells = ref.shape[0] - (2 if ref.dtype == jnp.bfloat16 else 1) * count
    parts = ref[:cells].astype(jnp.float32).reshape(count, cells // count, C_LAT)
    tail = ref[cells:].astype(jnp.float32)
    squares = tail[:count] + tail[count:] if ref.dtype == jnp.bfloat16 else tail
    return [parts[i] for i in range(count)], [squares[i : i + 1] for i in range(count)]


def write_sums(ref, parts, squares):
    cells = len(parts) * parts[0].shape[0]
    across = jnp.concatenate(squares, axis=0)
    if ref.dtype == jnp.bfloat16:
        coarse = across.astype(jnp.bfloat16).astype(jnp.float32)
        across = jnp.concatenate([coarse, across - coarse], axis=0)
    ref[:cells] = jnp.concatenate(parts, axis=0).astype(ref.dtype)
    ref[cells:] = across.astype(ref.dtype)


def attend_body(rank_ref, proj_ref, *rest):
    blocks, (keep_ref, send_ref, proj_buf, proj_sem) = rest[:-4], rest[-4:]
    devices = len(blocks)
    _, local, span = blocks[0].shape
    tokens = devices * local
    start = pl.multiple_of(rank_ref[0] * span, span)
    copy = pltpu.make_async_copy(proj_ref.at[pl.ds(start, span), :], proj_buf, proj_sem)
    copy.start()
    query, key, value = (
        jnp.concatenate([block[which] for block in blocks], axis=0) for which in range(3)
    )
    score_scale = 1.0 / math.sqrt(HD)
    heads = []
    for unit in range(span // HD):
        lanes = slice(unit * HD, (unit + 1) * HD)
        scores = dot_f32(query[:, lanes], key[:, lanes], 1, 1) * score_scale
        largest = jnp.max(scores, axis=1, keepdims=True)
        weights = jnp.exp(scores - largest)
        totals = jnp.sum(weights, axis=1, keepdims=True)
        mixture = dot_f32(weights.astype(jnp.bfloat16), value[:, lanes])
        heads.append((mixture / totals).astype(jnp.bfloat16))
    attended = jnp.concatenate(heads, axis=1)
    widened = attended.astype(jnp.float32)
    squares = jnp.sum(widened * widened, axis=1, keepdims=True)
    copy.wait()
    partial = dot_f32(attended, proj_buf[...]).reshape(devices, local, C_LAT)
    lane = lax.broadcasted_iota(jnp.int32, (devices, local, C_LAT), 2)
    row = lax.broadcasted_iota(jnp.int32, (devices, local, C_LAT), 1)
    spread = jnp.broadcast_to(squares, (tokens, C_LAT)).reshape(devices, local, C_LAT)
    across = jnp.sum(jnp.where(lane == row, spread, 0.0), axis=1)
    order = exchange_order(devices)
    for ref, first in ((keep_ref, 0), (send_ref, 1)):
        chosen = [order.index(step) for step in range(first, devices, 2)]
        write_sums(ref, [partial[i] for i in chosen], [across[i : i + 1] for i in chosen])


def fold_body(keep_ref, got_ref, next_ref, send_ref, count, split):
    parts, squares = read_sums(keep_ref, count)
    more_parts, more_squares = read_sums(got_ref, count)
    parts = [x + y for x, y in zip(parts, more_parts)]
    squares = [x + y for x, y in zip(squares, more_squares)]
    for ref, first in ((next_ref, 0), (send_ref, 1)):
        chosen = range(first, count, 2) if split else range(count)
        write_sums(ref, [parts[i] for i in chosen], [squares[i] for i in chosen])


def latents_body(keep_ref, *rest):
    gots, out_ref = rest[:-1], rest[-1]
    count = len(rest)
    local = out_ref.shape[0] // count
    parts, squares = read_sums(keep_ref, count)
    for step, got in enumerate(gots, 1):
        more_parts, more_squares = read_sums(got, count)
        parts = [parts[i] + more_parts[i ^ step] for i in range(count)]
        squares = [squares[i] + more_squares[i ^ step] for i in range(count)]
    lane = lax.broadcasted_iota(jnp.int32, (local, C_LAT), 1)
    row = lax.broadcasted_iota(jnp.int32, (local, C_LAT), 0)
    done = []
    for part, square in zip(parts, squares):
        column = jnp.sum(jnp.where(lane == row, square, 0.0), axis=1, keepdims=True)
        done.append(part * lax.rsqrt(column / D + 1e-06))
    out_ref[...] = jnp.concatenate(done, axis=0).astype(jnp.bfloat16)


def convolve_body(
    rank_ref, in_weight_ref, in_bias_ref, mid_weight_ref, mid_bias_ref, *rest
):
    quarters, (out_ref, latents_ref, cols, mid_buf, mid_sem) = rest[:-5], rest[-5:]
    fetch = pltpu.make_async_copy(mid_weight_ref, mid_buf, mid_sem)
    fetch.start()
    frame = latents_ref.shape[0] // F
    count = out_ref.shape[0] // W // len(quarters)
    local = quarters[0].shape[0] // count
    for low, quarter in enumerate(quarters):
        for high in range(count):
            block = rank_ref[0] ^ (high * len(quarters) + low)
            latents_ref[pl.ds(pl.multiple_of(block * local, 16), local), :] = quarter[
                high * local : (high + 1) * local, :
            ]
    own = mid_weight_ref.shape[1] // 9
    column = lax.broadcasted_iota(jnp.int32, (frame, C_LAT), 0) % W
    for index in range(F):
        cells = latents_ref[index * frame : (index + 1) * frame, :].astype(jnp.float32)
        shifted = (
            jnp.where(column == 0, 0.0, pltpu.roll(cells, 1, 0)),
            cells,
            jnp.where(column == W - 1, 0.0, pltpu.roll(cells, frame - 1, 0)),
        )
        blank = jnp.zeros((W, C_LAT), jnp.float32)
        for col_off, moved in enumerate(shifted):
            above = jnp.concatenate([blank, moved[:-W]], axis=0)
            below = jnp.concatenate([moved[W:], blank], axis=0)
            for row_off, piece in enumerate((above, moved, below)):
                at = ((index * 3 + row_off) * 3 + col_off) * C_LAT
                cols[:, at : at + C_LAT] = piece.astype(jnp.bfloat16)
    deep = 9 * C_LAT
    firsts = []
    actives = []
    for index in range(F):
        low = (F - 1 - index) * deep
        first = (
            dot_f32(cols[...], in_weight_ref[low : low + F * deep, :]) + in_bias_ref[...]
        ).astype(jnp.bfloat16)
        wide = first.astype(jnp.float32)
        firsts.append(first)
        actives.append((wide / (1.0 + jnp.exp(-wide))).astype(jnp.bfloat16))
    channel = lax.broadcasted_iota(jnp.int32, (own, CH), 1)
    mine = channel == lax.broadcasted_iota(jnp.int32, (own, CH), 0) + rank_ref[0] * own
    bias = jnp.sum(jnp.where(mine, mid_bias_ref[...], 0.0), axis=1, keepdims=True)
    chosen = jnp.where(mine, 1.0, 0.0).astype(jnp.bfloat16)
    spot = lax.broadcasted_iota(jnp.int32, (own, frame), 1)
    spot_column = spot % W
    fetch.wait()
    outs = []
    for index in range(F):
        taps = sum(
            dot_f32(mid_buf[source - index + 1], actives[source], 1, 1)
            for source in range(F)
        )
        total = None
        for col_off in range(3):
            merged = None
            for row_off in range(3):
                at = (row_off * 3 + col_off) * own
                piece = taps[at : at + own, :]
                if row_off == 0:
                    piece = jnp.where(spot < W, 0.0, pltpu.roll(piece, W, 1))
                elif row_off == 2:
                    piece = jnp.where(spot >= frame - W, 0.0, pltpu.roll(piece, frame - W, 1))
                merged = piece if merged is None else merged + piece
            if col_off == 0:
                merged = jnp.where(spot_column == 0, 0.0, pltpu.roll(merged, 1, 1))
            elif col_off == 2:
                merged = jnp.where(spot_column == W - 1, 0.0, pltpu.roll(merged, frame - 1, 1))
            total = merged if total is None else total + merged
        middle = (total + bias).astype(jnp.bfloat16).astype(jnp.float32)
        outs.append((dot_f32(chosen, firsts[index], 1, 1) + middle).astype(jnp.bfloat16))
    stacked = jnp.concatenate(outs, axis=0)
    source = lax.broadcasted_iota(jnp.int32, (F * own, 128), 0)
    target = lax.broadcasted_iota(jnp.int32, (F * own, 128), 1)
    inner = source % own
    place = (source // own) * own + (inner % 4) * (own // 4) + inner // 4
    moves = jnp.where(place == target, 1.0, 0.0).astype(jnp.bfloat16)
    out_ref[...] = dot_f32(stacked, moves, 0, 0).astype(jnp.bfloat16)


def shuffle_body(rows_ref, out_ref, wide):
    devices = rows_ref.shape[0] // W
    share = C_LAT // devices
    rows = rows_ref[...].astype(jnp.float32)
    lane = lax.broadcasted_iota(jnp.int32, (W, 128), 1) // share
    for index in range(F):
        for part in range(4):
            origin = (index * 4 + part) * share
            total = None
            for source in range(devices):
                block = rows[source * W : (source + 1) * W, :]
                moved = pltpu.roll(block, (source * share - origin) % 128, 1)
                total = moved if total is None else jnp.where(lane == source, moved, total)
            wide[index, part // 2, pl.ds(part % 2, W, stride=2), :] = total
    out_ref[0] = wide[...].astype(jnp.bfloat16)


def near(array):
    return pltpu.with_memory_space_constraint(array, pltpu.VMEM)


def far(array):
    return pltpu.with_memory_space_constraint(array, pltpu.HBM)


SCALAR = pl.BlockSpec(memory_space=pltpu.SMEM)
LOCAL = pl.BlockSpec(memory_space=pltpu.VMEM)
REMOTE = pl.BlockSpec(memory_space=pltpu.HBM)


def launch(body, name, outs, in_specs, operands, scratch=(), mib=8):
    return pl.pallas_call(
        body,
        out_shape=outs,
        in_specs=in_specs,
        out_specs=jax.tree.map(lambda _: LOCAL, outs),
        scratch_shapes=scratch,
        compiler_params=pltpu.CompilerParams(vmem_limit_bytes=mib << 20),
        name=name,
    )(*operands)


def exchange_order(devices):
    half = devices // 2
    order = [0, half]
    for step in range(1, half):
        order += [step, half + step]
    return order


def swap(array, step):
    devices = lax.axis_size("seq")
    return near(lax.ppermute(array, "seq", [(i, i ^ step) for i in range(devices)]))


def sums_shape(count, local, dtype):
    tail = 2 * count if dtype == jnp.bfloat16 else count
    return pltpu.VMEM((count * local + tail, C_LAT), dtype)


def whole_heads(
    query_rows, key_rows, value_rows, proj_weight, in_weight, in_bias, mid_weight, mid_bias
):
    devices = lax.axis_size("seq")
    local = query_rows.shape[0]
    span = D // devices
    frame = devices * local // F
    own = mid_weight.shape[4]
    rank = lax.axis_index("seq").reshape(1).astype(jnp.int32)
    blocks = launch(
        pack_body,
        "pack",
        [pltpu.VMEM((3, local, span), jnp.bfloat16)] * devices,
        [SCALAR] + [REMOTE] * 3,
        (rank, far(query_rows), far(key_rows), far(value_rows)),
        [pltpu.SemaphoreType.DMA((devices, 3))],
    )
    landed = [
        swap(block, step) if step else near(block)
        for block, step in zip(blocks, exchange_order(devices))
    ]
    half = devices // 2
    quarter = devices // 4
    keep, send = launch(
        attend_body,
        "attend",
        [sums_shape(half, local, jnp.float32), sums_shape(half, local, jnp.bfloat16)],
        [SCALAR, REMOTE] + [LOCAL] * devices,
        (rank, far(proj_weight), *landed),
        [pltpu.VMEM((span, C_LAT), jnp.bfloat16), pltpu.SemaphoreType.DMA(())],
        32,
    )
    keep, send = launch(
        functools.partial(fold_body, count=half, split=True),
        "fold_core",
        [sums_shape(quarter, local, jnp.float32), sums_shape(quarter, local, jnp.bfloat16)],
        [LOCAL] * 2,
        (near(keep), swap(send, 1)),
    )
    keep, send = launch(
        functools.partial(fold_body, count=quarter, split=False),
        "fold_pair",
        [sums_shape(quarter, local, jnp.float32), sums_shape(quarter, local, jnp.bfloat16)],
        [LOCAL] * 2,
        (near(keep), swap(send, 2)),
    )
    gots = [swap(send, 4 * step) for step in range(1, quarter)]
    ready = launch(
        latents_body,
        "latents",
        pltpu.VMEM((quarter * local, C_LAT), jnp.bfloat16),
        [LOCAL] * (1 + len(gots)),
        (near(keep), *gots),
    )
    paired = swap(ready, 2)
    columns = launch(
        convolve_body,
        "convolve",
        pltpu.VMEM((frame, 128), jnp.bfloat16),
        [SCALAR] + [LOCAL] * 2 + [REMOTE] + [LOCAL] * 5,
        (
            rank,
            near(in_weight.reshape(27 * C_LAT, CH)),
            near(in_bias.reshape(1, CH)),
            far(mid_weight.transpose(0, 1, 2, 4, 3).reshape(3, 9 * own, CH)),
            near(mid_bias.reshape(1, CH)),
            near(ready),
            swap(ready, 1),
            paired,
            swap(paired, 1),
        ),
        [
            pltpu.VMEM((devices * local, C_LAT), jnp.bfloat16),
            pltpu.VMEM((frame, F * 9 * C_LAT), jnp.bfloat16),
            pltpu.VMEM((3, 9 * own, CH), jnp.bfloat16),
            pltpu.SemaphoreType.DMA(()),
        ],
        32,
    )
    arrived = lax.all_to_all(
        columns.reshape(devices, W, 128), "seq", split_axis=0, concat_axis=0, tiled=True
    )
    return pl.pallas_call(
        shuffle_body,
        out_shape=jax.ShapeDtypeStruct((1, F, 2, 2 * W, C_LAT), jnp.bfloat16),
        in_specs=[LOCAL],
        out_specs=LOCAL,
        scratch_shapes=[pltpu.VMEM((F, 2, 2 * W, C_LAT), jnp.float32)],
        compiler_params=pltpu.CompilerParams(vmem_limit_bytes=8 << 20),
        name="shuffle",
    )(near(arrived.reshape(frame, 128)))


def on_device(*operands):
    devices = lax.axis_size("seq")
    if devices > HEADS or devices < 8 or devices & (devices - 1):
        return shared_heads(*operands)
    return whole_heads(*operands)


def solution(mesh):
    return jax.shard_map(
        on_device,
        mesh=mesh,
        in_specs=(
            P(("groups", "seq"), None),
            P(("groups", "seq"), None),
            P(("groups", "seq"), None),
            P(),
            P(),
            P(),
            P(None, None, None, None, "seq"),
            P(),
        ),
        out_specs=P(("groups", "seq"), None, None, None, None),
        check_vma=False,
    )
```

```python
import functools
import math

import jax
import jax.numpy as jnp
from jax import lax
from jax.experimental import pallas as pl
from jax.experimental.pallas import tpu as pltpu
from jax.sharding import PartitionSpec as P


D = 4096
HEADS = 32
HD = 128
C_LAT = 128
CH = 512
W = 24
F = 2
HT = 1


def padded_2(block, sides, width):
    for axis, dim in sides:
        count = lax.axis_size(axis)
        forward = [(i, i + 1) for i in range(count - 1)]
        backward = [(target, source) for source, target in forward]
        low = lax.ppermute(
            lax.slice_in_dim(block, block.shape[dim] - width, None, axis=dim), axis, forward
        )
        high = lax.ppermute(lax.slice_in_dim(block, 0, width, axis=dim), axis, backward)
        block = jnp.concatenate([low, block, high], axis=dim)
    return block


def unfold(padded, frames, height, columns):
    pieces = [
        padded[
            frame_off : frame_off + frames, row_off : row_off + height, col_off : col_off + columns
        ]
        for frame_off in range(3)
        for row_off in range(3)
        for col_off in range(3)
    ]
    return jnp.concatenate(pieces, axis=-1).reshape(frames * height * columns, -1)


def normed_latents(token_rows, proj_weight):
    widened = token_rows.astype(jnp.float32)
    normed = (
        widened * lax.rsqrt(jnp.mean(widened * widened, axis=1, keepdims=True) + 1e-06)
    ).astype(jnp.bfloat16)
    return jnp.dot(normed, proj_weight, preferred_element_type=jnp.float32).astype(jnp.bfloat16)


def extend(tile_cells):
    bordered = padded_2(tile_cells, (("seq", 1),), 1)
    return jnp.pad(bordered, ((1, 1), (0, 0), (1, 1), (0, 0)))


def shuffle_tile(summed, frames, height, columns):
    channels = summed.shape[-1] // 4
    return (
        summed.reshape(frames, height, columns, channels, 2, 2)
        .transpose(0, 1, 4, 2, 5, 3)
        .reshape(frames, 2 * height, 2 * columns, channels)
    )


def shared_heads(
    query_rows, key_rows, value_rows, proj_weight, in_weight, in_bias, mid_weight, mid_bias
):
    devices = lax.axis_size("seq")
    halves = max(1, devices // HEADS)
    unit_count = HEADS * halves // devices
    local_tokens = query_rows.shape[0]
    shard_rows = local_tokens // W
    half_width = W // halves
    score_scale = 1.0 / math.sqrt(HD)

    def by_head(rows):
        shaped = rows.reshape(local_tokens, HEADS, HD).transpose(1, 0, 2)
        shaped = jnp.broadcast_to(shaped[:, None], (HEADS, halves, local_tokens, HD))
        return shaped.reshape(devices, unit_count, local_tokens, HD)

    shaped = query_rows.reshape(shard_rows, halves, half_width, HEADS, HD).transpose(3, 1, 0, 2, 4)
    query_units = lax.all_to_all(
        shaped.reshape(devices, unit_count, shard_rows, half_width, HD),
        "seq",
        split_axis=0,
        concat_axis=0,
        tiled=True,
    )
    key_units = lax.all_to_all(by_head(key_rows), "seq", split_axis=0, concat_axis=0, tiled=True)
    value_units = lax.all_to_all(
        by_head(value_rows), "seq", split_axis=0, concat_axis=0, tiled=True
    )
    key_heads = key_units.transpose(1, 0, 2, 3).reshape(unit_count, -1, HD)
    value_heads = value_units.transpose(1, 0, 2, 3).reshape(unit_count, -1, HD)
    query_total = devices * shard_rows * half_width
    block_rows = 512 if query_total % 512 == 0 else query_total
    query_heads = (
        query_units.transpose(1, 0, 2, 3, 4)
        .reshape(unit_count, query_total // block_rows, block_rows, HD)
        .transpose(1, 0, 2, 3)
    )

    def attend(query_block):
        scores = (
            jnp.einsum("uqd,ukd->uqk", query_block, key_heads, preferred_element_type=jnp.float32)
            * score_scale
        )
        largest = jnp.max(scores, axis=2, keepdims=True)
        weights = jnp.exp(scores - largest)
        totals = jnp.sum(weights, axis=2, keepdims=True)
        mixture = jnp.einsum(
            "uqk,ukd->uqd",
            weights.astype(jnp.bfloat16),
            value_heads,
            preferred_element_type=jnp.float32,
        )
        return (mixture / totals).astype(jnp.bfloat16)

    attended = lax.map(attend, query_heads)
    attended = attended.transpose(1, 0, 2, 3).reshape(
        unit_count, devices, shard_rows, half_width, HD
    )
    arranged = attended.reshape(unit_count, F, devices, HT, half_width, HD).transpose(
        2, 0, 1, 3, 4, 5
    )
    arrived = lax.all_to_all(arranged, "seq", split_axis=0, concat_axis=0, tiled=True)
    arrived = arrived.reshape(HEADS, halves, F, HT, half_width, HD).transpose(2, 3, 1, 4, 0, 5)
    latents = normed_latents(arrived.reshape(F * HT * W, D), proj_weight).reshape(F, HT, W, C_LAT)
    unfolded_in = unfold(extend(latents), F, HT, W)
    first = (
        jnp.dot(unfolded_in, in_weight.reshape(27 * C_LAT, CH), preferred_element_type=jnp.float32)
        + in_bias
    ).astype(jnp.bfloat16)
    active = jax.nn.silu(first.astype(jnp.float32)).astype(jnp.bfloat16)
    unfolded_mid = unfold(extend(active.reshape(F, HT, W, CH)), F, HT, W)
    piece = lax.all_gather(mid_weight, "seq", axis=4, tiled=True)
    column_span = piece.shape[4]
    middle = (
        jnp.dot(
            unfolded_mid, piece.reshape(27 * CH, column_span), preferred_element_type=jnp.float32
        )
        + mid_bias
    ).astype(jnp.bfloat16)
    summed = first.astype(jnp.float32) + middle.astype(jnp.float32)
    return shuffle_tile(summed, F, HT, W).astype(jnp.bfloat16)[None]


def dot_f32(left, right, left_dim=1, right_dim=0):
    return lax.dot_general(
        left, right, (((left_dim,), (right_dim,)), ((), ())), preferred_element_type=jnp.float32
    )


def pack_body(rank_ref, query_ref, key_ref, value_ref, *rest, steps, span):
    blocks, sems = rest[:-1], rest[-1]
    copies = []
    for place, step in enumerate(steps):
        start = pl.multiple_of((rank_ref[0] ^ step) * span, span)
        for which, ref in enumerate((query_ref, key_ref, value_ref)):
            copies.append(
                pltpu.make_async_copy(
                    ref.at[:, pl.ds(start, span)], blocks[place].at[which], sems.at[place, which]
                )
            )
    for copy in copies:
        copy.start()
    for copy in copies:
        copy.wait()


def slice_body(rank_ref, proj_ref, out_ref, sem):
    span = out_ref.shape[0]
    start = pl.multiple_of(rank_ref[0] * span, span)
    copy = pltpu.make_async_copy(proj_ref.at[pl.ds(start, span), :], out_ref, sem)
    copy.start()
    copy.wait()


def read_sums(ref, count):
    cells = ref.shape[0] - (2 if ref.dtype == jnp.bfloat16 else 1) * count
    parts = ref[:cells].astype(jnp.float32).reshape(count, cells // count, C_LAT)
    tail = ref[cells:].astype(jnp.float32)
    squares = tail[:count] + tail[count:] if ref.dtype == jnp.bfloat16 else tail
    return [parts[i] for i in range(count)], [squares[i : i + 1] for i in range(count)]


def write_sums(ref, parts, squares):
    cells = len(parts) * parts[0].shape[0]
    across = jnp.concatenate(squares, axis=0)
    if ref.dtype == jnp.bfloat16:
        coarse = across.astype(jnp.bfloat16).astype(jnp.float32)
        across = jnp.concatenate([coarse, across - coarse], axis=0)
    ref[:cells] = jnp.concatenate(parts, axis=0).astype(ref.dtype)
    ref[cells:] = across.astype(ref.dtype)


def attend_body(mid_weight_ref, proj_ref, *rest):
    blocks, (keep_ref, send_ref, mid_ref, mid_sem) = rest[:-4], rest[-4:]
    fetch = pltpu.make_async_copy(mid_weight_ref, mid_ref, mid_sem)
    fetch.start()
    devices = len(blocks)
    _, local, span = blocks[0].shape
    tokens = devices * local
    query, key, value = (
        jnp.concatenate([block[which] for block in blocks], axis=0) for which in range(3)
    )
    score_scale = 1.0 / math.sqrt(HD)
    heads = []
    for unit in range(span // HD):
        lanes = slice(unit * HD, (unit + 1) * HD)
        scores = dot_f32(query[:, lanes], key[:, lanes], 1, 1) * score_scale
        largest = jnp.max(scores, axis=1, keepdims=True)
        weights = jnp.exp(scores - largest)
        totals = jnp.sum(weights, axis=1, keepdims=True)
        mixture = dot_f32(weights.astype(jnp.bfloat16), value[:, lanes])
        heads.append((mixture / totals).astype(jnp.bfloat16))
    attended = jnp.concatenate(heads, axis=1)
    widened = attended.astype(jnp.float32)
    squares = jnp.sum(widened * widened, axis=1, keepdims=True)
    partial = dot_f32(attended, proj_ref[...]).reshape(devices, local, C_LAT)
    lane = lax.broadcasted_iota(jnp.int32, (devices, local, C_LAT), 2)
    row = lax.broadcasted_iota(jnp.int32, (devices, local, C_LAT), 1)
    spread = jnp.broadcast_to(squares, (tokens, C_LAT)).reshape(devices, local, C_LAT)
    across = jnp.sum(jnp.where(lane == row, spread, 0.0), axis=1)
    order = exchange_order(devices)[1:] + [0]
    for ref, first in ((keep_ref, 0), (send_ref, 1)):
        chosen = [order.index(step) for step in range(first, devices, 2)]
        write_sums(ref, [partial[i] for i in chosen], [across[i : i + 1] for i in chosen])
    fetch.wait()


def fold_body(keep_ref, got_ref, next_ref, send_ref, count, split):
    parts, squares = read_sums(keep_ref, count)
    more_parts, more_squares = read_sums(got_ref, count)
    parts = [x + y for x, y in zip(parts, more_parts)]
    squares = [x + y for x, y in zip(squares, more_squares)]
    for ref, first in ((next_ref, 0), (send_ref, 1)):
        chosen = range(first, count, 2) if split else range(count)
        write_sums(ref, [parts[i] for i in chosen], [squares[i] for i in chosen])


def latents_body(keep_ref, *rest):
    gots, out_ref = rest[:-1], rest[-1]
    count = len(rest)
    local = out_ref.shape[0] // count
    parts, squares = read_sums(keep_ref, count)
    for step, got in enumerate(gots, 1):
        more_parts, more_squares = read_sums(got, count)
        parts = [parts[i] + more_parts[i ^ step] for i in range(count)]
        squares = [squares[i] + more_squares[i ^ step] for i in range(count)]
    lane = lax.broadcasted_iota(jnp.int32, (local, C_LAT), 1)
    row = lax.broadcasted_iota(jnp.int32, (local, C_LAT), 0)
    done = []
    for part, square in zip(parts, squares):
        column = jnp.sum(jnp.where(lane == row, square, 0.0), axis=1, keepdims=True)
        done.append(part * lax.rsqrt(column / D + 1e-06))
    out_ref[...] = jnp.concatenate(done, axis=0).astype(jnp.bfloat16)


def convolve_body(
    rank_ref, in_weight_ref, in_bias_ref, mid_weight_ref, mid_bias_ref, *rest
):
    quarters, (out_ref, latents_ref, cols) = rest[:-3], rest[-3:]
    frame = latents_ref.shape[0] // F
    count = out_ref.shape[0] // len(quarters)
    local = quarters[0].shape[0] // count
    for low, quarter in enumerate(quarters):
        for high in range(count):
            block = rank_ref[0] ^ (high * len(quarters) + low)
            latents_ref[pl.ds(pl.multiple_of(block * local, 16), local), :] = quarter[
                high * local : (high + 1) * local, :
            ]
    own = mid_weight_ref.shape[1] // 9
    column = lax.broadcasted_iota(jnp.int32, (frame, C_LAT), 0) % W
    for index in range(F):
        cells = latents_ref[index * frame : (index + 1) * frame, :].astype(jnp.float32)
        shifted = (
            jnp.where(column == 0, 0.0, pltpu.roll(cells, 1, 0)),
            cells,
            jnp.where(column == W - 1, 0.0, pltpu.roll(cells, frame - 1, 0)),
        )
        blank = jnp.zeros((W, C_LAT), jnp.float32)
        for col_off, moved in enumerate(shifted):
            above = jnp.concatenate([blank, moved[:-W]], axis=0)
            below = jnp.concatenate([moved[W:], blank], axis=0)
            for row_off, piece in enumerate((above, moved, below)):
                at = ((index * 3 + row_off) * 3 + col_off) * C_LAT
                cols[:, at : at + C_LAT] = piece.astype(jnp.bfloat16)
    deep = 9 * C_LAT
    firsts = []
    actives = []
    for index in range(F):
        low = (F - 1 - index) * deep
        first = (
            dot_f32(cols[...], in_weight_ref[low : low + F * deep, :]) + in_bias_ref[...]
        ).astype(jnp.bfloat16)
        wide = first.astype(jnp.float32)
        firsts.append(first)
        actives.append((wide / (1.0 + jnp.exp(-wide))).astype(jnp.bfloat16))
    channel = lax.broadcasted_iota(jnp.int32, (own, CH), 1)
    mine = channel == lax.broadcasted_iota(jnp.int32, (own, CH), 0) + rank_ref[0] * own
    bias = jnp.sum(jnp.where(mine, mid_bias_ref[...], 0.0), axis=1, keepdims=True)
    chosen = jnp.where(mine, 1.0, 0.0).astype(jnp.bfloat16)
    spot = lax.broadcasted_iota(jnp.int32, (own, frame), 1)
    spot_column = spot % W
    outs = []
    for index in range(F):
        taps = sum(
            dot_f32(mid_weight_ref[source - index + 1], actives[source], 1, 1)
            for source in range(F)
        )
        total = None
        for col_off in range(3):
            merged = None
            for row_off in range(3):
                at = (row_off * 3 + col_off) * own
                piece = taps[at : at + own, :]
                if row_off == 0:
                    piece = jnp.where(spot < W, 0.0, pltpu.roll(piece, W, 1))
                elif row_off == 2:
                    piece = jnp.where(spot >= frame - W, 0.0, pltpu.roll(piece, frame - W, 1))
                merged = piece if merged is None else merged + piece
            if col_off == 0:
                merged = jnp.where(spot_column == 0, 0.0, pltpu.roll(merged, 1, 1))
            elif col_off == 2:
                merged = jnp.where(spot_column == W - 1, 0.0, pltpu.roll(merged, frame - 1, 1))
            total = merged if total is None else total + merged
        middle = (total + bias).astype(jnp.bfloat16).astype(jnp.float32)
        outs.append((dot_f32(chosen, firsts[index], 1, 1) + middle).astype(jnp.bfloat16))
    stacked = jnp.concatenate(outs, axis=0)
    source = lax.broadcasted_iota(jnp.int32, (F * own, 128), 0)
    target = lax.broadcasted_iota(jnp.int32, (F * own, 128), 1)
    inner = source % own
    place = (source // own) * own + (inner % 4) * (own // 4) + inner // 4
    moves = jnp.where(place == target % 64, 1.0, 0.0).astype(jnp.bfloat16)
    moved = dot_f32(stacked, moves, 0, 0).reshape(frame // W, W, 128)
    tail = jnp.concatenate([moved[:, 16:], jnp.zeros((frame // W, 32 - W, 128), jnp.float32)], axis=1)
    lane = lax.broadcasted_iota(jnp.int32, (frame // W, 16, 128), 2)
    out_ref[...] = jnp.where(lane < 64, moved[:, :16], tail).astype(jnp.bfloat16)


def shuffle_body(rows_ref, out_ref, wide):
    devices = rows_ref.shape[0]
    share = C_LAT // devices
    rows = rows_ref[...].astype(jnp.float32)
    lane = lax.broadcasted_iota(jnp.int32, (W, 128), 1) // share
    for index in range(F):
        for part in range(4):
            origin = (index * 4 + part) * share
            total = None
            for source in range(devices):
                shift = source * share - origin
                moved = jnp.concatenate(
                    [
                        pltpu.roll(rows[source], shift % 128, 1),
                        pltpu.roll(rows[source, : W - 16], (shift + 64) % 128, 1),
                    ],
                    axis=0,
                )
                total = moved if total is None else jnp.where(lane == source, moved, total)
            wide[index, part // 2, pl.ds(part % 2, W, stride=2), :] = total
    out_ref[0] = wide[...].astype(jnp.bfloat16)


def near(array):
    return pltpu.with_memory_space_constraint(array, pltpu.VMEM)


def far(array):
    return pltpu.with_memory_space_constraint(array, pltpu.HBM)


SCALAR = pl.BlockSpec(memory_space=pltpu.SMEM)
LOCAL = pl.BlockSpec(memory_space=pltpu.VMEM)
REMOTE = pl.BlockSpec(memory_space=pltpu.HBM)


def launch(body, name, outs, in_specs, operands, scratch=(), mib=8):
    return pl.pallas_call(
        body,
        out_shape=outs,
        in_specs=in_specs,
        out_specs=jax.tree.map(lambda _: LOCAL, outs),
        scratch_shapes=scratch,
        compiler_params=pltpu.CompilerParams(vmem_limit_bytes=mib << 20),
        name=name,
    )(*operands)


def exchange_order(devices):
    half = devices // 2
    order = [0, half]
    for step in range(1, half):
        order += [step, half + step]
    return order


def swap(array, step):
    devices = lax.axis_size("seq")
    return near(lax.ppermute(array, "seq", [(i, i ^ step) for i in range(devices)]))


def sums_shape(count, local, dtype):
    tail = 2 * count if dtype == jnp.bfloat16 else count
    return pltpu.VMEM((count * local + tail, C_LAT), dtype)


def whole_heads(
    query_rows, key_rows, value_rows, proj_weight, in_weight, in_bias, mid_weight, mid_bias
):
    devices = lax.axis_size("seq")
    local = query_rows.shape[0]
    span = D // devices
    frame = devices * local // F
    own = mid_weight.shape[4]
    rank = lax.axis_index("seq").reshape(1).astype(jnp.int32)
    order = exchange_order(devices)
    landed = []
    for steps in (order[1:3], order[3:] + order[:1]):
        blocks = launch(
            functools.partial(pack_body, steps=steps, span=span),
            "pack",
            [pltpu.VMEM((3, local, span), jnp.bfloat16)] * len(steps),
            [SCALAR] + [REMOTE] * 3,
            (rank, far(query_rows), far(key_rows), far(value_rows)),
            [pltpu.SemaphoreType.DMA((len(steps), 3))],
        )
        landed += [swap(block, step) if step else near(block) for block, step in zip(blocks, steps)]
    proj_rows = launch(
        slice_body,
        "slice",
        pltpu.VMEM((span, C_LAT), jnp.bfloat16),
        [SCALAR, REMOTE],
        (rank, far(proj_weight)),
        [pltpu.SemaphoreType.DMA(())],
    )
    half = devices // 2
    quarter = devices // 4
    keep, send, mid_near = launch(
        attend_body,
        "attend",
        [
            sums_shape(half, local, jnp.float32),
            sums_shape(half, local, jnp.bfloat16),
            pltpu.VMEM((3, 9 * own, CH), jnp.bfloat16),
        ],
        [REMOTE] + [LOCAL] * (1 + devices),
        (
            far(mid_weight.transpose(0, 1, 2, 4, 3).reshape(3, 9 * own, CH)),
            near(proj_rows),
            *landed,
        ),
        [pltpu.SemaphoreType.DMA(())],
        32,
    )
    keep, send = launch(
        functools.partial(fold_body, count=half, split=True),
        "fold_core",
        [sums_shape(quarter, local, jnp.float32), sums_shape(quarter, local, jnp.bfloat16)],
        [LOCAL] * 2,
        (near(keep), swap(send, 1)),
    )
    keep, send = launch(
        functools.partial(fold_body, count=quarter, split=False),
        "fold_pair",
        [sums_shape(quarter, local, jnp.float32), sums_shape(quarter, local, jnp.bfloat16)],
        [LOCAL] * 2,
        (near(keep), swap(send, 2)),
    )
    gots = [swap(send, 4 * step) for step in range(1, quarter)]
    ready = launch(
        latents_body,
        "latents",
        pltpu.VMEM((quarter * local, C_LAT), jnp.bfloat16),
        [LOCAL] * (1 + len(gots)),
        (near(keep), *gots),
    )
    paired = swap(ready, 2)
    columns = launch(
        convolve_body,
        "convolve",
        pltpu.VMEM((devices, 16, 128), jnp.bfloat16),
        [SCALAR] + [LOCAL] * 8,
        (
            rank,
            near(in_weight.reshape(27 * C_LAT, CH)),
            near(in_bias.reshape(1, CH)),
            near(mid_near),
            near(mid_bias.reshape(1, CH)),
            near(ready),
            swap(ready, 1),
            paired,
            swap(paired, 1),
        ),
        [
            pltpu.VMEM((devices * local, C_LAT), jnp.bfloat16),
            pltpu.VMEM((frame, F * 9 * C_LAT), jnp.bfloat16),
        ],
        32,
    )
    arrived = lax.all_to_all(columns, "seq", split_axis=0, concat_axis=0, tiled=True)
    return pl.pallas_call(
        shuffle_body,
        out_shape=jax.ShapeDtypeStruct((1, F, 2, 2 * W, C_LAT), jnp.bfloat16),
        in_specs=[LOCAL],
        out_specs=LOCAL,
        scratch_shapes=[pltpu.VMEM((F, 2, 2 * W, C_LAT), jnp.float32)],
        compiler_params=pltpu.CompilerParams(vmem_limit_bytes=8 << 20),
        name="shuffle",
    )(near(arrived))


def on_device(*operands):
    devices = lax.axis_size("seq")
    if devices > HEADS or devices < 16 or devices & (devices - 1):
        return shared_heads(*operands)
    return whole_heads(*operands)


def solution(mesh):
    return jax.shard_map(
        on_device,
        mesh=mesh,
        in_specs=(
            P(("groups", "seq"), None),
            P(("groups", "seq"), None),
            P(("groups", "seq"), None),
            P(),
            P(),
            P(),
            P(None, None, None, None, "seq"),
            P(),
        ),
        out_specs=P(("groups", "seq"), None, None, None, None),
        check_vma=False,
    )
```

```python
import functools
import math

import jax
import jax.numpy as jnp
from jax import lax
from jax.experimental import pallas as pl
from jax.experimental.pallas import tpu as pltpu
from jax.sharding import PartitionSpec as P


D = 4096
HEADS = 32
HD = 128
C_LAT = 128
CH = 512
W = 24
F = 2
HT = 1


def padded_2(block, sides, width):
    for axis, dim in sides:
        count = lax.axis_size(axis)
        forward = [(i, i + 1) for i in range(count - 1)]
        backward = [(target, source) for source, target in forward]
        low = lax.ppermute(
            lax.slice_in_dim(block, block.shape[dim] - width, None, axis=dim), axis, forward
        )
        high = lax.ppermute(lax.slice_in_dim(block, 0, width, axis=dim), axis, backward)
        block = jnp.concatenate([low, block, high], axis=dim)
    return block


def unfold(padded, frames, height, columns):
    pieces = [
        padded[
            frame_off : frame_off + frames, row_off : row_off + height, col_off : col_off + columns
        ]
        for frame_off in range(3)
        for row_off in range(3)
        for col_off in range(3)
    ]
    return jnp.concatenate(pieces, axis=-1).reshape(frames * height * columns, -1)


def normed_latents(token_rows, proj_weight):
    widened = token_rows.astype(jnp.float32)
    normed = (
        widened * lax.rsqrt(jnp.mean(widened * widened, axis=1, keepdims=True) + 1e-06)
    ).astype(jnp.bfloat16)
    return jnp.dot(normed, proj_weight, preferred_element_type=jnp.float32).astype(jnp.bfloat16)


def extend(tile_cells):
    bordered = padded_2(tile_cells, (("seq", 1),), 1)
    return jnp.pad(bordered, ((1, 1), (0, 0), (1, 1), (0, 0)))


def shuffle_tile(summed, frames, height, columns):
    channels = summed.shape[-1] // 4
    return (
        summed.reshape(frames, height, columns, channels, 2, 2)
        .transpose(0, 1, 4, 2, 5, 3)
        .reshape(frames, 2 * height, 2 * columns, channels)
    )


def shared_heads(
    query_rows, key_rows, value_rows, proj_weight, in_weight, in_bias, mid_weight, mid_bias
):
    devices = lax.axis_size("seq")
    halves = max(1, devices // HEADS)
    unit_count = HEADS * halves // devices
    local_tokens = query_rows.shape[0]
    shard_rows = local_tokens // W
    half_width = W // halves
    score_scale = 1.0 / math.sqrt(HD)

    def by_head(rows):
        shaped = rows.reshape(local_tokens, HEADS, HD).transpose(1, 0, 2)
        shaped = jnp.broadcast_to(shaped[:, None], (HEADS, halves, local_tokens, HD))
        return shaped.reshape(devices, unit_count, local_tokens, HD)

    shaped = query_rows.reshape(shard_rows, halves, half_width, HEADS, HD).transpose(3, 1, 0, 2, 4)
    query_units = lax.all_to_all(
        shaped.reshape(devices, unit_count, shard_rows, half_width, HD),
        "seq",
        split_axis=0,
        concat_axis=0,
        tiled=True,
    )
    key_units = lax.all_to_all(by_head(key_rows), "seq", split_axis=0, concat_axis=0, tiled=True)
    value_units = lax.all_to_all(
        by_head(value_rows), "seq", split_axis=0, concat_axis=0, tiled=True
    )
    key_heads = key_units.transpose(1, 0, 2, 3).reshape(unit_count, -1, HD)
    value_heads = value_units.transpose(1, 0, 2, 3).reshape(unit_count, -1, HD)
    query_total = devices * shard_rows * half_width
    block_rows = 512 if query_total % 512 == 0 else query_total
    query_heads = (
        query_units.transpose(1, 0, 2, 3, 4)
        .reshape(unit_count, query_total // block_rows, block_rows, HD)
        .transpose(1, 0, 2, 3)
    )

    def attend(query_block):
        scores = (
            jnp.einsum("uqd,ukd->uqk", query_block, key_heads, preferred_element_type=jnp.float32)
            * score_scale
        )
        largest = jnp.max(scores, axis=2, keepdims=True)
        weights = jnp.exp(scores - largest)
        totals = jnp.sum(weights, axis=2, keepdims=True)
        mixture = jnp.einsum(
            "uqk,ukd->uqd",
            weights.astype(jnp.bfloat16),
            value_heads,
            preferred_element_type=jnp.float32,
        )
        return (mixture / totals).astype(jnp.bfloat16)

    attended = lax.map(attend, query_heads)
    attended = attended.transpose(1, 0, 2, 3).reshape(
        unit_count, devices, shard_rows, half_width, HD
    )
    arranged = attended.reshape(unit_count, F, devices, HT, half_width, HD).transpose(
        2, 0, 1, 3, 4, 5
    )
    arrived = lax.all_to_all(arranged, "seq", split_axis=0, concat_axis=0, tiled=True)
    arrived = arrived.reshape(HEADS, halves, F, HT, half_width, HD).transpose(2, 3, 1, 4, 0, 5)
    latents = normed_latents(arrived.reshape(F * HT * W, D), proj_weight).reshape(F, HT, W, C_LAT)
    unfolded_in = unfold(extend(latents), F, HT, W)
    first = (
        jnp.dot(unfolded_in, in_weight.reshape(27 * C_LAT, CH), preferred_element_type=jnp.float32)
        + in_bias
    ).astype(jnp.bfloat16)
    active = jax.nn.silu(first.astype(jnp.float32)).astype(jnp.bfloat16)
    unfolded_mid = unfold(extend(active.reshape(F, HT, W, CH)), F, HT, W)
    piece = lax.all_gather(mid_weight, "seq", axis=4, tiled=True)
    column_span = piece.shape[4]
    middle = (
        jnp.dot(
            unfolded_mid, piece.reshape(27 * CH, column_span), preferred_element_type=jnp.float32
        )
        + mid_bias
    ).astype(jnp.bfloat16)
    summed = first.astype(jnp.float32) + middle.astype(jnp.float32)
    return shuffle_tile(summed, F, HT, W).astype(jnp.bfloat16)[None]


def dot_f32(left, right, left_dim=1, right_dim=0):
    return lax.dot_general(
        left, right, (((left_dim,), (right_dim,)), ((), ())), preferred_element_type=jnp.float32
    )


def pack_body(rank_ref, query_ref, key_ref, value_ref, *rest, steps, span):
    blocks, sems = rest[:-1], rest[-1]
    copies = []
    for place, step in enumerate(steps):
        start = pl.multiple_of((rank_ref[0] ^ step) * span, span)
        for which, ref in enumerate((query_ref, key_ref, value_ref)):
            copies.append(
                pltpu.make_async_copy(
                    ref.at[:, pl.ds(start, span)], blocks[place].at[which], sems.at[place, which]
                )
            )
    for copy in copies:
        copy.start()
    for copy in copies:
        copy.wait()


def slice_body(rank_ref, proj_ref, out_ref, sem):
    span = out_ref.shape[0]
    start = pl.multiple_of(rank_ref[0] * span, span)
    copy = pltpu.make_async_copy(proj_ref.at[pl.ds(start, span), :], out_ref, sem)
    copy.start()
    copy.wait()


def read_sums(ref, count):
    cells = ref.shape[0] - (2 if ref.dtype == jnp.bfloat16 else 1) * count
    parts = ref[:cells].astype(jnp.float32).reshape(count, cells // count, C_LAT)
    tail = ref[cells:].astype(jnp.float32)
    squares = tail[:count] + tail[count:] if ref.dtype == jnp.bfloat16 else tail
    return [parts[i] for i in range(count)], [squares[i : i + 1] for i in range(count)]


def write_sums(ref, parts, squares):
    cells = len(parts) * parts[0].shape[0]
    across = jnp.concatenate(squares, axis=0)
    if ref.dtype == jnp.bfloat16:
        coarse = across.astype(jnp.bfloat16).astype(jnp.float32)
        across = jnp.concatenate([coarse, across - coarse], axis=0)
    ref[:cells] = jnp.concatenate(parts, axis=0).astype(ref.dtype)
    ref[cells:] = across.astype(ref.dtype)


def stack(blocks, which, lanes):
    return jnp.concatenate([block[which, :, lanes] for block in blocks], axis=0)


def weigh(query, key, floor=None):
    scores = dot_f32(query, key, 1, 1) * (1.0 / math.sqrt(HD))
    largest = jnp.max(scores, axis=1, keepdims=True)
    if floor is not None:
        largest = jnp.maximum(largest, floor)
    weights = jnp.exp(scores - largest)
    return weights.astype(jnp.bfloat16), jnp.sum(weights, axis=1, keepdims=True), largest


def attend_early_body(mid_weight_ref, *rest, units):
    blocks, outs = rest[: -2 * units - 3], rest[-2 * units - 3 :]
    sum_ref, stats, (mid_ref, mid_sem) = outs[0], outs[1:-2], outs[-2:]
    fetch = pltpu.make_async_copy(mid_weight_ref, mid_ref, mid_sem)
    fetch.start()
    for unit in range(units):
        lanes = slice(unit * HD, (unit + 1) * HD)
        query, key, value = (stack(blocks, which, lanes) for which in range(3))
        weights, totals, largest = weigh(query, key)
        sum_ref[:, lanes] = dot_f32(weights, value)
        stats[2 * unit][...] = totals
        stats[2 * unit + 1][...] = largest
    fetch.wait()


def attend_late_body(proj_ref, sum_ref, *rest, units):
    stats, blocks, (keep_ref, send_ref) = rest[: 2 * units], rest[2 * units : -2], rest[-2:]
    devices = len(blocks)
    _, local, _ = blocks[0].shape
    tokens = devices * local
    ready = sum_ref.shape[0] // local
    early, late = blocks[:ready], blocks[ready:]
    heads = []
    for unit in range(units):
        lanes = slice(unit * HD, (unit + 1) * HD)
        totals, largest = stats[2 * unit][...], stats[2 * unit + 1][...]
        late_key, late_value = stack(late, 1, lanes), stack(late, 2, lanes)
        weights, more, highest = weigh(stack(early, 0, lanes), late_key, largest)
        shrink = jnp.exp(largest - highest)
        mixture = sum_ref[:, lanes] * shrink + dot_f32(weights, late_value)
        first = (mixture / (totals * shrink + more)).astype(jnp.bfloat16)
        weights, totals, _ = weigh(stack(late, 0, lanes), stack(blocks, 1, lanes))
        second = (dot_f32(weights, stack(blocks, 2, lanes)) / totals).astype(jnp.bfloat16)
        heads.append(jnp.concatenate([first, second], axis=0))
    attended = jnp.concatenate(heads, axis=1)
    widened = attended.astype(jnp.float32)
    squares = jnp.sum(widened * widened, axis=1, keepdims=True)
    partial = dot_f32(attended, proj_ref[...]).reshape(devices, local, C_LAT)
    lane = lax.broadcasted_iota(jnp.int32, (devices, local, C_LAT), 2)
    row = lax.broadcasted_iota(jnp.int32, (devices, local, C_LAT), 1)
    spread = jnp.broadcast_to(squares, (tokens, C_LAT)).reshape(devices, local, C_LAT)
    across = jnp.sum(jnp.where(lane == row, spread, 0.0), axis=1)
    order = exchange_order(devices)
    for ref, first in ((keep_ref, 0), (send_ref, 1)):
        chosen = [order.index(step) for step in range(first, devices, 2)]
        write_sums(ref, [partial[i] for i in chosen], [across[i : i + 1] for i in chosen])


def fold_body(keep_ref, got_ref, next_ref, send_ref, count, split):
    parts, squares = read_sums(keep_ref, count)
    more_parts, more_squares = read_sums(got_ref, count)
    parts = [x + y for x, y in zip(parts, more_parts)]
    squares = [x + y for x, y in zip(squares, more_squares)]
    for ref, first in ((next_ref, 0), (send_ref, 1)):
        chosen = range(first, count, 2) if split else range(count)
        write_sums(ref, [parts[i] for i in chosen], [squares[i] for i in chosen])


def latents_body(keep_ref, *rest):
    gots, out_ref = rest[:-1], rest[-1]
    count = len(rest)
    local = out_ref.shape[0] // count
    parts, squares = read_sums(keep_ref, count)
    for step, got in enumerate(gots, 1):
        more_parts, more_squares = read_sums(got, count)
        parts = [parts[i] + more_parts[i ^ step] for i in range(count)]
        squares = [squares[i] + more_squares[i ^ step] for i in range(count)]
    lane = lax.broadcasted_iota(jnp.int32, (local, C_LAT), 1)
    row = lax.broadcasted_iota(jnp.int32, (local, C_LAT), 0)
    done = []
    for part, square in zip(parts, squares):
        column = jnp.sum(jnp.where(lane == row, square, 0.0), axis=1, keepdims=True)
        done.append(part * lax.rsqrt(column / D + 1e-06))
    out_ref[...] = jnp.concatenate(done, axis=0).astype(jnp.bfloat16)


def convolve_body(
    rank_ref, in_weight_ref, in_bias_ref, mid_weight_ref, mid_bias_ref, *rest
):
    quarters, (out_ref, latents_ref, cols) = rest[:-3], rest[-3:]
    frame = latents_ref.shape[0] // F
    count = out_ref.shape[0] // len(quarters)
    local = quarters[0].shape[0] // count
    for low, quarter in enumerate(quarters):
        for high in range(count):
            block = rank_ref[0] ^ (high * len(quarters) + low)
            latents_ref[pl.ds(pl.multiple_of(block * local, 16), local), :] = quarter[
                high * local : (high + 1) * local, :
            ]
    own = mid_weight_ref.shape[1] // 9
    column = lax.broadcasted_iota(jnp.int32, (frame, C_LAT), 0) % W
    for index in range(F):
        cells = latents_ref[index * frame : (index + 1) * frame, :].astype(jnp.float32)
        shifted = (
            jnp.where(column == 0, 0.0, pltpu.roll(cells, 1, 0)),
            cells,
            jnp.where(column == W - 1, 0.0, pltpu.roll(cells, frame - 1, 0)),
        )
        blank = jnp.zeros((W, C_LAT), jnp.float32)
        for col_off, moved in enumerate(shifted):
            above = jnp.concatenate([blank, moved[:-W]], axis=0)
            below = jnp.concatenate([moved[W:], blank], axis=0)
            for row_off, piece in enumerate((above, moved, below)):
                at = ((index * 3 + row_off) * 3 + col_off) * C_LAT
                cols[:, at : at + C_LAT] = piece.astype(jnp.bfloat16)
    deep = 9 * C_LAT
    firsts = []
    actives = []
    for index in range(F):
        low = (F - 1 - index) * deep
        first = (
            dot_f32(cols[...], in_weight_ref[low : low + F * deep, :]) + in_bias_ref[...]
        ).astype(jnp.bfloat16)
        wide = first.astype(jnp.float32)
        firsts.append(first)
        actives.append((wide / (1.0 + jnp.exp(-wide))).astype(jnp.bfloat16))
    channel = lax.broadcasted_iota(jnp.int32, (own, CH), 1)
    mine = channel == lax.broadcasted_iota(jnp.int32, (own, CH), 0) + rank_ref[0] * own
    bias = jnp.sum(jnp.where(mine, mid_bias_ref[...], 0.0), axis=1, keepdims=True)
    chosen = jnp.where(mine, 1.0, 0.0).astype(jnp.bfloat16)
    spot = lax.broadcasted_iota(jnp.int32, (own, frame), 1)
    spot_column = spot % W
    outs = []
    for index in range(F):
        taps = sum(
            dot_f32(mid_weight_ref[source - index + 1], actives[source], 1, 1)
            for source in range(F)
        )
        total = None
        for col_off in range(3):
            merged = None
            for row_off in range(3):
                at = (row_off * 3 + col_off) * own
                piece = taps[at : at + own, :]
                if row_off == 0:
                    piece = jnp.where(spot < W, 0.0, pltpu.roll(piece, W, 1))
                elif row_off == 2:
                    piece = jnp.where(spot >= frame - W, 0.0, pltpu.roll(piece, frame - W, 1))
                merged = piece if merged is None else merged + piece
            if col_off == 0:
                merged = jnp.where(spot_column == 0, 0.0, pltpu.roll(merged, 1, 1))
            elif col_off == 2:
                merged = jnp.where(spot_column == W - 1, 0.0, pltpu.roll(merged, frame - 1, 1))
            total = merged if total is None else total + merged
        middle = (total + bias).astype(jnp.bfloat16).astype(jnp.float32)
        outs.append((dot_f32(chosen, firsts[index], 1, 1) + middle).astype(jnp.bfloat16))
    stacked = jnp.concatenate(outs, axis=0)
    source = lax.broadcasted_iota(jnp.int32, (F * own, 128), 0)
    target = lax.broadcasted_iota(jnp.int32, (F * own, 128), 1)
    inner = source % own
    place = (source // own) * own + (inner % 4) * (own // 4) + inner // 4
    moves = jnp.where(place == target % 64, 1.0, 0.0).astype(jnp.bfloat16)
    moved = dot_f32(stacked, moves, 0, 0).reshape(frame // W, W, 128)
    tail = jnp.concatenate([moved[:, 16:], jnp.zeros((frame // W, 32 - W, 128), jnp.float32)], axis=1)
    lane = lax.broadcasted_iota(jnp.int32, (frame // W, 16, 128), 2)
    out_ref[...] = jnp.where(lane < 64, moved[:, :16], tail).astype(jnp.bfloat16)


def shuffle_body(rows_ref, out_ref, wide):
    devices = rows_ref.shape[0]
    share = C_LAT // devices
    rows = rows_ref[...].astype(jnp.float32)
    lane = lax.broadcasted_iota(jnp.int32, (W, 128), 1) // share
    for index in range(F):
        for part in range(4):
            origin = (index * 4 + part) * share
            total = None
            for source in range(devices):
                shift = source * share - origin
                moved = jnp.concatenate(
                    [
                        pltpu.roll(rows[source], shift % 128, 1),
                        pltpu.roll(rows[source, : W - 16], (shift + 64) % 128, 1),
                    ],
                    axis=0,
                )
                total = moved if total is None else jnp.where(lane == source, moved, total)
            wide[index, part // 2, pl.ds(part % 2, W, stride=2), :] = total
    out_ref[0] = wide[...].astype(jnp.bfloat16)


def near(array):
    return pltpu.with_memory_space_constraint(array, pltpu.VMEM)


def far(array):
    return pltpu.with_memory_space_constraint(array, pltpu.HBM)


SCALAR = pl.BlockSpec(memory_space=pltpu.SMEM)
LOCAL = pl.BlockSpec(memory_space=pltpu.VMEM)
REMOTE = pl.BlockSpec(memory_space=pltpu.HBM)


def launch(body, name, outs, in_specs, operands, scratch=(), mib=8):
    return pl.pallas_call(
        body,
        out_shape=outs,
        in_specs=in_specs,
        out_specs=jax.tree.map(lambda _: LOCAL, outs),
        scratch_shapes=scratch,
        compiler_params=pltpu.CompilerParams(vmem_limit_bytes=mib << 20),
        name=name,
    )(*operands)


def exchange_order(devices):
    half = devices // 2
    order = [0, half]
    for step in range(1, half):
        order += [step, half + step]
    return order


def swap(array, step):
    devices = lax.axis_size("seq")
    return near(lax.ppermute(array, "seq", [(i, i ^ step) for i in range(devices)]))


def sums_shape(count, local, dtype):
    tail = 2 * count if dtype == jnp.bfloat16 else count
    return pltpu.VMEM((count * local + tail, C_LAT), dtype)


def whole_heads(
    query_rows, key_rows, value_rows, proj_weight, in_weight, in_bias, mid_weight, mid_bias
):
    devices = lax.axis_size("seq")
    local = query_rows.shape[0]
    span = D // devices
    frame = devices * local // F
    own = mid_weight.shape[4]
    rank = lax.axis_index("seq").reshape(1).astype(jnp.int32)
    order = exchange_order(devices)
    blocks = launch(
        functools.partial(pack_body, steps=order, span=span),
        "pack",
        [pltpu.VMEM((3, local, span), jnp.bfloat16)] * devices,
        [SCALAR] + [REMOTE] * 3,
        (rank, far(query_rows), far(key_rows), far(value_rows)),
        [pltpu.SemaphoreType.DMA((devices, 3))],
    )
    landed = [swap(block, step) if step else near(block) for block, step in zip(blocks, order)]
    proj_rows = launch(
        slice_body,
        "slice",
        pltpu.VMEM((span, C_LAT), jnp.bfloat16),
        [SCALAR, REMOTE],
        (rank, far(proj_weight)),
        [pltpu.SemaphoreType.DMA(())],
    )
    half = devices // 2
    quarter = devices // 4
    units = span // HD
    ready = devices - max(1, devices // 8)
    mixture, *stats, mid_near = launch(
        functools.partial(attend_early_body, units=units),
        "attend_early",
        [pltpu.VMEM((ready * local, span), jnp.float32)]
        + [pltpu.VMEM((ready * local, 1), jnp.float32)] * (2 * units)
        + [pltpu.VMEM((3, 9 * own, CH), jnp.bfloat16)],
        [REMOTE] + [LOCAL] * ready,
        (far(mid_weight.transpose(0, 1, 2, 4, 3).reshape(3, 9 * own, CH)), *landed[:ready]),
        [pltpu.SemaphoreType.DMA(())],
        24,
    )
    keep, send = launch(
        functools.partial(attend_late_body, units=units),
        "attend_late",
        [sums_shape(half, local, jnp.float32), sums_shape(half, local, jnp.bfloat16)],
        [LOCAL] * (2 + 2 * units + devices),
        (near(proj_rows), near(mixture), *[near(stat) for stat in stats], *landed),
        mib=24,
    )
    keep, send = launch(
        functools.partial(fold_body, count=half, split=True),
        "fold_core",
        [sums_shape(quarter, local, jnp.float32), sums_shape(quarter, local, jnp.bfloat16)],
        [LOCAL] * 2,
        (near(keep), swap(send, 1)),
    )
    keep, send = launch(
        functools.partial(fold_body, count=quarter, split=False),
        "fold_pair",
        [sums_shape(quarter, local, jnp.float32), sums_shape(quarter, local, jnp.bfloat16)],
        [LOCAL] * 2,
        (near(keep), swap(send, 2)),
    )
    gots = [swap(send, 4 * step) for step in range(1, quarter)]
    ready = launch(
        latents_body,
        "latents",
        pltpu.VMEM((quarter * local, C_LAT), jnp.bfloat16),
        [LOCAL] * (1 + len(gots)),
        (near(keep), *gots),
    )
    paired = swap(ready, 2)
    columns = launch(
        convolve_body,
        "convolve",
        pltpu.VMEM((devices, 16, 128), jnp.bfloat16),
        [SCALAR] + [LOCAL] * 8,
        (
            rank,
            near(in_weight.reshape(27 * C_LAT, CH)),
            near(in_bias.reshape(1, CH)),
            near(mid_near),
            near(mid_bias.reshape(1, CH)),
            near(ready),
            swap(ready, 1),
            paired,
            swap(paired, 1),
        ),
        [
            pltpu.VMEM((devices * local, C_LAT), jnp.bfloat16),
            pltpu.VMEM((frame, F * 9 * C_LAT), jnp.bfloat16),
        ],
        32,
    )
    arrived = lax.all_to_all(columns, "seq", split_axis=0, concat_axis=0, tiled=True)
    return pl.pallas_call(
        shuffle_body,
        out_shape=jax.ShapeDtypeStruct((1, F, 2, 2 * W, C_LAT), jnp.bfloat16),
        in_specs=[LOCAL],
        out_specs=LOCAL,
        scratch_shapes=[pltpu.VMEM((F, 2, 2 * W, C_LAT), jnp.float32)],
        compiler_params=pltpu.CompilerParams(vmem_limit_bytes=8 << 20),
        name="shuffle",
    )(near(arrived))


def on_device(*operands):
    devices = lax.axis_size("seq")
    if devices > HEADS or devices < 16 or devices & (devices - 1):
        return shared_heads(*operands)
    return whole_heads(*operands)


def solution(mesh):
    return jax.shard_map(
        on_device,
        mesh=mesh,
        in_specs=(
            P(("groups", "seq"), None),
            P(("groups", "seq"), None),
            P(("groups", "seq"), None),
            P(),
            P(),
            P(),
            P(None, None, None, None, "seq"),
            P(),
        ),
        out_specs=P(("groups", "seq"), None, None, None, None),
        check_vma=False,
    )
```

```python
import functools
import math

import jax
import jax.numpy as jnp
from jax import lax
from jax.experimental import pallas as pl
from jax.experimental.pallas import tpu as pltpu
from jax.sharding import PartitionSpec as P


D = 4096
HEADS = 32
HD = 128
C_LAT = 128
CH = 512
W = 24
F = 2
HT = 1


def padded_2(block, sides, width):
    for axis, dim in sides:
        count = lax.axis_size(axis)
        forward = [(i, i + 1) for i in range(count - 1)]
        backward = [(target, source) for source, target in forward]
        low = lax.ppermute(
            lax.slice_in_dim(block, block.shape[dim] - width, None, axis=dim), axis, forward
        )
        high = lax.ppermute(lax.slice_in_dim(block, 0, width, axis=dim), axis, backward)
        block = jnp.concatenate([low, block, high], axis=dim)
    return block


def unfold(padded, frames, height, columns):
    pieces = [
        padded[
            frame_off : frame_off + frames, row_off : row_off + height, col_off : col_off + columns
        ]
        for frame_off in range(3)
        for row_off in range(3)
        for col_off in range(3)
    ]
    return jnp.concatenate(pieces, axis=-1).reshape(frames * height * columns, -1)


def normed_latents(token_rows, proj_weight):
    widened = token_rows.astype(jnp.float32)
    normed = (
        widened * lax.rsqrt(jnp.mean(widened * widened, axis=1, keepdims=True) + 1e-06)
    ).astype(jnp.bfloat16)
    return jnp.dot(normed, proj_weight, preferred_element_type=jnp.float32).astype(jnp.bfloat16)


def extend(tile_cells):
    bordered = padded_2(tile_cells, (("seq", 1),), 1)
    return jnp.pad(bordered, ((1, 1), (0, 0), (1, 1), (0, 0)))


def shuffle_tile(summed, frames, height, columns):
    channels = summed.shape[-1] // 4
    return (
        summed.reshape(frames, height, columns, channels, 2, 2)
        .transpose(0, 1, 4, 2, 5, 3)
        .reshape(frames, 2 * height, 2 * columns, channels)
    )


def shared_heads(
    query_rows, key_rows, value_rows, proj_weight, in_weight, in_bias, mid_weight, mid_bias
):
    devices = lax.axis_size("seq")
    halves = max(1, devices // HEADS)
    unit_count = HEADS * halves // devices
    local_tokens = query_rows.shape[0]
    shard_rows = local_tokens // W
    half_width = W // halves
    score_scale = 1.0 / math.sqrt(HD)

    def by_head(rows):
        shaped = rows.reshape(local_tokens, HEADS, HD).transpose(1, 0, 2)
        shaped = jnp.broadcast_to(shaped[:, None], (HEADS, halves, local_tokens, HD))
        return shaped.reshape(devices, unit_count, local_tokens, HD)

    shaped = query_rows.reshape(shard_rows, halves, half_width, HEADS, HD).transpose(3, 1, 0, 2, 4)
    query_units = lax.all_to_all(
        shaped.reshape(devices, unit_count, shard_rows, half_width, HD),
        "seq",
        split_axis=0,
        concat_axis=0,
        tiled=True,
    )
    key_units = lax.all_to_all(by_head(key_rows), "seq", split_axis=0, concat_axis=0, tiled=True)
    value_units = lax.all_to_all(
        by_head(value_rows), "seq", split_axis=0, concat_axis=0, tiled=True
    )
    key_heads = key_units.transpose(1, 0, 2, 3).reshape(unit_count, -1, HD)
    value_heads = value_units.transpose(1, 0, 2, 3).reshape(unit_count, -1, HD)
    query_total = devices * shard_rows * half_width
    block_rows = 512 if query_total % 512 == 0 else query_total
    query_heads = (
        query_units.transpose(1, 0, 2, 3, 4)
        .reshape(unit_count, query_total // block_rows, block_rows, HD)
        .transpose(1, 0, 2, 3)
    )

    def attend(query_block):
        scores = (
            jnp.einsum("uqd,ukd->uqk", query_block, key_heads, preferred_element_type=jnp.float32)
            * score_scale
        )
        largest = jnp.max(scores, axis=2, keepdims=True)
        weights = jnp.exp(scores - largest)
        totals = jnp.sum(weights, axis=2, keepdims=True)
        mixture = jnp.einsum(
            "uqk,ukd->uqd",
            weights.astype(jnp.bfloat16),
            value_heads,
            preferred_element_type=jnp.float32,
        )
        return (mixture / totals).astype(jnp.bfloat16)

    attended = lax.map(attend, query_heads)
    attended = attended.transpose(1, 0, 2, 3).reshape(
        unit_count, devices, shard_rows, half_width, HD
    )
    arranged = attended.reshape(unit_count, F, devices, HT, half_width, HD).transpose(
        2, 0, 1, 3, 4, 5
    )
    arrived = lax.all_to_all(arranged, "seq", split_axis=0, concat_axis=0, tiled=True)
    arrived = arrived.reshape(HEADS, halves, F, HT, half_width, HD).transpose(2, 3, 1, 4, 0, 5)
    latents = normed_latents(arrived.reshape(F * HT * W, D), proj_weight).reshape(F, HT, W, C_LAT)
    unfolded_in = unfold(extend(latents), F, HT, W)
    first = (
        jnp.dot(unfolded_in, in_weight.reshape(27 * C_LAT, CH), preferred_element_type=jnp.float32)
        + in_bias
    ).astype(jnp.bfloat16)
    active = jax.nn.silu(first.astype(jnp.float32)).astype(jnp.bfloat16)
    unfolded_mid = unfold(extend(active.reshape(F, HT, W, CH)), F, HT, W)
    piece = lax.all_gather(mid_weight, "seq", axis=4, tiled=True)
    column_span = piece.shape[4]
    middle = (
        jnp.dot(
            unfolded_mid, piece.reshape(27 * CH, column_span), preferred_element_type=jnp.float32
        )
        + mid_bias
    ).astype(jnp.bfloat16)
    summed = first.astype(jnp.float32) + middle.astype(jnp.float32)
    return shuffle_tile(summed, F, HT, W).astype(jnp.bfloat16)[None]


def dot_f32(left, right, left_dim=1, right_dim=0):
    return lax.dot_general(
        left, right, (((left_dim,), (right_dim,)), ((), ())), preferred_element_type=jnp.float32
    )


def pack_body(rank_ref, query_ref, key_ref, value_ref, *rest, plan, span):
    blocks, sems = rest[:-1], rest[-1]
    sources = (query_ref, key_ref, value_ref)
    copies = []
    for place, (step, which) in enumerate(plan):
        start = pl.multiple_of((rank_ref[0] ^ step) * span, span)
        for slot, index in enumerate(which):
            copies.append(
                pltpu.make_async_copy(
                    sources[index].at[:, pl.ds(start, span)],
                    blocks[place].at[slot],
                    sems.at[place, slot],
                )
            )
    for copy in copies:
        copy.start()
    for copy in copies:
        copy.wait()


def slice_body(rank_ref, proj_ref, out_ref, sem):
    span = out_ref.shape[0]
    start = pl.multiple_of(rank_ref[0] * span, span)
    copy = pltpu.make_async_copy(proj_ref.at[pl.ds(start, span), :], out_ref, sem)
    copy.start()
    copy.wait()


def read_sums(ref, count):
    cells = ref.shape[0] - (2 if ref.dtype == jnp.bfloat16 else 1) * count
    parts = ref[:cells].astype(jnp.float32).reshape(count, cells // count, C_LAT)
    tail = ref[cells:].astype(jnp.float32)
    squares = tail[:count] + tail[count:] if ref.dtype == jnp.bfloat16 else tail
    return [parts[i] for i in range(count)], [squares[i : i + 1] for i in range(count)]


def write_sums(ref, parts, squares):
    cells = len(parts) * parts[0].shape[0]
    across = jnp.concatenate(squares, axis=0)
    if ref.dtype == jnp.bfloat16:
        coarse = across.astype(jnp.bfloat16).astype(jnp.float32)
        across = jnp.concatenate([coarse, across - coarse], axis=0)
    ref[:cells] = jnp.concatenate(parts, axis=0).astype(ref.dtype)
    ref[cells:] = across.astype(ref.dtype)


def stack(blocks, which, lanes):
    return jnp.concatenate([block[block.shape[0] - 3 + which, :, lanes] for block in blocks], axis=0)


def attend_rows(query_blocks, pair_blocks, proj_ref):
    count = len(query_blocks)
    _, local, span = query_blocks[0].shape
    heads = []
    for unit in range(span // HD):
        lanes = slice(unit * HD, (unit + 1) * HD)
        query = jnp.concatenate([block[0, :, lanes] for block in query_blocks], axis=0)
        scores = dot_f32(query, stack(pair_blocks, 1, lanes), 1, 1) * (1.0 / math.sqrt(HD))
        weights = jnp.exp(scores - jnp.max(scores, axis=1, keepdims=True))
        totals = jnp.sum(weights, axis=1, keepdims=True)
        mixture = dot_f32(weights.astype(jnp.bfloat16), stack(pair_blocks, 2, lanes))
        heads.append((mixture / totals).astype(jnp.bfloat16))
    attended = jnp.concatenate(heads, axis=1)
    widened = attended.astype(jnp.float32)
    squares = jnp.sum(widened * widened, axis=1, keepdims=True)
    partial = dot_f32(attended, proj_ref[...]).reshape(count, local, C_LAT)
    lane = lax.broadcasted_iota(jnp.int32, (count, local, C_LAT), 2)
    row = lax.broadcasted_iota(jnp.int32, (count, local, C_LAT), 1)
    spread = jnp.broadcast_to(squares, (count * local, C_LAT)).reshape(count, local, C_LAT)
    across = jnp.sum(jnp.where(lane == row, spread, 0.0), axis=1)
    return [partial[i] for i in range(count)], [across[i : i + 1] for i in range(count)]


def attend_early_body(mid_weight_ref, proj_ref, *rest, early):
    pairs, (sums_ref, mid_ref, mid_sem) = rest[:-3], rest[-3:]
    fetch = pltpu.make_async_copy(mid_weight_ref, mid_ref, mid_sem)
    fetch.start()
    write_sums(sums_ref, *attend_rows(pairs[:early], pairs, proj_ref))
    fetch.wait()


def attend_late_body(proj_ref, sums_ref, *rest, early, order):
    devices = len(order)
    pairs, queries, (keep_ref, send_ref) = rest[:devices], rest[devices:-2], rest[-2:]
    parts, squares = read_sums(sums_ref, early)
    more_parts, more_squares = attend_rows(queries, pairs, proj_ref)
    parts, squares = parts + more_parts, squares + more_squares
    for ref, first in ((keep_ref, 0), (send_ref, 1)):
        chosen = [order.index(step) for step in range(first, devices, 2)]
        write_sums(ref, [parts[i] for i in chosen], [squares[i] for i in chosen])


def fold_body(keep_ref, got_ref, next_ref, send_ref, count, split):
    parts, squares = read_sums(keep_ref, count)
    more_parts, more_squares = read_sums(got_ref, count)
    parts = [x + y for x, y in zip(parts, more_parts)]
    squares = [x + y for x, y in zip(squares, more_squares)]
    for ref, first in ((next_ref, 0), (send_ref, 1)):
        chosen = range(first, count, 2) if split else range(count)
        write_sums(ref, [parts[i] for i in chosen], [squares[i] for i in chosen])


def latents_body(keep_ref, *rest):
    gots, out_ref = rest[:-1], rest[-1]
    count = len(rest)
    local = out_ref.shape[0] // count
    parts, squares = read_sums(keep_ref, count)
    for step, got in enumerate(gots, 1):
        more_parts, more_squares = read_sums(got, count)
        parts = [parts[i] + more_parts[i ^ step] for i in range(count)]
        squares = [squares[i] + more_squares[i ^ step] for i in range(count)]
    lane = lax.broadcasted_iota(jnp.int32, (local, C_LAT), 1)
    row = lax.broadcasted_iota(jnp.int32, (local, C_LAT), 0)
    done = []
    for part, square in zip(parts, squares):
        column = jnp.sum(jnp.where(lane == row, square, 0.0), axis=1, keepdims=True)
        done.append(part * lax.rsqrt(column / D + 1e-06))
    out_ref[...] = jnp.concatenate(done, axis=0).astype(jnp.bfloat16)


def convolve_body(
    rank_ref, in_weight_ref, in_bias_ref, mid_weight_ref, mid_bias_ref, *rest
):
    quarters, (out_ref, latents_ref, cols) = rest[:-3], rest[-3:]
    frame = latents_ref.shape[0] // F
    count = out_ref.shape[0] // len(quarters)
    local = quarters[0].shape[0] // count
    for low, quarter in enumerate(quarters):
        for high in range(count):
            block = rank_ref[0] ^ (high * len(quarters) + low)
            latents_ref[pl.ds(pl.multiple_of(block * local, 16), local), :] = quarter[
                high * local : (high + 1) * local, :
            ]
    own = mid_weight_ref.shape[1] // 9
    column = lax.broadcasted_iota(jnp.int32, (frame, C_LAT), 0) % W
    for index in range(F):
        cells = latents_ref[index * frame : (index + 1) * frame, :].astype(jnp.float32)
        shifted = (
            jnp.where(column == 0, 0.0, pltpu.roll(cells, 1, 0)),
            cells,
            jnp.where(column == W - 1, 0.0, pltpu.roll(cells, frame - 1, 0)),
        )
        blank = jnp.zeros((W, C_LAT), jnp.float32)
        for col_off, moved in enumerate(shifted):
            above = jnp.concatenate([blank, moved[:-W]], axis=0)
            below = jnp.concatenate([moved[W:], blank], axis=0)
            for row_off, piece in enumerate((above, moved, below)):
                at = ((index * 3 + row_off) * 3 + col_off) * C_LAT
                cols[:, at : at + C_LAT] = piece.astype(jnp.bfloat16)
    deep = 9 * C_LAT
    firsts = []
    actives = []
    for index in range(F):
        low = (F - 1 - index) * deep
        first = (
            dot_f32(cols[...], in_weight_ref[low : low + F * deep, :]) + in_bias_ref[...]
        ).astype(jnp.bfloat16)
        wide = first.astype(jnp.float32)
        firsts.append(first)
        actives.append((wide / (1.0 + jnp.exp(-wide))).astype(jnp.bfloat16))
    channel = lax.broadcasted_iota(jnp.int32, (own, CH), 1)
    mine = channel == lax.broadcasted_iota(jnp.int32, (own, CH), 0) + rank_ref[0] * own
    bias = jnp.sum(jnp.where(mine, mid_bias_ref[...], 0.0), axis=1, keepdims=True)
    chosen = jnp.where(mine, 1.0, 0.0).astype(jnp.bfloat16)
    spot = lax.broadcasted_iota(jnp.int32, (own, frame), 1)
    spot_column = spot % W
    outs = []
    for index in range(F):
        taps = sum(
            dot_f32(mid_weight_ref[source - index + 1], actives[source], 1, 1)
            for source in range(F)
        )
        total = None
        for col_off in range(3):
            merged = None
            for row_off in range(3):
                at = (row_off * 3 + col_off) * own
                piece = taps[at : at + own, :]
                if row_off == 0:
                    piece = jnp.where(spot < W, 0.0, pltpu.roll(piece, W, 1))
                elif row_off == 2:
                    piece = jnp.where(spot >= frame - W, 0.0, pltpu.roll(piece, frame - W, 1))
                merged = piece if merged is None else merged + piece
            if col_off == 0:
                merged = jnp.where(spot_column == 0, 0.0, pltpu.roll(merged, 1, 1))
            elif col_off == 2:
                merged = jnp.where(spot_column == W - 1, 0.0, pltpu.roll(merged, frame - 1, 1))
            total = merged if total is None else total + merged
        middle = (total + bias).astype(jnp.bfloat16).astype(jnp.float32)
        outs.append((dot_f32(chosen, firsts[index], 1, 1) + middle).astype(jnp.bfloat16))
    stacked = jnp.concatenate(outs, axis=0)
    source = lax.broadcasted_iota(jnp.int32, (F * own, 128), 0)
    target = lax.broadcasted_iota(jnp.int32, (F * own, 128), 1)
    inner = source % own
    place = (source // own) * own + (inner % 4) * (own // 4) + inner // 4
    moves = jnp.where(place == target % 64, 1.0, 0.0).astype(jnp.bfloat16)
    moved = dot_f32(stacked, moves, 0, 0).reshape(frame // W, W, 128)
    tail = jnp.concatenate([moved[:, 16:], jnp.zeros((frame // W, 32 - W, 128), jnp.float32)], axis=1)
    lane = lax.broadcasted_iota(jnp.int32, (frame // W, 16, 128), 2)
    out_ref[...] = jnp.where(lane < 64, moved[:, :16], tail).astype(jnp.bfloat16)


def shuffle_body(rows_ref, out_ref, wide):
    devices = rows_ref.shape[0]
    share = C_LAT // devices
    rows = rows_ref[...].astype(jnp.float32)
    lane = lax.broadcasted_iota(jnp.int32, (W, 128), 1) // share
    for index in range(F):
        for part in range(4):
            origin = (index * 4 + part) * share
            total = None
            for source in range(devices):
                shift = source * share - origin
                moved = jnp.concatenate(
                    [
                        pltpu.roll(rows[source], shift % 128, 1),
                        pltpu.roll(rows[source, : W - 16], (shift + 64) % 128, 1),
                    ],
                    axis=0,
                )
                total = moved if total is None else jnp.where(lane == source, moved, total)
            wide[index, part // 2, pl.ds(part % 2, W, stride=2), :] = total
    out_ref[0] = wide[...].astype(jnp.bfloat16)


def near(array):
    return pltpu.with_memory_space_constraint(array, pltpu.VMEM)


def far(array):
    return pltpu.with_memory_space_constraint(array, pltpu.HBM)


SCALAR = pl.BlockSpec(memory_space=pltpu.SMEM)
LOCAL = pl.BlockSpec(memory_space=pltpu.VMEM)
REMOTE = pl.BlockSpec(memory_space=pltpu.HBM)


def launch(body, outs, in_specs, operands, scratch=(), mib=8):
    return pl.pallas_call(
        body,
        out_shape=outs,
        in_specs=in_specs,
        out_specs=jax.tree.map(lambda _: LOCAL, outs),
        scratch_shapes=scratch,
        compiler_params=pltpu.CompilerParams(vmem_limit_bytes=mib << 20),
    )(*operands)


def exchange_order(devices):
    half = devices // 2
    order = [0, half]
    for step in range(1, half):
        order += [step, half + step]
    return order


def swap(array, step):
    devices = lax.axis_size("seq")
    return near(lax.ppermute(array, "seq", [(i, i ^ step) for i in range(devices)]))


def sums_shape(count, local, dtype):
    tail = 2 * count if dtype == jnp.bfloat16 else count
    return pltpu.VMEM((count * local + tail, C_LAT), dtype)


def whole_heads(
    query_rows, key_rows, value_rows, proj_weight, in_weight, in_bias, mid_weight, mid_bias
):
    devices = lax.axis_size("seq")
    local = query_rows.shape[0]
    span = D // devices
    frame = devices * local // F
    own = mid_weight.shape[4]
    rank = lax.axis_index("seq").reshape(1).astype(jnp.int32)
    order = exchange_order(devices)
    early = devices - devices // 4
    plan = [(step, (0, 1, 2)) for step in order[:early]]
    plan += [(step, (1, 2)) for step in order[early:]] + [(step, (0,)) for step in order[early:]]
    blocks = launch(
        functools.partial(pack_body, plan=plan, span=span),
        [pltpu.VMEM((len(which), local, span), jnp.bfloat16) for _, which in plan],
        [SCALAR] + [REMOTE] * 3,
        (rank, far(query_rows), far(key_rows), far(value_rows)),
        [pltpu.SemaphoreType.DMA((len(plan), 3))],
    )
    landed = [swap(block, step) if step else near(block) for block, (step, _) in zip(blocks, plan)]
    proj_rows = launch(
        slice_body,
        pltpu.VMEM((span, C_LAT), jnp.bfloat16),
        [SCALAR, REMOTE],
        (rank, far(proj_weight)),
        [pltpu.SemaphoreType.DMA(())],
    )
    half = devices // 2
    quarter = devices // 4
    sums, mid_near = launch(
        functools.partial(attend_early_body, early=early),
        [sums_shape(early, local, jnp.float32), pltpu.VMEM((3, 9 * own, CH), jnp.bfloat16)],
        [REMOTE] + [LOCAL] * (1 + devices),
        (
            far(mid_weight.transpose(0, 1, 2, 4, 3).reshape(3, 9 * own, CH)),
            near(proj_rows),
            *landed[:devices],
        ),
        [pltpu.SemaphoreType.DMA(())],
        28,
    )
    keep, send = launch(
        functools.partial(attend_late_body, early=early, order=order),
        [sums_shape(half, local, jnp.float32), sums_shape(half, local, jnp.bfloat16)],
        [LOCAL] * (2 + len(plan)),
        (near(proj_rows), near(sums), *landed),
        mib=20,
    )
    keep, send = launch(
        functools.partial(fold_body, count=half, split=True),
        [sums_shape(quarter, local, jnp.float32), sums_shape(quarter, local, jnp.bfloat16)],
        [LOCAL] * 2,
        (near(keep), swap(send, 1)),
    )
    keep, send = launch(
        functools.partial(fold_body, count=quarter, split=False),
        [sums_shape(quarter, local, jnp.float32), sums_shape(quarter, local, jnp.bfloat16)],
        [LOCAL] * 2,
        (near(keep), swap(send, 2)),
    )
    gots = []
    for step in range(1, quarter):
        gots.append(swap(send, 4 * step))
    ready = launch(
        latents_body,
        pltpu.VMEM((quarter * local, C_LAT), jnp.bfloat16),
        [LOCAL] * (1 + len(gots)),
        (near(keep), *gots),
    )
    paired = swap(ready, 2)
    columns = launch(
        convolve_body,
        pltpu.VMEM((devices, 16, 128), jnp.bfloat16),
        [SCALAR] + [LOCAL] * 8,
        (
            rank,
            near(in_weight.reshape(27 * C_LAT, CH)),
            near(in_bias.reshape(1, CH)),
            near(mid_near),
            near(mid_bias.reshape(1, CH)),
            near(ready),
            swap(ready, 1),
            paired,
            swap(paired, 1),
        ),
        [
            pltpu.VMEM((devices * local, C_LAT), jnp.bfloat16),
            pltpu.VMEM((frame, F * 9 * C_LAT), jnp.bfloat16),
        ],
        32,
    )
    arrived = lax.all_to_all(columns, "seq", split_axis=0, concat_axis=0, tiled=True)
    return pl.pallas_call(
        shuffle_body,
        out_shape=jax.ShapeDtypeStruct((1, F, 2, 2 * W, C_LAT), jnp.bfloat16),
        in_specs=[LOCAL],
        out_specs=LOCAL,
        scratch_shapes=[pltpu.VMEM((F, 2, 2 * W, C_LAT), jnp.float32)],
        compiler_params=pltpu.CompilerParams(vmem_limit_bytes=8 << 20),
        name="shuffle",
    )(near(arrived))


def local_heads(devices):
    return 16 <= devices <= HEADS and devices & (devices - 1) == 0


def on_device(*operands):
    if not local_heads(lax.axis_size("seq")):
        return shared_heads(*operands)
    return whole_heads(*operands)


def solution(mesh):
    return jax.shard_map(
        on_device,
        mesh=mesh,
        in_specs=(
            P(("groups", "seq"), None),
            P(("groups", "seq"), None),
            P(("groups", "seq"), None),
            P(),
            P(),
            P(),
            P(None, None, None, None, "seq"),
            P(),
        ),
        out_specs=P(("groups", "seq"), None, None, None, None),
        check_vma=False,
    )
```

```python
import functools
import math

import jax
import jax.numpy as jnp
from jax import lax
from jax.experimental import pallas as pl
from jax.experimental.pallas import tpu as pltpu
from jax.sharding import PartitionSpec as P


D = 4096
HEADS = 32
HD = 128
C_LAT = 128
CH = 512
W = 24
F = 2
HT = 1


def padded_2(block, sides, width):
    for axis, dim in sides:
        count = lax.axis_size(axis)
        forward = [(i, i + 1) for i in range(count - 1)]
        backward = [(target, source) for source, target in forward]
        low = lax.ppermute(
            lax.slice_in_dim(block, block.shape[dim] - width, None, axis=dim), axis, forward
        )
        high = lax.ppermute(lax.slice_in_dim(block, 0, width, axis=dim), axis, backward)
        block = jnp.concatenate([low, block, high], axis=dim)
    return block


def unfold(padded, frames, height, columns):
    pieces = [
        padded[
            frame_off : frame_off + frames, row_off : row_off + height, col_off : col_off + columns
        ]
        for frame_off in range(3)
        for row_off in range(3)
        for col_off in range(3)
    ]
    return jnp.concatenate(pieces, axis=-1).reshape(frames * height * columns, -1)


def normed_latents(token_rows, proj_weight):
    widened = token_rows.astype(jnp.float32)
    normed = (
        widened * lax.rsqrt(jnp.mean(widened * widened, axis=1, keepdims=True) + 1e-06)
    ).astype(jnp.bfloat16)
    return jnp.dot(normed, proj_weight, preferred_element_type=jnp.float32).astype(jnp.bfloat16)


def extend(tile_cells):
    bordered = padded_2(tile_cells, (("seq", 1),), 1)
    return jnp.pad(bordered, ((1, 1), (0, 0), (1, 1), (0, 0)))


def shuffle_tile(summed, frames, height, columns):
    channels = summed.shape[-1] // 4
    return (
        summed.reshape(frames, height, columns, channels, 2, 2)
        .transpose(0, 1, 4, 2, 5, 3)
        .reshape(frames, 2 * height, 2 * columns, channels)
    )


def shared_heads(
    query_rows, key_rows, value_rows, proj_weight, in_weight, in_bias, mid_weight, mid_bias
):
    devices = lax.axis_size("seq")
    halves = max(1, devices // HEADS)
    unit_count = HEADS * halves // devices
    local_tokens = query_rows.shape[0]
    shard_rows = local_tokens // W
    half_width = W // halves
    score_scale = 1.0 / math.sqrt(HD)

    def by_head(rows):
        shaped = rows.reshape(local_tokens, HEADS, HD).transpose(1, 0, 2)
        shaped = jnp.broadcast_to(shaped[:, None], (HEADS, halves, local_tokens, HD))
        return shaped.reshape(devices, unit_count, local_tokens, HD)

    shaped = query_rows.reshape(shard_rows, halves, half_width, HEADS, HD).transpose(3, 1, 0, 2, 4)
    query_units = lax.all_to_all(
        shaped.reshape(devices, unit_count, shard_rows, half_width, HD),
        "seq",
        split_axis=0,
        concat_axis=0,
        tiled=True,
    )
    key_units = lax.all_to_all(by_head(key_rows), "seq", split_axis=0, concat_axis=0, tiled=True)
    value_units = lax.all_to_all(
        by_head(value_rows), "seq", split_axis=0, concat_axis=0, tiled=True
    )
    key_heads = key_units.transpose(1, 0, 2, 3).reshape(unit_count, -1, HD)
    value_heads = value_units.transpose(1, 0, 2, 3).reshape(unit_count, -1, HD)
    query_total = devices * shard_rows * half_width
    block_rows = 512 if query_total % 512 == 0 else query_total
    query_heads = (
        query_units.transpose(1, 0, 2, 3, 4)
        .reshape(unit_count, query_total // block_rows, block_rows, HD)
        .transpose(1, 0, 2, 3)
    )

    def attend(query_block):
        scores = (
            jnp.einsum("uqd,ukd->uqk", query_block, key_heads, preferred_element_type=jnp.float32)
            * score_scale
        )
        largest = jnp.max(scores, axis=2, keepdims=True)
        weights = jnp.exp(scores - largest)
        totals = jnp.sum(weights, axis=2, keepdims=True)
        mixture = jnp.einsum(
            "uqk,ukd->uqd",
            weights.astype(jnp.bfloat16),
            value_heads,
            preferred_element_type=jnp.float32,
        )
        return (mixture / totals).astype(jnp.bfloat16)

    attended = lax.map(attend, query_heads)
    attended = attended.transpose(1, 0, 2, 3).reshape(
        unit_count, devices, shard_rows, half_width, HD
    )
    arranged = attended.reshape(unit_count, F, devices, HT, half_width, HD).transpose(
        2, 0, 1, 3, 4, 5
    )
    arrived = lax.all_to_all(arranged, "seq", split_axis=0, concat_axis=0, tiled=True)
    arrived = arrived.reshape(HEADS, halves, F, HT, half_width, HD).transpose(2, 3, 1, 4, 0, 5)
    latents = normed_latents(arrived.reshape(F * HT * W, D), proj_weight).reshape(F, HT, W, C_LAT)
    unfolded_in = unfold(extend(latents), F, HT, W)
    first = (
        jnp.dot(unfolded_in, in_weight.reshape(27 * C_LAT, CH), preferred_element_type=jnp.float32)
        + in_bias
    ).astype(jnp.bfloat16)
    active = jax.nn.silu(first.astype(jnp.float32)).astype(jnp.bfloat16)
    unfolded_mid = unfold(extend(active.reshape(F, HT, W, CH)), F, HT, W)
    piece = lax.all_gather(mid_weight, "seq", axis=4, tiled=True)
    column_span = piece.shape[4]
    middle = (
        jnp.dot(
            unfolded_mid, piece.reshape(27 * CH, column_span), preferred_element_type=jnp.float32
        )
        + mid_bias
    ).astype(jnp.bfloat16)
    summed = first.astype(jnp.float32) + middle.astype(jnp.float32)
    return shuffle_tile(summed, F, HT, W).astype(jnp.bfloat16)[None]


def dot_f32(left, right, left_dim=1, right_dim=0):
    return lax.dot_general(
        left, right, (((left_dim,), (right_dim,)), ((), ())), preferred_element_type=jnp.float32
    )


def pack_body(rank_ref, query_ref, key_ref, value_ref, *rest, steps, span):
    blocks, sems = rest[:-1], rest[-1]
    copies = []
    for place, step in enumerate(steps):
        start = pl.multiple_of((rank_ref[0] ^ step) * span, span)
        for which, ref in enumerate((query_ref, key_ref, value_ref)):
            copies.append(
                pltpu.make_async_copy(
                    ref.at[:, pl.ds(start, span)], blocks[place].at[which], sems.at[place, which]
                )
            )
    for copy in copies:
        copy.start()
    for copy in copies:
        copy.wait()


def slice_body(rank_ref, proj_ref, out_ref, sem):
    span = out_ref.shape[0]
    start = pl.multiple_of(rank_ref[0] * span, span)
    copy = pltpu.make_async_copy(proj_ref.at[pl.ds(start, span), :], out_ref, sem)
    copy.start()
    copy.wait()


def read_sums(ref, count):
    cells = ref.shape[0] - (2 if ref.dtype == jnp.bfloat16 else 1) * count
    parts = ref[:cells].astype(jnp.float32).reshape(count, cells // count, C_LAT)
    tail = ref[cells:].astype(jnp.float32)
    squares = tail[:count] + tail[count:] if ref.dtype == jnp.bfloat16 else tail
    return [parts[i] for i in range(count)], [squares[i : i + 1] for i in range(count)]


def write_sums(ref, parts, squares):
    cells = len(parts) * parts[0].shape[0]
    across = jnp.concatenate(squares, axis=0)
    if ref.dtype == jnp.bfloat16:
        coarse = across.astype(jnp.bfloat16).astype(jnp.float32)
        across = jnp.concatenate([coarse, across - coarse], axis=0)
    ref[:cells] = jnp.concatenate(parts, axis=0).astype(ref.dtype)
    ref[cells:] = across.astype(ref.dtype)


def attend_body(mid_weight_ref, proj_ref, *rest, order):
    blocks, (keep_ref, send_ref, mid_ref, mid_sem) = rest[:-4], rest[-4:]
    fetch = pltpu.make_async_copy(mid_weight_ref, mid_ref, mid_sem)
    fetch.start()
    devices = len(blocks)
    _, local, span = blocks[0].shape
    tokens = devices * local
    width = tokens
    sharpness = math.log2(math.e) / math.sqrt(HD)
    operands = [
        [
            jnp.concatenate([block[which, :, unit * HD : (unit + 1) * HD] for block in blocks], axis=0)
            for which in range(3)
        ]
        for unit in range(span // HD)
    ]
    items = [(unit, first) for unit in range(span // HD) for first in range(0, tokens, width)]

    def scored(item):
        query, key, _ = operands[item[0]]
        return dot_f32(key, query[item[1] : item[1] + width], 1, 1)

    pieces = []
    coming = scored(items[0])
    for place, (unit, first) in enumerate(items):
        scores = coming
        if place + 1 < len(items):
            coming = scored(items[place + 1])
        largest = jnp.max(scores, axis=0, keepdims=True)
        weights = jnp.exp2((scores - largest) * sharpness)
        totals = jnp.sum(weights, axis=0, keepdims=True)
        mixture = dot_f32(operands[unit][2], weights.astype(jnp.bfloat16), 0, 0)
        pieces.append((mixture * (1.0 / totals)).astype(jnp.bfloat16))
    count = tokens // width
    heads = [
        jnp.concatenate(pieces[unit * count : (unit + 1) * count], axis=1)
        for unit in range(span // HD)
    ]
    attended = jnp.concatenate(heads, axis=0)
    widened = attended.astype(jnp.float32)
    squares = jnp.sum(widened * widened, axis=0, keepdims=True)
    squares = jnp.concatenate([squares, jnp.zeros((1, C_LAT), jnp.float32)], axis=1)
    partial = dot_f32(attended, proj_ref[...], 0, 0).reshape(devices, local, C_LAT)
    for ref, first in ((keep_ref, 0), (send_ref, 1)):
        chosen = [order.index(step) for step in range(first, devices, 2)]
        write_sums(
            ref,
            [partial[i] for i in chosen],
            [squares[:, i * local : i * local + C_LAT] for i in chosen],
        )
    fetch.wait()


def fold_body(keep_ref, got_ref, next_ref, send_ref, count, split):
    parts, squares = read_sums(keep_ref, count)
    more_parts, more_squares = read_sums(got_ref, count)
    parts = [x + y for x, y in zip(parts, more_parts)]
    squares = [x + y for x, y in zip(squares, more_squares)]
    for ref, first in ((next_ref, 0), (send_ref, 1)):
        chosen = range(first, count, 2) if split else range(count)
        write_sums(ref, [parts[i] for i in chosen], [squares[i] for i in chosen])


def latents_body(keep_ref, *rest):
    gots, out_ref = rest[:-1], rest[-1]
    count = len(rest)
    local = out_ref.shape[0] // count
    parts, squares = read_sums(keep_ref, count)
    for step, got in enumerate(gots, 1):
        more_parts, more_squares = read_sums(got, count)
        parts = [parts[i] + more_parts[i ^ step] for i in range(count)]
        squares = [squares[i] + more_squares[i ^ step] for i in range(count)]
    lane = lax.broadcasted_iota(jnp.int32, (local, C_LAT), 1)
    row = lax.broadcasted_iota(jnp.int32, (local, C_LAT), 0)
    done = []
    for part, square in zip(parts, squares):
        column = jnp.sum(jnp.where(lane == row, square, 0.0), axis=1, keepdims=True)
        done.append(part * lax.rsqrt(column / D + 1e-06))
    out_ref[...] = jnp.concatenate(done, axis=0).astype(jnp.bfloat16)


def convolve_body(
    rank_ref, in_weight_ref, in_bias_ref, mid_weight_ref, mid_bias_ref, *rest
):
    quarters, (out_ref, latents_ref, cols) = rest[:-3], rest[-3:]
    frame = latents_ref.shape[0] // F
    count = out_ref.shape[0] // len(quarters)
    local = quarters[0].shape[0] // count
    for low, quarter in enumerate(quarters):
        for high in range(count):
            block = rank_ref[0] ^ (high * len(quarters) + low)
            latents_ref[pl.ds(pl.multiple_of(block * local, 16), local), :] = quarter[
                high * local : (high + 1) * local, :
            ]
    own = mid_weight_ref.shape[1] // 9
    column = lax.broadcasted_iota(jnp.int32, (frame, C_LAT), 0) % W
    for index in range(F):
        cells = latents_ref[index * frame : (index + 1) * frame, :].astype(jnp.float32)
        shifted = (
            jnp.where(column == 0, 0.0, pltpu.roll(cells, 1, 0)),
            cells,
            jnp.where(column == W - 1, 0.0, pltpu.roll(cells, frame - 1, 0)),
        )
        blank = jnp.zeros((W, C_LAT), jnp.float32)
        for col_off, moved in enumerate(shifted):
            above = jnp.concatenate([blank, moved[:-W]], axis=0)
            below = jnp.concatenate([moved[W:], blank], axis=0)
            for row_off, piece in enumerate((above, moved, below)):
                at = ((index * 3 + row_off) * 3 + col_off) * C_LAT
                cols[:, at : at + C_LAT] = piece.astype(jnp.bfloat16)
    deep = 9 * C_LAT
    firsts = []
    actives = []
    for index in range(F):
        low = (F - 1 - index) * deep
        first = (
            dot_f32(cols[...], in_weight_ref[low : low + F * deep, :]) + in_bias_ref[...]
        ).astype(jnp.bfloat16)
        wide = first.astype(jnp.float32)
        firsts.append(first)
        actives.append((wide * lax.logistic(wide)).astype(jnp.bfloat16))
    channel = lax.broadcasted_iota(jnp.int32, (own, CH), 1)
    mine = channel == lax.broadcasted_iota(jnp.int32, (own, CH), 0) + rank_ref[0] * own
    bias = jnp.sum(jnp.where(mine, mid_bias_ref[...], 0.0), axis=1, keepdims=True)
    chosen = jnp.where(mine, 1.0, 0.0).astype(jnp.bfloat16)
    spot = lax.broadcasted_iota(jnp.int32, (own, frame), 1)
    spot_column = spot % W
    outs = []
    for index in range(F):
        taps = sum(
            dot_f32(mid_weight_ref[source - index + 1], actives[source], 1, 1)
            for source in range(F)
        )
        total = None
        for col_off in range(3):
            merged = None
            for row_off in range(3):
                at = (row_off * 3 + col_off) * own
                piece = taps[at : at + own, :]
                if row_off == 0:
                    piece = jnp.where(spot < W, 0.0, pltpu.roll(piece, W, 1))
                elif row_off == 2:
                    piece = jnp.where(spot >= frame - W, 0.0, pltpu.roll(piece, frame - W, 1))
                merged = piece if merged is None else merged + piece
            if col_off == 0:
                merged = jnp.where(spot_column == 0, 0.0, pltpu.roll(merged, 1, 1))
            elif col_off == 2:
                merged = jnp.where(spot_column == W - 1, 0.0, pltpu.roll(merged, frame - 1, 1))
            total = merged if total is None else total + merged
        middle = (total + bias).astype(jnp.bfloat16).astype(jnp.float32)
        outs.append((dot_f32(chosen, firsts[index], 1, 1) + middle).astype(jnp.bfloat16))
    stacked = jnp.concatenate(outs, axis=0)
    source = lax.broadcasted_iota(jnp.int32, (F * own, 128), 0)
    target = lax.broadcasted_iota(jnp.int32, (F * own, 128), 1)
    inner = source % own
    place = (source // own) * own + (inner % 4) * (own // 4) + inner // 4
    moves = jnp.where(place == target % 64, 1.0, 0.0).astype(jnp.bfloat16)
    moved = dot_f32(stacked, moves, 0, 0).reshape(frame // W, W, 128)
    tail = jnp.concatenate([moved[:, 16:], jnp.zeros((frame // W, 32 - W, 128), jnp.float32)], axis=1)
    lane = lax.broadcasted_iota(jnp.int32, (frame // W, 16, 128), 2)
    out_ref[...] = jnp.where(lane < 64, moved[:, :16], tail).astype(jnp.bfloat16)


def shuffle_body(rows_ref, out_ref, wide):
    devices = rows_ref.shape[0]
    share = C_LAT // devices
    rows = rows_ref[...].astype(jnp.float32)
    lane = lax.broadcasted_iota(jnp.int32, (W, 128), 1) // share
    for index in range(F):
        for part in range(4):
            origin = (index * 4 + part) * share
            total = None
            for source in range(devices):
                shift = source * share - origin
                moved = jnp.concatenate(
                    [
                        pltpu.roll(rows[source], shift % 128, 1),
                        pltpu.roll(rows[source, : W - 16], (shift + 64) % 128, 1),
                    ],
                    axis=0,
                )
                total = moved if total is None else jnp.where(lane == source, moved, total)
            wide[index, part // 2, pl.ds(part % 2, W, stride=2), :] = total
    out_ref[0] = wide[...].astype(jnp.bfloat16)


def near(array):
    return pltpu.with_memory_space_constraint(array, pltpu.VMEM)


def far(array):
    return pltpu.with_memory_space_constraint(array, pltpu.HBM)


SCALAR = pl.BlockSpec(memory_space=pltpu.SMEM)
LOCAL = pl.BlockSpec(memory_space=pltpu.VMEM)
REMOTE = pl.BlockSpec(memory_space=pltpu.HBM)


def launch(body, outs, in_specs, operands, scratch=(), mib=8):
    return pl.pallas_call(
        body,
        out_shape=outs,
        in_specs=in_specs,
        out_specs=jax.tree.map(lambda _: LOCAL, outs),
        scratch_shapes=scratch,
        compiler_params=pltpu.CompilerParams(vmem_limit_bytes=mib << 20),
    )(*operands)


def exchange_order(devices):
    half = devices // 2
    order = [0, half]
    for step in range(1, half):
        order += [step, half + step]
    return order


def swap(array, step):
    devices = lax.axis_size("seq")
    return near(lax.ppermute(array, "seq", [(i, i ^ step) for i in range(devices)]))


def sums_shape(count, local, dtype):
    tail = 2 * count if dtype == jnp.bfloat16 else count
    return pltpu.VMEM((count * local + tail, C_LAT), dtype)


def whole_heads(
    query_rows, key_rows, value_rows, proj_weight, in_weight, in_bias, mid_weight, mid_bias
):
    devices = lax.axis_size("seq")
    local = query_rows.shape[0]
    span = D // devices
    frame = devices * local // F
    own = mid_weight.shape[4]
    rank = lax.axis_index("seq").reshape(1).astype(jnp.int32)
    order = exchange_order(devices)
    blocks = launch(
        functools.partial(pack_body, steps=order, span=span),
        [pltpu.VMEM((3, local, span), jnp.bfloat16)] * devices,
        [SCALAR] + [REMOTE] * 3,
        (rank, far(query_rows), far(key_rows), far(value_rows)),
        [pltpu.SemaphoreType.DMA((devices, 3))],
    )
    landed = [swap(block, step) if step else near(block) for block, step in zip(blocks, order)]
    proj_rows = launch(
        slice_body,
        pltpu.VMEM((span, C_LAT), jnp.bfloat16),
        [SCALAR, REMOTE],
        (rank, far(proj_weight)),
        [pltpu.SemaphoreType.DMA(())],
    )
    half = devices // 2
    quarter = devices // 4
    keep, send, mid_near = launch(
        functools.partial(attend_body, order=order),
        [
            sums_shape(half, local, jnp.float32),
            sums_shape(half, local, jnp.bfloat16),
            pltpu.VMEM((3, 9 * own, CH), jnp.bfloat16),
        ],
        [REMOTE] + [LOCAL] * (1 + devices),
        (
            far(mid_weight.transpose(0, 1, 2, 4, 3).reshape(3, 9 * own, CH)),
            near(proj_rows),
            *landed,
        ),
        [pltpu.SemaphoreType.DMA(())],
        32,
    )
    keep, send = launch(
        functools.partial(fold_body, count=half, split=True),
        [sums_shape(quarter, local, jnp.float32), sums_shape(quarter, local, jnp.bfloat16)],
        [LOCAL] * 2,
        (near(keep), swap(send, 1)),
    )
    keep, send = launch(
        functools.partial(fold_body, count=quarter, split=False),
        [sums_shape(quarter, local, jnp.float32), sums_shape(quarter, local, jnp.bfloat16)],
        [LOCAL] * 2,
        (near(keep), swap(send, 2)),
    )
    gots = []
    for step in range(1, quarter):
        gots.append(swap(send, 4 * step))
    ready = launch(
        latents_body,
        pltpu.VMEM((quarter * local, C_LAT), jnp.bfloat16),
        [LOCAL] * (1 + len(gots)),
        (near(keep), *gots),
    )
    paired = swap(ready, 2)
    columns = launch(
        convolve_body,
        pltpu.VMEM((devices, 16, 128), jnp.bfloat16),
        [SCALAR] + [LOCAL] * 8,
        (
            rank,
            near(in_weight.reshape(27 * C_LAT, CH)),
            near(in_bias.reshape(1, CH)),
            near(mid_near),
            near(mid_bias.reshape(1, CH)),
            near(ready),
            swap(ready, 1),
            paired,
            swap(paired, 1),
        ),
        [
            pltpu.VMEM((devices * local, C_LAT), jnp.bfloat16),
            pltpu.VMEM((frame, F * 9 * C_LAT), jnp.bfloat16),
        ],
        32,
    )
    arrived = lax.all_to_all(columns, "seq", split_axis=0, concat_axis=0, tiled=True)
    return pl.pallas_call(
        shuffle_body,
        out_shape=jax.ShapeDtypeStruct((1, F, 2, 2 * W, C_LAT), jnp.bfloat16),
        in_specs=[LOCAL],
        out_specs=LOCAL,
        scratch_shapes=[pltpu.VMEM((F, 2, 2 * W, C_LAT), jnp.float32)],
        compiler_params=pltpu.CompilerParams(vmem_limit_bytes=8 << 20),
        name="shuffle",
    )(near(arrived))


def local_heads(devices):
    return 16 <= devices <= HEADS and devices & (devices - 1) == 0


def on_device(*operands):
    if not local_heads(lax.axis_size("seq")):
        return shared_heads(*operands)
    return whole_heads(*operands)


def solution(mesh):
    return jax.shard_map(
        on_device,
        mesh=mesh,
        in_specs=(
            P(("groups", "seq"), None),
            P(("groups", "seq"), None),
            P(("groups", "seq"), None),
            P(),
            P(),
            P(),
            P(None, None, None, None, "seq"),
            P(),
        ),
        out_specs=P(("groups", "seq"), None, None, None, None),
        check_vma=False,
    )
```

```python
import functools
import math

import jax
import jax.numpy as jnp
from jax import lax
from jax.experimental import pallas as pl
from jax.experimental.pallas import tpu as pltpu
from jax.sharding import PartitionSpec as P


D = 4096
HEADS = 32
HD = 128
C_LAT = 128
CH = 512
W = 24
F = 2
HT = 1


def padded_2(block, sides, width):
    for axis, dim in sides:
        count = lax.axis_size(axis)
        forward = [(i, i + 1) for i in range(count - 1)]
        backward = [(target, source) for source, target in forward]
        low = lax.ppermute(
            lax.slice_in_dim(block, block.shape[dim] - width, None, axis=dim), axis, forward
        )
        high = lax.ppermute(lax.slice_in_dim(block, 0, width, axis=dim), axis, backward)
        block = jnp.concatenate([low, block, high], axis=dim)
    return block


def unfold(padded, frames, height, columns):
    pieces = [
        padded[
            frame_off : frame_off + frames, row_off : row_off + height, col_off : col_off + columns
        ]
        for frame_off in range(3)
        for row_off in range(3)
        for col_off in range(3)
    ]
    return jnp.concatenate(pieces, axis=-1).reshape(frames * height * columns, -1)


def normed_latents(token_rows, proj_weight):
    widened = token_rows.astype(jnp.float32)
    normed = (
        widened * lax.rsqrt(jnp.mean(widened * widened, axis=1, keepdims=True) + 1e-06)
    ).astype(jnp.bfloat16)
    return jnp.dot(normed, proj_weight, preferred_element_type=jnp.float32).astype(jnp.bfloat16)


def extend(tile_cells):
    bordered = padded_2(tile_cells, (("seq", 1),), 1)
    return jnp.pad(bordered, ((1, 1), (0, 0), (1, 1), (0, 0)))


def shuffle_tile(summed, frames, height, columns):
    channels = summed.shape[-1] // 4
    return (
        summed.reshape(frames, height, columns, channels, 2, 2)
        .transpose(0, 1, 4, 2, 5, 3)
        .reshape(frames, 2 * height, 2 * columns, channels)
    )


def shared_heads(
    query_rows, key_rows, value_rows, proj_weight, in_weight, in_bias, mid_weight, mid_bias
):
    devices = lax.axis_size("seq")
    halves = max(1, devices // HEADS)
    unit_count = HEADS * halves // devices
    local_tokens = query_rows.shape[0]
    shard_rows = local_tokens // W
    half_width = W // halves
    score_scale = 1.0 / math.sqrt(HD)

    def by_head(rows):
        shaped = rows.reshape(local_tokens, HEADS, HD).transpose(1, 0, 2)
        shaped = jnp.broadcast_to(shaped[:, None], (HEADS, halves, local_tokens, HD))
        return shaped.reshape(devices, unit_count, local_tokens, HD)

    shaped = query_rows.reshape(shard_rows, halves, half_width, HEADS, HD).transpose(3, 1, 0, 2, 4)
    query_units = lax.all_to_all(
        shaped.reshape(devices, unit_count, shard_rows, half_width, HD),
        "seq",
        split_axis=0,
        concat_axis=0,
        tiled=True,
    )
    key_units = lax.all_to_all(by_head(key_rows), "seq", split_axis=0, concat_axis=0, tiled=True)
    value_units = lax.all_to_all(
        by_head(value_rows), "seq", split_axis=0, concat_axis=0, tiled=True
    )
    key_heads = key_units.transpose(1, 0, 2, 3).reshape(unit_count, -1, HD)
    value_heads = value_units.transpose(1, 0, 2, 3).reshape(unit_count, -1, HD)
    query_total = devices * shard_rows * half_width
    block_rows = 512 if query_total % 512 == 0 else query_total
    query_heads = (
        query_units.transpose(1, 0, 2, 3, 4)
        .reshape(unit_count, query_total // block_rows, block_rows, HD)
        .transpose(1, 0, 2, 3)
    )

    def attend(query_block):
        scores = (
            jnp.einsum("uqd,ukd->uqk", query_block, key_heads, preferred_element_type=jnp.float32)
            * score_scale
        )
        largest = jnp.max(scores, axis=2, keepdims=True)
        weights = jnp.exp(scores - largest)
        totals = jnp.sum(weights, axis=2, keepdims=True)
        mixture = jnp.einsum(
            "uqk,ukd->uqd",
            weights.astype(jnp.bfloat16),
            value_heads,
            preferred_element_type=jnp.float32,
        )
        return (mixture / totals).astype(jnp.bfloat16)

    attended = lax.map(attend, query_heads)
    attended = attended.transpose(1, 0, 2, 3).reshape(
        unit_count, devices, shard_rows, half_width, HD
    )
    arranged = attended.reshape(unit_count, F, devices, HT, half_width, HD).transpose(
        2, 0, 1, 3, 4, 5
    )
    arrived = lax.all_to_all(arranged, "seq", split_axis=0, concat_axis=0, tiled=True)
    arrived = arrived.reshape(HEADS, halves, F, HT, half_width, HD).transpose(2, 3, 1, 4, 0, 5)
    latents = normed_latents(arrived.reshape(F * HT * W, D), proj_weight).reshape(F, HT, W, C_LAT)
    unfolded_in = unfold(extend(latents), F, HT, W)
    first = (
        jnp.dot(unfolded_in, in_weight.reshape(27 * C_LAT, CH), preferred_element_type=jnp.float32)
        + in_bias
    ).astype(jnp.bfloat16)
    active = jax.nn.silu(first.astype(jnp.float32)).astype(jnp.bfloat16)
    unfolded_mid = unfold(extend(active.reshape(F, HT, W, CH)), F, HT, W)
    piece = lax.all_gather(mid_weight, "seq", axis=4, tiled=True)
    column_span = piece.shape[4]
    middle = (
        jnp.dot(
            unfolded_mid, piece.reshape(27 * CH, column_span), preferred_element_type=jnp.float32
        )
        + mid_bias
    ).astype(jnp.bfloat16)
    summed = first.astype(jnp.float32) + middle.astype(jnp.float32)
    return shuffle_tile(summed, F, HT, W).astype(jnp.bfloat16)[None]


def dot_f32(left, right, left_dim=1, right_dim=0):
    return lax.dot_general(
        left, right, (((left_dim,), (right_dim,)), ((), ())), preferred_element_type=jnp.float32
    )


def pack_body(query_ref, key_ref, value_ref, *rest, steps, span):
    blocks, sems = rest[:-1], rest[-1]
    rank = lax.axis_index("seq")
    copies = []
    for place, step in enumerate(steps):
        start = pl.multiple_of((rank ^ step) * span, span)
        for which, ref in enumerate((query_ref, key_ref, value_ref)):
            copies.append(
                pltpu.make_async_copy(
                    ref.at[:, pl.ds(start, span)], blocks[place].at[which], sems.at[place, which]
                )
            )
    for copy in copies:
        copy.start()
    for copy in copies:
        copy.wait()


def slice_body(proj_ref, out_ref, sem):
    span = out_ref.shape[0]
    start = pl.multiple_of(lax.axis_index("seq") * span, span)
    copy = pltpu.make_async_copy(proj_ref.at[pl.ds(start, span), :], out_ref, sem)
    copy.start()
    copy.wait()


def read_sums(ref, count):
    cells = ref.shape[0] - (2 if ref.dtype == jnp.bfloat16 else 1) * count
    parts = ref[:cells].astype(jnp.float32).reshape(count, cells // count, C_LAT)
    tail = ref[cells:].astype(jnp.float32)
    squares = tail[:count] + tail[count:] if ref.dtype == jnp.bfloat16 else tail
    return [parts[i] for i in range(count)], [squares[i : i + 1] for i in range(count)]


def write_sums(ref, parts, squares):
    cells = len(parts) * parts[0].shape[0]
    across = jnp.concatenate(squares, axis=0)
    if ref.dtype == jnp.bfloat16:
        coarse = across.astype(jnp.bfloat16).astype(jnp.float32)
        across = jnp.concatenate([coarse, across - coarse], axis=0)
    ref[:cells] = jnp.concatenate(parts, axis=0).astype(ref.dtype)
    ref[cells:] = across.astype(ref.dtype)


def attend_body(mid_weight_ref, proj_ref, *rest, order):
    blocks, (keep_ref, send_ref, mid_ref, mid_sem) = rest[:-4], rest[-4:]
    fetch = pltpu.make_async_copy(mid_weight_ref, mid_ref, mid_sem)
    fetch.start()
    devices = len(blocks)
    _, local, span = blocks[0].shape
    tokens = devices * local
    query, key, value = (
        jnp.concatenate([block[which] for block in blocks], axis=0) for which in range(3)
    )
    sharpness = math.log2(math.e) / math.sqrt(HD)
    units = [slice(first, first + HD) for first in range(0, span, HD)]
    scores = [dot_f32(query[:, lanes], key[:, lanes], 1, 1) for lanes in units]
    heads = []
    for lanes, score in zip(units, scores):
        weights = jnp.exp2((score - jnp.max(score, axis=1, keepdims=True)) * sharpness)
        totals = jnp.sum(weights, axis=1, keepdims=True)
        mixture = dot_f32(weights.astype(jnp.bfloat16), value[:, lanes])
        heads.append((mixture / totals).astype(jnp.bfloat16))
    attended = jnp.concatenate(heads, axis=1)
    widened = attended.astype(jnp.float32)
    squares = jnp.sum(widened * widened, axis=1, keepdims=True)
    partial = dot_f32(attended, proj_ref[...]).reshape(devices, local, C_LAT)
    lane = lax.broadcasted_iota(jnp.int32, (devices, local, C_LAT), 2)
    row = lax.broadcasted_iota(jnp.int32, (devices, local, C_LAT), 1)
    spread = jnp.broadcast_to(squares, (tokens, C_LAT)).reshape(devices, local, C_LAT)
    across = jnp.sum(jnp.where(lane == row, spread, 0.0), axis=1)
    for ref, first in ((keep_ref, 0), (send_ref, 1)):
        chosen = [order.index(step) for step in range(first, devices, 2)]
        write_sums(ref, [partial[i] for i in chosen], [across[i : i + 1] for i in chosen])
    fetch.wait()


def fold_body(keep_ref, got_ref, next_ref, send_ref, count, split):
    parts, squares = read_sums(keep_ref, count)
    more_parts, more_squares = read_sums(got_ref, count)
    parts = [x + y for x, y in zip(parts, more_parts)]
    squares = [x + y for x, y in zip(squares, more_squares)]
    for ref, first in ((next_ref, 0), (send_ref, 1)):
        chosen = range(first, count, 2) if split else range(count)
        write_sums(ref, [parts[i] for i in chosen], [squares[i] for i in chosen])


def latents_body(keep_ref, *rest):
    gots, out_ref = rest[:-1], rest[-1]
    count = len(rest)
    local = out_ref.shape[0] // count
    parts, squares = read_sums(keep_ref, count)
    for step, got in enumerate(gots, 1):
        more_parts, more_squares = read_sums(got, count)
        parts = [parts[i] + more_parts[i ^ step] for i in range(count)]
        squares = [squares[i] + more_squares[i ^ step] for i in range(count)]
    lane = lax.broadcasted_iota(jnp.int32, (local, C_LAT), 1)
    row = lax.broadcasted_iota(jnp.int32, (local, C_LAT), 0)
    done = []
    for part, square in zip(parts, squares):
        column = jnp.sum(jnp.where(lane == row, square, 0.0), axis=1, keepdims=True)
        done.append(part * lax.rsqrt(column / D + 1e-06))
    out_ref[...] = jnp.concatenate(done, axis=0).astype(jnp.bfloat16)


def convolve_body(
    in_weight_ref, in_bias_ref, mid_weight_ref, mid_bias_ref, *rest
):
    quarters, (out_ref, latents_ref, cols) = rest[:-3], rest[-3:]
    rank = lax.axis_index("seq")
    frame = latents_ref.shape[0] // F
    count = out_ref.shape[0] // len(quarters)
    local = quarters[0].shape[0] // count
    for low, quarter in enumerate(quarters):
        for high in range(count):
            block = rank ^ (high * len(quarters) + low)
            latents_ref[pl.ds(pl.multiple_of(block * local, 16), local), :] = quarter[
                high * local : (high + 1) * local, :
            ]
    own = mid_weight_ref.shape[0] // 27
    column = lax.broadcasted_iota(jnp.int32, (frame, C_LAT), 0) % W
    for index in range(F):
        cells = latents_ref[index * frame : (index + 1) * frame, :].astype(jnp.float32)
        shifted = (
            jnp.where(column == 0, 0.0, pltpu.roll(cells, 1, 0)),
            cells,
            jnp.where(column == W - 1, 0.0, pltpu.roll(cells, frame - 1, 0)),
        )
        blank = jnp.zeros((W, C_LAT), jnp.float32)
        for col_off, moved in enumerate(shifted):
            above = jnp.concatenate([blank, moved[:-W]], axis=0)
            below = jnp.concatenate([moved[W:], blank], axis=0)
            for row_off, piece in enumerate((above, moved, below)):
                at = (row_off * 3 + col_off) * C_LAT
                cols[index * frame : (index + 1) * frame, at : at + C_LAT] = piece.astype(
                    jnp.bfloat16
                )
    deep = 9 * C_LAT
    sums = [None] * F
    for tap in range(3):
        low, high = max(0, tap - 1), min(F, F + tap - 1)
        product = dot_f32(
            cols[low * frame : high * frame, :], in_weight_ref[tap * deep : (tap + 1) * deep, :]
        )
        for index in range(low, high):
            piece = product[(index - low) * frame : (index - low + 1) * frame]
            target = index - tap + 1
            sums[target] = piece if sums[target] is None else sums[target] + piece
    firsts = [(total + in_bias_ref[...]).astype(jnp.bfloat16) for total in sums]
    taps = [None] * F
    for index in range(F):
        wide = firsts[index].astype(jnp.float32)
        active = (wide * lax.logistic(wide)).astype(jnp.bfloat16)
        low, high = max(0, index + 2 - F), min(3, index + 2)
        product = dot_f32(mid_weight_ref[low * 9 * own : high * 9 * own, :], active, 1, 1)
        for tap in range(low, high):
            piece = product[(tap - low) * 9 * own : (tap - low + 1) * 9 * own]
            target = index - tap + 1
            taps[target] = piece if taps[target] is None else taps[target] + piece
    channel = lax.broadcasted_iota(jnp.int32, (own, CH), 1)
    mine = channel == lax.broadcasted_iota(jnp.int32, (own, CH), 0) + rank * own
    bias = jnp.sum(jnp.where(mine, mid_bias_ref[...], 0.0), axis=1, keepdims=True)
    chosen = jnp.where(mine, 1.0, 0.0).astype(jnp.bfloat16)
    spot = lax.broadcasted_iota(jnp.int32, (own, frame), 1)
    spot_column = spot % W
    outs = []
    for index in range(F):
        total = None
        for col_off in range(3):
            merged = None
            for row_off in range(3):
                at = (row_off * 3 + col_off) * own
                piece = taps[index][at : at + own, :]
                if row_off == 0:
                    piece = jnp.where(spot < W, 0.0, pltpu.roll(piece, W, 1))
                elif row_off == 2:
                    piece = jnp.where(spot >= frame - W, 0.0, pltpu.roll(piece, frame - W, 1))
                merged = piece if merged is None else merged + piece
            if col_off == 0:
                merged = jnp.where(spot_column == 0, 0.0, pltpu.roll(merged, 1, 1))
            elif col_off == 2:
                merged = jnp.where(spot_column == W - 1, 0.0, pltpu.roll(merged, frame - 1, 1))
            total = merged if total is None else total + merged
        middle = (total + bias).astype(jnp.bfloat16).astype(jnp.float32)
        outs.append((dot_f32(chosen, firsts[index], 1, 1) + middle).astype(jnp.bfloat16))
    stacked = jnp.concatenate(outs, axis=0)
    source = lax.broadcasted_iota(jnp.int32, (F * own, 128), 0)
    target = lax.broadcasted_iota(jnp.int32, (F * own, 128), 1)
    inner = source % own
    place = (source // own) * own + (inner % 4) * (own // 4) + inner // 4
    moves = jnp.where(place == target % 64, 1.0, 0.0).astype(jnp.bfloat16)
    moved = dot_f32(stacked, moves, 0, 0).reshape(frame // W, W, 128)
    tail = jnp.concatenate([moved[:, 16:], jnp.zeros((frame // W, 32 - W, 128), jnp.float32)], axis=1)
    lane = lax.broadcasted_iota(jnp.int32, (frame // W, 16, 128), 2)
    out_ref[...] = jnp.where(lane < 64, moved[:, :16], tail).astype(jnp.bfloat16)


def shuffle_body(rows_ref, out_ref, wide):
    devices = rows_ref.shape[0]
    share = C_LAT // devices
    rows = rows_ref[...].astype(jnp.float32)
    lane = lax.broadcasted_iota(jnp.int32, (W, 128), 1) // share
    for index in range(F):
        for part in range(4):
            origin = (index * 4 + part) * share
            total = None
            for source in range(devices):
                shift = source * share - origin
                moved = jnp.concatenate(
                    [
                        pltpu.roll(rows[source], shift % 128, 1),
                        pltpu.roll(rows[source, : W - 16], (shift + 64) % 128, 1),
                    ],
                    axis=0,
                )
                total = moved if total is None else jnp.where(lane == source, moved, total)
            wide[index, part // 2, pl.ds(part % 2, W, stride=2), :] = total
    out_ref[0] = wide[...].astype(jnp.bfloat16)


def near(array):
    return pltpu.with_memory_space_constraint(array, pltpu.VMEM)


def far(array):
    return pltpu.with_memory_space_constraint(array, pltpu.HBM)


LOCAL = pl.BlockSpec(memory_space=pltpu.VMEM)
REMOTE = pl.BlockSpec(memory_space=pltpu.HBM)


def launch(body, outs, in_specs, operands, scratch=(), mib=8):
    return pl.pallas_call(
        body,
        out_shape=outs,
        in_specs=in_specs,
        out_specs=jax.tree.map(lambda _: LOCAL, outs),
        scratch_shapes=scratch,
        compiler_params=pltpu.CompilerParams(vmem_limit_bytes=mib << 20),
    )(*operands)


def exchange_order(devices):
    half = devices // 2
    order = [0, half]
    for step in range(1, half):
        order += [step, half + step]
    return order


def swap(array, step):
    devices = lax.axis_size("seq")
    return near(lax.ppermute(array, "seq", [(i, i ^ step) for i in range(devices)]))


def sums_shape(count, local, dtype):
    tail = 2 * count if dtype == jnp.bfloat16 else count
    return pltpu.VMEM((count * local + tail, C_LAT), dtype)


def whole_heads(
    query_rows, key_rows, value_rows, proj_weight, in_weight, in_bias, mid_weight, mid_bias
):
    devices = lax.axis_size("seq")
    local = query_rows.shape[0]
    span = D // devices
    frame = devices * local // F
    own = mid_weight.shape[4]
    order = exchange_order(devices)
    order = order[1:] + [0]
    landed = []
    for steps in (order[:2], order[2:]):
        blocks = launch(
            functools.partial(pack_body, steps=steps, span=span),
            [pltpu.VMEM((3, local, span), jnp.bfloat16)] * len(steps),
            [REMOTE] * 3,
            (far(query_rows), far(key_rows), far(value_rows)),
            [pltpu.SemaphoreType.DMA((len(steps), 3))],
        )
        landed += [swap(block, step) if step else near(block) for block, step in zip(blocks, steps)]
    proj_rows = launch(
        slice_body,
        pltpu.VMEM((span, C_LAT), jnp.bfloat16),
        [REMOTE],
        (far(proj_weight),),
        [pltpu.SemaphoreType.DMA(())],
    )
    half = devices // 2
    quarter = devices // 4
    keep, send, mid_near = launch(
        functools.partial(attend_body, order=order),
        [
            sums_shape(half, local, jnp.float32),
            sums_shape(half, local, jnp.bfloat16),
            pltpu.VMEM((27 * own, CH), jnp.bfloat16),
        ],
        [REMOTE] + [LOCAL] * (1 + devices),
        (
            far(mid_weight.transpose(0, 1, 2, 4, 3).reshape(27 * own, CH)),
            near(proj_rows),
            *landed,
        ),
        [pltpu.SemaphoreType.DMA(())],
        32,
    )
    keep, send = launch(
        functools.partial(fold_body, count=half, split=True),
        [sums_shape(quarter, local, jnp.float32), sums_shape(quarter, local, jnp.bfloat16)],
        [LOCAL] * 2,
        (near(keep), swap(send, 1)),
    )
    keep, send = launch(
        functools.partial(fold_body, count=quarter, split=False),
        [sums_shape(quarter, local, jnp.float32), sums_shape(quarter, local, jnp.bfloat16)],
        [LOCAL] * 2,
        (near(keep), swap(send, 2)),
    )
    gots = []
    for step in range(1, quarter):
        gots.append(swap(send, 4 * step))
    ready = launch(
        latents_body,
        pltpu.VMEM((quarter * local, C_LAT), jnp.bfloat16),
        [LOCAL] * (1 + len(gots)),
        (near(keep), *gots),
    )
    paired = swap(ready, 2)
    columns = launch(
        convolve_body,
        pltpu.VMEM((devices, 16, 128), jnp.bfloat16),
        [LOCAL] * 8,
        (
            near(in_weight.reshape(27 * C_LAT, CH)),
            near(in_bias.reshape(1, CH)),
            near(mid_near),
            near(mid_bias.reshape(1, CH)),
            near(ready),
            swap(ready, 1),
            paired,
            swap(paired, 1),
        ),
        [
            pltpu.VMEM((devices * local, C_LAT), jnp.bfloat16),
            pltpu.VMEM((F * frame, 9 * C_LAT), jnp.bfloat16),
        ],
        32,
    )
    arrived = lax.all_to_all(columns, "seq", split_axis=0, concat_axis=0, tiled=True)
    return pl.pallas_call(
        shuffle_body,
        out_shape=jax.ShapeDtypeStruct((1, F, 2, 2 * W, C_LAT), jnp.bfloat16),
        in_specs=[LOCAL],
        out_specs=LOCAL,
        scratch_shapes=[pltpu.VMEM((F, 2, 2 * W, C_LAT), jnp.float32)],
        compiler_params=pltpu.CompilerParams(vmem_limit_bytes=8 << 20),
        name="shuffle",
    )(near(arrived))


def local_heads(devices):
    return 16 <= devices <= HEADS and devices & (devices - 1) == 0


def on_device(*operands):
    if not local_heads(lax.axis_size("seq")):
        return shared_heads(*operands)
    return whole_heads(*operands)


def solution(mesh):
    whole = jax.shard_map(
        on_device,
        mesh=mesh,
        in_specs=(
            P(("groups", "seq"), None),
            P(("groups", "seq"), None),
            P(("groups", "seq"), None),
            P(),
            P(),
            P(),
            P(None, None, None, None, "seq"),
            P(),
        ),
        out_specs=P(("groups", "seq"), None, None, None, None),
        check_vma=False,
    )
    devices = mesh.shape["seq"]
    if not local_heads(devices):
        return whole
    return whole
```

```python
import functools
import math

import jax
import jax.numpy as jnp
from jax import lax
from jax.experimental import pallas as pl
from jax.experimental.pallas import tpu as pltpu
from jax.sharding import PartitionSpec as P


D = 4096
HEADS = 32
HD = 128
C_LAT = 128
CH = 512
W = 24
F = 2
HT = 1


def padded_2(block, sides, width):
    for axis, dim in sides:
        count = lax.axis_size(axis)
        forward = [(i, i + 1) for i in range(count - 1)]
        backward = [(target, source) for source, target in forward]
        low = lax.ppermute(
            lax.slice_in_dim(block, block.shape[dim] - width, None, axis=dim), axis, forward
        )
        high = lax.ppermute(lax.slice_in_dim(block, 0, width, axis=dim), axis, backward)
        block = jnp.concatenate([low, block, high], axis=dim)
    return block


def unfold(padded, frames, height, columns):
    pieces = [
        padded[
            frame_off : frame_off + frames, row_off : row_off + height, col_off : col_off + columns
        ]
        for frame_off in range(3)
        for row_off in range(3)
        for col_off in range(3)
    ]
    return jnp.concatenate(pieces, axis=-1).reshape(frames * height * columns, -1)


def normed_latents(token_rows, proj_weight):
    widened = token_rows.astype(jnp.float32)
    normed = (
        widened * lax.rsqrt(jnp.mean(widened * widened, axis=1, keepdims=True) + 1e-06)
    ).astype(jnp.bfloat16)
    return jnp.dot(normed, proj_weight, preferred_element_type=jnp.float32).astype(jnp.bfloat16)


def extend(tile_cells):
    bordered = padded_2(tile_cells, (("seq", 1),), 1)
    return jnp.pad(bordered, ((1, 1), (0, 0), (1, 1), (0, 0)))


def shuffle_tile(summed, frames, height, columns):
    channels = summed.shape[-1] // 4
    return (
        summed.reshape(frames, height, columns, channels, 2, 2)
        .transpose(0, 1, 4, 2, 5, 3)
        .reshape(frames, 2 * height, 2 * columns, channels)
    )


def shared_heads(
    query_rows, key_rows, value_rows, proj_weight, in_weight, in_bias, mid_weight, mid_bias
):
    devices = lax.axis_size("seq")
    halves = max(1, devices // HEADS)
    unit_count = HEADS * halves // devices
    local_tokens = query_rows.shape[0]
    shard_rows = local_tokens // W
    half_width = W // halves
    score_scale = 1.0 / math.sqrt(HD)

    def by_head(rows):
        shaped = rows.reshape(local_tokens, HEADS, HD).transpose(1, 0, 2)
        shaped = jnp.broadcast_to(shaped[:, None], (HEADS, halves, local_tokens, HD))
        return shaped.reshape(devices, unit_count, local_tokens, HD)

    shaped = query_rows.reshape(shard_rows, halves, half_width, HEADS, HD).transpose(3, 1, 0, 2, 4)
    query_units = lax.all_to_all(
        shaped.reshape(devices, unit_count, shard_rows, half_width, HD),
        "seq",
        split_axis=0,
        concat_axis=0,
        tiled=True,
    )
    key_units = lax.all_to_all(by_head(key_rows), "seq", split_axis=0, concat_axis=0, tiled=True)
    value_units = lax.all_to_all(
        by_head(value_rows), "seq", split_axis=0, concat_axis=0, tiled=True
    )
    key_heads = key_units.transpose(1, 0, 2, 3).reshape(unit_count, -1, HD)
    value_heads = value_units.transpose(1, 0, 2, 3).reshape(unit_count, -1, HD)
    query_total = devices * shard_rows * half_width
    block_rows = 512 if query_total % 512 == 0 else query_total
    query_heads = (
        query_units.transpose(1, 0, 2, 3, 4)
        .reshape(unit_count, query_total // block_rows, block_rows, HD)
        .transpose(1, 0, 2, 3)
    )

    def attend(query_block):
        scores = (
            jnp.einsum("uqd,ukd->uqk", query_block, key_heads, preferred_element_type=jnp.float32)
            * score_scale
        )
        largest = jnp.max(scores, axis=2, keepdims=True)
        weights = jnp.exp(scores - largest)
        totals = jnp.sum(weights, axis=2, keepdims=True)
        mixture = jnp.einsum(
            "uqk,ukd->uqd",
            weights.astype(jnp.bfloat16),
            value_heads,
            preferred_element_type=jnp.float32,
        )
        return (mixture / totals).astype(jnp.bfloat16)

    attended = lax.map(attend, query_heads)
    attended = attended.transpose(1, 0, 2, 3).reshape(
        unit_count, devices, shard_rows, half_width, HD
    )
    arranged = attended.reshape(unit_count, F, devices, HT, half_width, HD).transpose(
        2, 0, 1, 3, 4, 5
    )
    arrived = lax.all_to_all(arranged, "seq", split_axis=0, concat_axis=0, tiled=True)
    arrived = arrived.reshape(HEADS, halves, F, HT, half_width, HD).transpose(2, 3, 1, 4, 0, 5)
    latents = normed_latents(arrived.reshape(F * HT * W, D), proj_weight).reshape(F, HT, W, C_LAT)
    unfolded_in = unfold(extend(latents), F, HT, W)
    first = (
        jnp.dot(unfolded_in, in_weight.reshape(27 * C_LAT, CH), preferred_element_type=jnp.float32)
        + in_bias
    ).astype(jnp.bfloat16)
    active = jax.nn.silu(first.astype(jnp.float32)).astype(jnp.bfloat16)
    unfolded_mid = unfold(extend(active.reshape(F, HT, W, CH)), F, HT, W)
    piece = lax.all_gather(mid_weight, "seq", axis=4, tiled=True)
    column_span = piece.shape[4]
    middle = (
        jnp.dot(
            unfolded_mid, piece.reshape(27 * CH, column_span), preferred_element_type=jnp.float32
        )
        + mid_bias
    ).astype(jnp.bfloat16)
    summed = first.astype(jnp.float32) + middle.astype(jnp.float32)
    return shuffle_tile(summed, F, HT, W).astype(jnp.bfloat16)[None]


def dot_f32(left, right, left_dim=1, right_dim=0):
    return lax.dot_general(
        left, right, (((left_dim,), (right_dim,)), ((), ())), preferred_element_type=jnp.float32
    )


def pack_body(query_ref, key_ref, value_ref, *rest, steps, span):
    blocks, sems = rest[:-1], rest[-1]
    rank = lax.axis_index("seq")
    copies = []
    for place, step in enumerate(steps):
        start = pl.multiple_of((rank ^ step) * span, span)
        for which, ref in enumerate((query_ref, key_ref, value_ref)):
            copies.append(
                pltpu.make_async_copy(
                    ref.at[:, pl.ds(start, span)], blocks[place].at[which], sems.at[place, which]
                )
            )
    for copy in copies:
        copy.start()
    for copy in copies:
        copy.wait()


def fetch_body(proj_ref, mid_weight_ref, rows_ref, mid_ref, sems):
    span = rows_ref.shape[0]
    start = pl.multiple_of(lax.axis_index("seq") * span, span)
    copies = (
        pltpu.make_async_copy(proj_ref.at[pl.ds(start, span), :], rows_ref, sems.at[0]),
        pltpu.make_async_copy(mid_weight_ref, mid_ref, sems.at[1]),
    )
    for copy in copies:
        copy.start()
    for copy in copies:
        copy.wait()


def read_sums(ref, count):
    cells = ref.shape[0] - (2 if ref.dtype == jnp.bfloat16 else 1) * count
    parts = ref[:cells].astype(jnp.float32).reshape(count, cells // count, C_LAT)
    tail = ref[cells:].astype(jnp.float32)
    squares = tail[:count] + tail[count:] if ref.dtype == jnp.bfloat16 else tail
    return [parts[i] for i in range(count)], [squares[i : i + 1] for i in range(count)]


def write_sums(ref, parts, squares):
    cells = len(parts) * parts[0].shape[0]
    across = jnp.concatenate(squares, axis=0)
    if ref.dtype == jnp.bfloat16:
        coarse = across.astype(jnp.bfloat16).astype(jnp.float32)
        across = jnp.concatenate([coarse, across - coarse], axis=0)
    ref[:cells] = jnp.concatenate(parts, axis=0).astype(ref.dtype)
    ref[cells:] = across.astype(ref.dtype)


def attend_body(proj_ref, *rest, order):
    blocks, (keep_ref, send_ref) = rest[:-2], rest[-2:]
    devices = len(blocks)
    _, local, span = blocks[0].shape
    tokens = devices * local
    query, key, value = (
        jnp.concatenate([block[which] for block in blocks], axis=0) for which in range(3)
    )
    sharpness = math.log2(math.e) / math.sqrt(HD)
    units = [slice(first, first + HD) for first in range(0, span, HD)]
    scores = [dot_f32(query[:, lanes], key[:, lanes], 1, 1) for lanes in units]
    heads = []
    for lanes, score in zip(units, scores):
        weights = jnp.exp2((score - jnp.max(score, axis=1, keepdims=True)) * sharpness)
        totals = jnp.sum(weights, axis=1, keepdims=True)
        mixture = dot_f32(weights.astype(jnp.bfloat16), value[:, lanes])
        heads.append((mixture / totals).astype(jnp.bfloat16))
    attended = jnp.concatenate(heads, axis=1)
    widened = attended.astype(jnp.float32)
    squares = jnp.sum(widened * widened, axis=1, keepdims=True)
    partial = dot_f32(attended, proj_ref[...]).reshape(devices, local, C_LAT)
    lane = lax.broadcasted_iota(jnp.int32, (devices, local, C_LAT), 2)
    row = lax.broadcasted_iota(jnp.int32, (devices, local, C_LAT), 1)
    spread = jnp.broadcast_to(squares, (tokens, C_LAT)).reshape(devices, local, C_LAT)
    across = jnp.sum(jnp.where(lane == row, spread, 0.0), axis=1)
    for ref, first in ((keep_ref, 0), (send_ref, 1)):
        chosen = [order.index(step) for step in range(first, devices, 2)]
        write_sums(ref, [partial[i] for i in chosen], [across[i : i + 1] for i in chosen])


def fold_body(keep_ref, got_ref, next_ref, send_ref, count, split):
    parts, squares = read_sums(keep_ref, count)
    more_parts, more_squares = read_sums(got_ref, count)
    parts = [x + y for x, y in zip(parts, more_parts)]
    squares = [x + y for x, y in zip(squares, more_squares)]
    for ref, first in ((next_ref, 0), (send_ref, 1)):
        chosen = range(first, count, 2) if split else range(count)
        write_sums(ref, [parts[i] for i in chosen], [squares[i] for i in chosen])


def latents_body(keep_ref, *rest):
    gots, out_ref = rest[:-1], rest[-1]
    count = len(rest)
    local = out_ref.shape[0] // count
    parts, squares = read_sums(keep_ref, count)
    for step, got in enumerate(gots, 1):
        more_parts, more_squares = read_sums(got, count)
        parts = [parts[i] + more_parts[i ^ step] for i in range(count)]
        squares = [squares[i] + more_squares[i ^ step] for i in range(count)]
    lane = lax.broadcasted_iota(jnp.int32, (local, C_LAT), 1)
    row = lax.broadcasted_iota(jnp.int32, (local, C_LAT), 0)
    done = []
    for part, square in zip(parts, squares):
        column = jnp.sum(jnp.where(lane == row, square, 0.0), axis=1, keepdims=True)
        done.append(part * lax.rsqrt(column / D + 1e-06))
    out_ref[...] = jnp.concatenate(done, axis=0).astype(jnp.bfloat16)


def convolve_body(
    in_weight_ref, in_bias_ref, mid_weight_ref, mid_bias_ref, *rest
):
    quarters, (out_ref, latents_ref, cols) = rest[:-3], rest[-3:]
    rank = lax.axis_index("seq")
    frame = latents_ref.shape[0] // F
    count = out_ref.shape[0] // len(quarters)
    local = quarters[0].shape[0] // count
    for low, quarter in enumerate(quarters):
        for high in range(count):
            block = rank ^ (high * len(quarters) + low)
            latents_ref[pl.ds(pl.multiple_of(block * local, 16), local), :] = quarter[
                high * local : (high + 1) * local, :
            ]
    own = mid_weight_ref.shape[1] // 9
    column = lax.broadcasted_iota(jnp.int32, (frame, C_LAT), 0) % W
    for index in range(F):
        cells = latents_ref[index * frame : (index + 1) * frame, :].astype(jnp.float32)
        shifted = (
            jnp.where(column == 0, 0.0, pltpu.roll(cells, 1, 0)),
            cells,
            jnp.where(column == W - 1, 0.0, pltpu.roll(cells, frame - 1, 0)),
        )
        blank = jnp.zeros((W, C_LAT), jnp.float32)
        for col_off, moved in enumerate(shifted):
            above = jnp.concatenate([blank, moved[:-W]], axis=0)
            below = jnp.concatenate([moved[W:], blank], axis=0)
            for row_off, piece in enumerate((above, moved, below)):
                at = ((index * 3 + row_off) * 3 + col_off) * C_LAT
                cols[:, at : at + C_LAT] = piece.astype(jnp.bfloat16)
    deep = 9 * C_LAT
    firsts = []
    actives = []
    for index in range(F):
        low = (F - 1 - index) * deep
        first = (
            dot_f32(cols[...], in_weight_ref[low : low + F * deep, :]) + in_bias_ref[...]
        ).astype(jnp.bfloat16)
        wide = first.astype(jnp.float32)
        firsts.append(first)
        actives.append((wide * lax.logistic(wide)).astype(jnp.bfloat16))
    channel = lax.broadcasted_iota(jnp.int32, (own, CH), 1)
    mine = channel == lax.broadcasted_iota(jnp.int32, (own, CH), 0) + rank * own
    bias = jnp.sum(jnp.where(mine, mid_bias_ref[...], 0.0), axis=1, keepdims=True)
    chosen = jnp.where(mine, 1.0, 0.0).astype(jnp.bfloat16)
    spot = lax.broadcasted_iota(jnp.int32, (own, frame), 1)
    spot_column = spot % W
    outs = []
    for index in range(F):
        taps = sum(
            dot_f32(mid_weight_ref[source - index + 1], actives[source], 1, 1)
            for source in range(F)
        )
        total = None
        for col_off in range(3):
            merged = None
            for row_off in range(3):
                at = (row_off * 3 + col_off) * own
                piece = taps[at : at + own, :]
                if row_off == 0:
                    piece = jnp.where(spot < W, 0.0, pltpu.roll(piece, W, 1))
                elif row_off == 2:
                    piece = jnp.where(spot >= frame - W, 0.0, pltpu.roll(piece, frame - W, 1))
                merged = piece if merged is None else merged + piece
            if col_off == 0:
                merged = jnp.where(spot_column == 0, 0.0, pltpu.roll(merged, 1, 1))
            elif col_off == 2:
                merged = jnp.where(spot_column == W - 1, 0.0, pltpu.roll(merged, frame - 1, 1))
            total = merged if total is None else total + merged
        middle = (total + bias).astype(jnp.bfloat16).astype(jnp.float32)
        outs.append((dot_f32(chosen, firsts[index], 1, 1) + middle).astype(jnp.bfloat16))
    stacked = jnp.concatenate(outs, axis=0)
    source = lax.broadcasted_iota(jnp.int32, (F * own, 128), 0)
    target = lax.broadcasted_iota(jnp.int32, (F * own, 128), 1)
    inner = source % own
    place = (source // own) * own + (inner % 4) * (own // 4) + inner // 4
    moves = jnp.where(place == target % 64, 1.0, 0.0).astype(jnp.bfloat16)
    moved = dot_f32(stacked, moves, 0, 0).reshape(frame // W, W, 128)
    tail = jnp.concatenate([moved[:, 16:], jnp.zeros((frame // W, 32 - W, 128), jnp.float32)], axis=1)
    lane = lax.broadcasted_iota(jnp.int32, (frame // W, 16, 128), 2)
    out_ref[...] = jnp.where(lane < 64, moved[:, :16], tail).astype(jnp.bfloat16)


def shuffle_body(rows_ref, out_ref, wide):
    devices = rows_ref.shape[0]
    share = C_LAT // devices
    rows = rows_ref[...].astype(jnp.float32)
    lane = lax.broadcasted_iota(jnp.int32, (W, 128), 1) // share
    for index in range(F):
        for part in range(4):
            origin = (index * 4 + part) * share
            total = None
            for source in range(devices):
                shift = source * share - origin
                moved = jnp.concatenate(
                    [
                        pltpu.roll(rows[source], shift % 128, 1),
                        pltpu.roll(rows[source, : W - 16], (shift + 64) % 128, 1),
                    ],
                    axis=0,
                )
                total = moved if total is None else jnp.where(lane == source, moved, total)
            wide[index, part // 2, pl.ds(part % 2, W, stride=2), :] = total
    out_ref[0] = wide[...].astype(jnp.bfloat16)


def near(array):
    return pltpu.with_memory_space_constraint(array, pltpu.VMEM)


def far(array):
    return pltpu.with_memory_space_constraint(array, pltpu.HBM)


LOCAL = pl.BlockSpec(memory_space=pltpu.VMEM)
REMOTE = pl.BlockSpec(memory_space=pltpu.HBM)


def launch(body, outs, in_specs, operands, scratch=(), mib=8):
    return pl.pallas_call(
        body,
        out_shape=outs,
        in_specs=in_specs,
        out_specs=jax.tree.map(lambda _: LOCAL, outs),
        scratch_shapes=scratch,
        compiler_params=pltpu.CompilerParams(vmem_limit_bytes=mib << 20),
    )(*operands)


def exchange_order(devices):
    half = devices // 2
    order = [0, half]
    for step in range(1, half):
        order += [step, half + step]
    return order


def swap(array, step):
    devices = lax.axis_size("seq")
    return near(lax.ppermute(array, "seq", [(i, i ^ step) for i in range(devices)]))


def sums_shape(count, local, dtype):
    tail = 2 * count if dtype == jnp.bfloat16 else count
    return pltpu.VMEM((count * local + tail, C_LAT), dtype)


def whole_heads(
    query_rows, key_rows, value_rows, proj_weight, in_weight, in_bias, mid_weight, mid_bias
):
    devices = lax.axis_size("seq")
    local = query_rows.shape[0]
    span = D // devices
    frame = devices * local // F
    own = mid_weight.shape[4]
    order = exchange_order(devices)
    order = order[1:] + [0]
    landed = []
    for steps in (order[:2], order[2:]):
        blocks = launch(
            functools.partial(pack_body, steps=steps, span=span),
            [pltpu.VMEM((3, local, span), jnp.bfloat16)] * len(steps),
            [REMOTE] * 3,
            (far(query_rows), far(key_rows), far(value_rows)),
            [pltpu.SemaphoreType.DMA((len(steps), 3))],
        )
        landed += [swap(block, step) if step else near(block) for block, step in zip(blocks, steps)]
    proj_rows, mid_near = launch(
        fetch_body,
        [
            pltpu.VMEM((span, C_LAT), jnp.bfloat16),
            pltpu.VMEM((3, 9 * own, CH), jnp.bfloat16),
        ],
        [REMOTE] * 2,
        (
            far(proj_weight),
            far(mid_weight.transpose(0, 1, 2, 4, 3).reshape(3, 9 * own, CH)),
        ),
        [pltpu.SemaphoreType.DMA((2,))],
    )
    half = devices // 2
    quarter = devices // 4
    keep, send = launch(
        functools.partial(attend_body, order=order),
        [sums_shape(half, local, jnp.float32), sums_shape(half, local, jnp.bfloat16)],
        [LOCAL] * (1 + devices),
        (near(proj_rows), *landed),
        mib=32,
    )
    keep, send = launch(
        functools.partial(fold_body, count=half, split=True),
        [sums_shape(quarter, local, jnp.float32), sums_shape(quarter, local, jnp.bfloat16)],
        [LOCAL] * 2,
        (near(keep), swap(send, 1)),
    )
    keep, send = launch(
        functools.partial(fold_body, count=quarter, split=False),
        [sums_shape(quarter, local, jnp.float32), sums_shape(quarter, local, jnp.bfloat16)],
        [LOCAL] * 2,
        (near(keep), swap(send, 2)),
    )
    gots = []
    for step in range(1, quarter):
        gots.append(swap(send, 4 * step))
    ready = launch(
        latents_body,
        pltpu.VMEM((quarter * local, C_LAT), jnp.bfloat16),
        [LOCAL] * (1 + len(gots)),
        (near(keep), *gots),
    )
    paired = swap(ready, 2)
    columns = launch(
        convolve_body,
        pltpu.VMEM((devices, 16, 128), jnp.bfloat16),
        [LOCAL] * 8,
        (
            near(in_weight.reshape(27 * C_LAT, CH)),
            near(in_bias.reshape(1, CH)),
            near(mid_near),
            near(mid_bias.reshape(1, CH)),
            near(ready),
            swap(ready, 1),
            paired,
            swap(paired, 1),
        ),
        [
            pltpu.VMEM((devices * local, C_LAT), jnp.bfloat16),
            pltpu.VMEM((frame, F * 9 * C_LAT), jnp.bfloat16),
        ],
        32,
    )
    arrived = lax.all_to_all(columns, "seq", split_axis=0, concat_axis=0, tiled=True)
    return pl.pallas_call(
        shuffle_body,
        out_shape=jax.ShapeDtypeStruct((1, F, 2, 2 * W, C_LAT), jnp.bfloat16),
        in_specs=[LOCAL],
        out_specs=LOCAL,
        scratch_shapes=[pltpu.VMEM((F, 2, 2 * W, C_LAT), jnp.float32)],
        compiler_params=pltpu.CompilerParams(vmem_limit_bytes=8 << 20),
        name="shuffle",
    )(near(arrived))


def local_heads(devices):
    return 16 <= devices <= HEADS and devices & (devices - 1) == 0


def on_device(*operands):
    if not local_heads(lax.axis_size("seq")):
        return shared_heads(*operands)
    return whole_heads(*operands)


def solution(mesh):
    whole = jax.shard_map(
        on_device,
        mesh=mesh,
        in_specs=(
            P(("groups", "seq"), None),
            P(("groups", "seq"), None),
            P(("groups", "seq"), None),
            P(),
            P(),
            P(),
            P(None, None, None, None, "seq"),
            P(),
        ),
        out_specs=P(("groups", "seq"), None, None, None, None),
        check_vma=False,
    )
    devices = mesh.shape["seq"]
    if not local_heads(devices):
        return whole
    return whole
```

```python
import functools
import math

import jax
import jax.numpy as jnp
from jax import lax
from jax.experimental import pallas as pl
from jax.experimental.pallas import tpu as pltpu
from jax.sharding import PartitionSpec as P


D = 4096
HEADS = 32
HD = 128
C_LAT = 128
CH = 512
W = 24
F = 2
HT = 1


def padded_2(block, sides, width):
    for axis, dim in sides:
        count = lax.axis_size(axis)
        forward = [(i, i + 1) for i in range(count - 1)]
        backward = [(target, source) for source, target in forward]
        low = lax.ppermute(
            lax.slice_in_dim(block, block.shape[dim] - width, None, axis=dim), axis, forward
        )
        high = lax.ppermute(lax.slice_in_dim(block, 0, width, axis=dim), axis, backward)
        block = jnp.concatenate([low, block, high], axis=dim)
    return block


def unfold(padded, frames, height, columns):
    pieces = [
        padded[
            frame_off : frame_off + frames, row_off : row_off + height, col_off : col_off + columns
        ]
        for frame_off in range(3)
        for row_off in range(3)
        for col_off in range(3)
    ]
    return jnp.concatenate(pieces, axis=-1).reshape(frames * height * columns, -1)


def normed_latents(token_rows, proj_weight):
    widened = token_rows.astype(jnp.float32)
    normed = (
        widened * lax.rsqrt(jnp.mean(widened * widened, axis=1, keepdims=True) + 1e-06)
    ).astype(jnp.bfloat16)
    return jnp.dot(normed, proj_weight, preferred_element_type=jnp.float32).astype(jnp.bfloat16)


def extend(tile_cells):
    bordered = padded_2(tile_cells, (("seq", 1),), 1)
    return jnp.pad(bordered, ((1, 1), (0, 0), (1, 1), (0, 0)))


def shuffle_tile(summed, frames, height, columns):
    channels = summed.shape[-1] // 4
    return (
        summed.reshape(frames, height, columns, channels, 2, 2)
        .transpose(0, 1, 4, 2, 5, 3)
        .reshape(frames, 2 * height, 2 * columns, channels)
    )


def shared_heads(
    query_rows, key_rows, value_rows, proj_weight, in_weight, in_bias, mid_weight, mid_bias
):
    devices = lax.axis_size("seq")
    halves = max(1, devices // HEADS)
    unit_count = HEADS * halves // devices
    local_tokens = query_rows.shape[0]
    shard_rows = local_tokens // W
    half_width = W // halves
    score_scale = 1.0 / math.sqrt(HD)

    def by_head(rows):
        shaped = rows.reshape(local_tokens, HEADS, HD).transpose(1, 0, 2)
        shaped = jnp.broadcast_to(shaped[:, None], (HEADS, halves, local_tokens, HD))
        return shaped.reshape(devices, unit_count, local_tokens, HD)

    shaped = query_rows.reshape(shard_rows, halves, half_width, HEADS, HD).transpose(3, 1, 0, 2, 4)
    query_units = lax.all_to_all(
        shaped.reshape(devices, unit_count, shard_rows, half_width, HD),
        "seq",
        split_axis=0,
        concat_axis=0,
        tiled=True,
    )
    key_units = lax.all_to_all(by_head(key_rows), "seq", split_axis=0, concat_axis=0, tiled=True)
    value_units = lax.all_to_all(
        by_head(value_rows), "seq", split_axis=0, concat_axis=0, tiled=True
    )
    key_heads = key_units.transpose(1, 0, 2, 3).reshape(unit_count, -1, HD)
    value_heads = value_units.transpose(1, 0, 2, 3).reshape(unit_count, -1, HD)
    query_total = devices * shard_rows * half_width
    block_rows = 512 if query_total % 512 == 0 else query_total
    query_heads = (
        query_units.transpose(1, 0, 2, 3, 4)
        .reshape(unit_count, query_total // block_rows, block_rows, HD)
        .transpose(1, 0, 2, 3)
    )

    def attend(query_block):
        scores = (
            jnp.einsum("uqd,ukd->uqk", query_block, key_heads, preferred_element_type=jnp.float32)
            * score_scale
        )
        largest = jnp.max(scores, axis=2, keepdims=True)
        weights = jnp.exp(scores - largest)
        totals = jnp.sum(weights, axis=2, keepdims=True)
        mixture = jnp.einsum(
            "uqk,ukd->uqd",
            weights.astype(jnp.bfloat16),
            value_heads,
            preferred_element_type=jnp.float32,
        )
        return (mixture / totals).astype(jnp.bfloat16)

    attended = lax.map(attend, query_heads)
    attended = attended.transpose(1, 0, 2, 3).reshape(
        unit_count, devices, shard_rows, half_width, HD
    )
    arranged = attended.reshape(unit_count, F, devices, HT, half_width, HD).transpose(
        2, 0, 1, 3, 4, 5
    )
    arrived = lax.all_to_all(arranged, "seq", split_axis=0, concat_axis=0, tiled=True)
    arrived = arrived.reshape(HEADS, halves, F, HT, half_width, HD).transpose(2, 3, 1, 4, 0, 5)
    latents = normed_latents(arrived.reshape(F * HT * W, D), proj_weight).reshape(F, HT, W, C_LAT)
    unfolded_in = unfold(extend(latents), F, HT, W)
    first = (
        jnp.dot(unfolded_in, in_weight.reshape(27 * C_LAT, CH), preferred_element_type=jnp.float32)
        + in_bias
    ).astype(jnp.bfloat16)
    active = jax.nn.silu(first.astype(jnp.float32)).astype(jnp.bfloat16)
    unfolded_mid = unfold(extend(active.reshape(F, HT, W, CH)), F, HT, W)
    piece = lax.all_gather(mid_weight, "seq", axis=4, tiled=True)
    column_span = piece.shape[4]
    middle = (
        jnp.dot(
            unfolded_mid, piece.reshape(27 * CH, column_span), preferred_element_type=jnp.float32
        )
        + mid_bias
    ).astype(jnp.bfloat16)
    summed = first.astype(jnp.float32) + middle.astype(jnp.float32)
    return shuffle_tile(summed, F, HT, W).astype(jnp.bfloat16)[None]


def dot_f32(left, right, left_dim=1, right_dim=0):
    return lax.dot_general(
        left, right, (((left_dim,), (right_dim,)), ((), ())), preferred_element_type=jnp.float32
    )


def pack_body(query_ref, key_ref, value_ref, *rest, steps, span):
    blocks, sems = rest[:-1], rest[-1]
    rank = lax.axis_index("seq")
    copies = []
    for place, step in enumerate(steps):
        start = pl.multiple_of((rank ^ step) * span, span)
        for which, ref in enumerate((query_ref, key_ref, value_ref)):
            copies.append(
                pltpu.make_async_copy(
                    ref.at[:, pl.ds(start, span)], blocks[place].at[which], sems.at[place, which]
                )
            )
    for copy in copies:
        copy.start()
    for copy in copies:
        copy.wait()


def fetch_body(proj_ref, mid_weight_ref, rows_ref, mid_ref, sems):
    span = rows_ref.shape[0]
    start = pl.multiple_of(lax.axis_index("seq") * span, span)
    copies = (
        pltpu.make_async_copy(proj_ref.at[pl.ds(start, span), :], rows_ref, sems.at[0]),
        pltpu.make_async_copy(mid_weight_ref, mid_ref, sems.at[1]),
    )
    for copy in copies:
        copy.start()
    for copy in copies:
        copy.wait()


def read_sums(ref, count):
    cells = ref.shape[0] - (2 if ref.dtype == jnp.bfloat16 else 1) * count
    parts = ref[:cells].astype(jnp.float32).reshape(count, cells // count, C_LAT)
    tail = ref[cells:].astype(jnp.float32)
    squares = tail[:count] + tail[count:] if ref.dtype == jnp.bfloat16 else tail
    return [parts[i] for i in range(count)], [squares[i : i + 1] for i in range(count)]


def write_sums(ref, parts, squares):
    cells = len(parts) * parts[0].shape[0]
    across = jnp.concatenate(squares, axis=0)
    if ref.dtype == jnp.bfloat16:
        coarse = across.astype(jnp.bfloat16).astype(jnp.float32)
        across = jnp.concatenate([coarse, across - coarse], axis=0)
    ref[:cells] = jnp.concatenate(parts, axis=0).astype(ref.dtype)
    ref[cells:] = across.astype(ref.dtype)


def attend_body(proj_ref, *rest, order):
    blocks, (keep_ref, send_ref) = rest[:-2], rest[-2:]
    devices = len(blocks)
    _, local, span = blocks[0].shape
    tokens = devices * local
    query, key, value = (
        jnp.concatenate([block[which] for block in blocks], axis=0) for which in range(3)
    )
    sharpness = math.log2(math.e) / math.sqrt(HD)
    units = [slice(first, first + HD) for first in range(0, span, HD)]
    scores = [dot_f32(query[:, lanes], key[:, lanes], 1, 1) for lanes in units]
    heads = []
    for lanes, score in zip(units, scores):
        weights = jnp.exp2((score - jnp.max(score, axis=1, keepdims=True)) * sharpness)
        totals = jnp.sum(weights, axis=1, keepdims=True)
        mixture = dot_f32(weights.astype(jnp.bfloat16), value[:, lanes])
        heads.append((mixture / totals).astype(jnp.bfloat16))
    attended = jnp.concatenate(heads, axis=1)
    widened = attended.astype(jnp.float32)
    squares = jnp.sum(widened * widened, axis=1, keepdims=True)
    partial = dot_f32(attended, proj_ref[...]).reshape(devices, local, C_LAT)
    lane = lax.broadcasted_iota(jnp.int32, (devices, local, C_LAT), 2)
    row = lax.broadcasted_iota(jnp.int32, (devices, local, C_LAT), 1)
    spread = jnp.broadcast_to(squares, (tokens, C_LAT)).reshape(devices, local, C_LAT)
    across = jnp.sum(jnp.where(lane == row, spread, 0.0), axis=1)
    for ref, first in ((keep_ref, 0), (send_ref, 1)):
        chosen = [order.index(step) for step in range(first, devices, 2)]
        write_sums(ref, [partial[i] for i in chosen], [across[i : i + 1] for i in chosen])


def fold_body(keep_ref, got_ref, next_ref, send_ref, count, split):
    parts, squares = read_sums(keep_ref, count)
    more_parts, more_squares = read_sums(got_ref, count)
    parts = [x + y for x, y in zip(parts, more_parts)]
    squares = [x + y for x, y in zip(squares, more_squares)]
    for ref, first in ((next_ref, 0), (send_ref, 1)):
        chosen = range(first, count, 2) if split else range(count)
        write_sums(ref, [parts[i] for i in chosen], [squares[i] for i in chosen])


def latents_body(keep_ref, *rest):
    gots, out_ref = rest[:-1], rest[-1]
    count = len(rest)
    local = out_ref.shape[0] // count
    parts, squares = read_sums(keep_ref, count)
    for step, got in enumerate(gots, 1):
        more_parts, more_squares = read_sums(got, count)
        parts = [parts[i] + more_parts[i ^ step] for i in range(count)]
        squares = [squares[i] + more_squares[i ^ step] for i in range(count)]
    lane = lax.broadcasted_iota(jnp.int32, (local, C_LAT), 1)
    row = lax.broadcasted_iota(jnp.int32, (local, C_LAT), 0)
    done = []
    for part, square in zip(parts, squares):
        column = jnp.sum(jnp.where(lane == row, square, 0.0), axis=1, keepdims=True)
        done.append(part * lax.rsqrt(column / D + 1e-06))
    out_ref[...] = jnp.concatenate(done, axis=0).astype(jnp.bfloat16)


def convolve_body(
    in_weight_ref, in_bias_ref, mid_weight_ref, mid_bias_ref, *rest
):
    quarters, (out_ref, latents_ref, cols) = rest[:-3], rest[-3:]
    rank = lax.axis_index("seq")
    frame = latents_ref.shape[0] // F
    count = out_ref.shape[0] // len(quarters)
    local = quarters[0].shape[0] // count
    for low, quarter in enumerate(quarters):
        for high in range(count):
            block = rank ^ (high * len(quarters) + low)
            latents_ref[pl.ds(pl.multiple_of(block * local, 16), local), :] = quarter[
                high * local : (high + 1) * local, :
            ]
    own = mid_weight_ref.shape[1] // 9
    column = lax.broadcasted_iota(jnp.int32, (frame, C_LAT), 0) % W
    for index in range(F):
        cells = latents_ref[index * frame : (index + 1) * frame, :].astype(jnp.float32)
        shifted = (
            jnp.where(column == 0, 0.0, pltpu.roll(cells, 1, 0)),
            cells,
            jnp.where(column == W - 1, 0.0, pltpu.roll(cells, frame - 1, 0)),
        )
        blank = jnp.zeros((W, C_LAT), jnp.float32)
        for col_off, moved in enumerate(shifted):
            above = jnp.concatenate([blank, moved[:-W]], axis=0)
            below = jnp.concatenate([moved[W:], blank], axis=0)
            for row_off, piece in enumerate((above, moved, below)):
                at = ((index * 3 + row_off) * 3 + col_off) * C_LAT
                cols[:, at : at + C_LAT] = piece.astype(jnp.bfloat16)
    deep = 9 * C_LAT
    firsts = []
    actives = []
    for index in range(F):
        low = (F - 1 - index) * deep
        first = (
            dot_f32(cols[...], in_weight_ref[low : low + F * deep, :]) + in_bias_ref[...]
        ).astype(jnp.bfloat16)
        wide = first.astype(jnp.float32)
        firsts.append(first)
        actives.append((wide * lax.logistic(wide)).astype(jnp.bfloat16))
    channel = lax.broadcasted_iota(jnp.int32, (own, CH), 1)
    mine = channel == lax.broadcasted_iota(jnp.int32, (own, CH), 0) + rank * own
    bias = jnp.sum(jnp.where(mine, mid_bias_ref[...], 0.0), axis=1, keepdims=True)
    chosen = jnp.where(mine, 1.0, 0.0).astype(jnp.bfloat16)
    spot = lax.broadcasted_iota(jnp.int32, (own, frame), 1)
    spot_column = spot % W
    outs = []
    for index in range(F):
        taps = sum(
            dot_f32(mid_weight_ref[source - index + 1], actives[source], 1, 1)
            for source in range(F)
        )
        total = None
        for col_off in range(3):
            merged = None
            for row_off in range(3):
                at = (row_off * 3 + col_off) * own
                piece = taps[at : at + own, :]
                if row_off == 0:
                    piece = jnp.where(spot < W, 0.0, pltpu.roll(piece, W, 1))
                elif row_off == 2:
                    piece = jnp.where(spot >= frame - W, 0.0, pltpu.roll(piece, frame - W, 1))
                merged = piece if merged is None else merged + piece
            if col_off == 0:
                merged = jnp.where(spot_column == 0, 0.0, pltpu.roll(merged, 1, 1))
            elif col_off == 2:
                merged = jnp.where(spot_column == W - 1, 0.0, pltpu.roll(merged, frame - 1, 1))
            total = merged if total is None else total + merged
        middle = (total + bias).astype(jnp.bfloat16).astype(jnp.float32)
        outs.append((dot_f32(chosen, firsts[index], 1, 1) + middle).astype(jnp.bfloat16))
    stacked = jnp.concatenate(outs, axis=0)
    source = lax.broadcasted_iota(jnp.int32, (F * own, 128), 0)
    target = lax.broadcasted_iota(jnp.int32, (F * own, 128), 1)
    inner = source % own
    place = (source // own) * own + (inner % 4) * (own // 4) + inner // 4
    moves = jnp.where(place == target % 64, 1.0, 0.0).astype(jnp.bfloat16)
    moved = dot_f32(stacked, moves, 0, 0).reshape(frame // W, W, 128)
    tail = jnp.concatenate([moved[:, 16:], jnp.zeros((frame // W, 32 - W, 128), jnp.float32)], axis=1)
    lane = lax.broadcasted_iota(jnp.int32, (frame // W, 16, 128), 2)
    out_ref[...] = jnp.where(lane < 64, moved[:, :16], tail).astype(jnp.bfloat16)


def shuffle_body(rows_ref, out_ref, wide):
    devices = rows_ref.shape[0]
    share = C_LAT // devices
    rows = rows_ref[...].astype(jnp.float32)
    lane = lax.broadcasted_iota(jnp.int32, (W, 128), 1) // share
    for index in range(F):
        for part in range(4):
            origin = (index * 4 + part) * share
            total = None
            for source in range(devices):
                shift = source * share - origin
                moved = jnp.concatenate(
                    [
                        pltpu.roll(rows[source], shift % 128, 1),
                        pltpu.roll(rows[source, : W - 16], (shift + 64) % 128, 1),
                    ],
                    axis=0,
                )
                total = moved if total is None else jnp.where(lane == source, moved, total)
            wide[index, part // 2, pl.ds(part % 2, W, stride=2), :] = total
    out_ref[0] = wide[...].astype(jnp.bfloat16)


def near(array):
    return pltpu.with_memory_space_constraint(array, pltpu.VMEM)


def far(array):
    return pltpu.with_memory_space_constraint(array, pltpu.HBM)


LOCAL = pl.BlockSpec(memory_space=pltpu.VMEM)
REMOTE = pl.BlockSpec(memory_space=pltpu.HBM)


def launch(body, outs, in_specs, operands, scratch=(), mib=8):
    return pl.pallas_call(
        body,
        out_shape=outs,
        in_specs=in_specs,
        out_specs=jax.tree.map(lambda _: LOCAL, outs),
        scratch_shapes=scratch,
        compiler_params=pltpu.CompilerParams(vmem_limit_bytes=mib << 20),
    )(*operands)


def exchange_order(devices):
    half = devices // 2
    order = [0, half]
    for step in range(1, half):
        order += [step, half + step]
    return order


def swap(array, step):
    devices = lax.axis_size("seq")
    return near(lax.ppermute(array, "seq", [(i, i ^ step) for i in range(devices)]))


def sums_shape(count, local, dtype):
    tail = 2 * count if dtype == jnp.bfloat16 else count
    return pltpu.VMEM((count * local + tail, C_LAT), dtype)


def whole_heads(
    query_rows, key_rows, value_rows, proj_weight, in_weight, in_bias, mid_weight, mid_bias
):
    devices = lax.axis_size("seq")
    local = query_rows.shape[0]
    span = D // devices
    frame = devices * local // F
    own = mid_weight.shape[4]
    order = exchange_order(devices)
    order = order[1:] + [0]
    landed = []
    for steps in (order[:2], order[2:]):
        blocks = launch(
            functools.partial(pack_body, steps=steps, span=span),
            [pltpu.VMEM((3, local, span), jnp.bfloat16)] * len(steps),
            [REMOTE] * 3,
            (far(query_rows), far(key_rows), far(value_rows)),
            [pltpu.SemaphoreType.DMA((len(steps), 3))],
        )
        landed += [swap(block, step) if step else near(block) for block, step in zip(blocks, steps)]
    proj_rows, mid_near = launch(
        fetch_body,
        [
            pltpu.VMEM((span, C_LAT), jnp.bfloat16),
            pltpu.VMEM((3, 9 * own, CH), jnp.bfloat16),
        ],
        [REMOTE] * 2,
        (
            far(proj_weight),
            far(mid_weight.transpose(0, 1, 2, 4, 3).reshape(3, 9 * own, CH)),
        ),
        [pltpu.SemaphoreType.DMA((2,))],
    )
    half = devices // 2
    quarter = devices // 4
    keep, send = launch(
        functools.partial(attend_body, order=order),
        [sums_shape(half, local, jnp.float32), sums_shape(half, local, jnp.bfloat16)],
        [LOCAL] * (1 + devices),
        (near(proj_rows), *landed),
        mib=32,
    )
    keep, send = launch(
        functools.partial(fold_body, count=half, split=True),
        [sums_shape(quarter, local, jnp.float32), sums_shape(quarter, local, jnp.bfloat16)],
        [LOCAL] * 2,
        (near(keep), swap(send, 1)),
    )
    keep, send = launch(
        functools.partial(fold_body, count=quarter, split=False),
        [sums_shape(quarter, local, jnp.float32), sums_shape(quarter, local, jnp.bfloat16)],
        [LOCAL] * 2,
        (near(keep), swap(send, 2)),
    )
    gots = []
    for step in range(1, quarter):
        gots.append(swap(send, 4 * step))
    ready = launch(
        latents_body,
        pltpu.VMEM((quarter * local, C_LAT), jnp.bfloat16),
        [LOCAL] * (1 + len(gots)),
        (near(keep), *gots),
    )
    quarters = [near(ready)]
    for step in range(1, 4):
        quarters.append(swap(ready, step))
    columns = launch(
        convolve_body,
        pltpu.VMEM((devices, 16, 128), jnp.bfloat16),
        [LOCAL] * 8,
        (
            near(in_weight.reshape(27 * C_LAT, CH)),
            near(in_bias.reshape(1, CH)),
            near(mid_near),
            near(mid_bias.reshape(1, CH)),
            *quarters,
        ),
        [
            pltpu.VMEM((devices * local, C_LAT), jnp.bfloat16),
            pltpu.VMEM((frame, F * 9 * C_LAT), jnp.bfloat16),
        ],
        32,
    )
    arrived = lax.all_to_all(columns, "seq", split_axis=0, concat_axis=0, tiled=True)
    return pl.pallas_call(
        shuffle_body,
        out_shape=jax.ShapeDtypeStruct((1, F, 2, 2 * W, C_LAT), jnp.bfloat16),
        in_specs=[LOCAL],
        out_specs=LOCAL,
        scratch_shapes=[pltpu.VMEM((F, 2, 2 * W, C_LAT), jnp.float32)],
        compiler_params=pltpu.CompilerParams(vmem_limit_bytes=8 << 20),
        name="shuffle",
    )(near(arrived))


def local_heads(devices):
    return 16 <= devices <= HEADS and devices & (devices - 1) == 0


def on_device(*operands):
    if not local_heads(lax.axis_size("seq")):
        return shared_heads(*operands)
    return whole_heads(*operands)


def solution(mesh):
    whole = jax.shard_map(
        on_device,
        mesh=mesh,
        in_specs=(
            P(("groups", "seq"), None),
            P(("groups", "seq"), None),
            P(("groups", "seq"), None),
            P(),
            P(),
            P(),
            P(None, None, None, None, "seq"),
            P(),
        ),
        out_specs=P(("groups", "seq"), None, None, None, None),
        check_vma=False,
    )
    devices = mesh.shape["seq"]
    if not local_heads(devices):
        return whole
    return whole
```

```python
import functools
import math

import jax
import jax.numpy as jnp
from jax import lax
from jax.experimental import pallas as pl
from jax.experimental.pallas import tpu as pltpu
from jax.sharding import PartitionSpec as P


D = 4096
HEADS = 32
HD = 128
C_LAT = 128
CH = 512
W = 24
F = 2
HT = 1


def padded_2(block, sides, width):
    for axis, dim in sides:
        count = lax.axis_size(axis)
        forward = [(i, i + 1) for i in range(count - 1)]
        backward = [(target, source) for source, target in forward]
        low = lax.ppermute(
            lax.slice_in_dim(block, block.shape[dim] - width, None, axis=dim), axis, forward
        )
        high = lax.ppermute(lax.slice_in_dim(block, 0, width, axis=dim), axis, backward)
        block = jnp.concatenate([low, block, high], axis=dim)
    return block


def unfold(padded, frames, height, columns):
    pieces = [
        padded[
            frame_off : frame_off + frames, row_off : row_off + height, col_off : col_off + columns
        ]
        for frame_off in range(3)
        for row_off in range(3)
        for col_off in range(3)
    ]
    return jnp.concatenate(pieces, axis=-1).reshape(frames * height * columns, -1)


def normed_latents(token_rows, proj_weight):
    widened = token_rows.astype(jnp.float32)
    normed = (
        widened * lax.rsqrt(jnp.mean(widened * widened, axis=1, keepdims=True) + 1e-06)
    ).astype(jnp.bfloat16)
    return jnp.dot(normed, proj_weight, preferred_element_type=jnp.float32).astype(jnp.bfloat16)


def extend(tile_cells):
    bordered = padded_2(tile_cells, (("seq", 1),), 1)
    return jnp.pad(bordered, ((1, 1), (0, 0), (1, 1), (0, 0)))


def shuffle_tile(summed, frames, height, columns):
    channels = summed.shape[-1] // 4
    return (
        summed.reshape(frames, height, columns, channels, 2, 2)
        .transpose(0, 1, 4, 2, 5, 3)
        .reshape(frames, 2 * height, 2 * columns, channels)
    )


def shared_heads(
    query_rows, key_rows, value_rows, proj_weight, in_weight, in_bias, mid_weight, mid_bias
):
    devices = lax.axis_size("seq")
    halves = max(1, devices // HEADS)
    unit_count = HEADS * halves // devices
    local_tokens = query_rows.shape[0]
    shard_rows = local_tokens // W
    half_width = W // halves
    score_scale = 1.0 / math.sqrt(HD)

    def by_head(rows):
        shaped = rows.reshape(local_tokens, HEADS, HD).transpose(1, 0, 2)
        shaped = jnp.broadcast_to(shaped[:, None], (HEADS, halves, local_tokens, HD))
        return shaped.reshape(devices, unit_count, local_tokens, HD)

    shaped = query_rows.reshape(shard_rows, halves, half_width, HEADS, HD).transpose(3, 1, 0, 2, 4)
    query_units = lax.all_to_all(
        shaped.reshape(devices, unit_count, shard_rows, half_width, HD),
        "seq",
        split_axis=0,
        concat_axis=0,
        tiled=True,
    )
    key_units = lax.all_to_all(by_head(key_rows), "seq", split_axis=0, concat_axis=0, tiled=True)
    value_units = lax.all_to_all(
        by_head(value_rows), "seq", split_axis=0, concat_axis=0, tiled=True
    )
    key_heads = key_units.transpose(1, 0, 2, 3).reshape(unit_count, -1, HD)
    value_heads = value_units.transpose(1, 0, 2, 3).reshape(unit_count, -1, HD)
    query_total = devices * shard_rows * half_width
    block_rows = 512 if query_total % 512 == 0 else query_total
    query_heads = (
        query_units.transpose(1, 0, 2, 3, 4)
        .reshape(unit_count, query_total // block_rows, block_rows, HD)
        .transpose(1, 0, 2, 3)
    )

    def attend(query_block):
        scores = (
            jnp.einsum("uqd,ukd->uqk", query_block, key_heads, preferred_element_type=jnp.float32)
            * score_scale
        )
        largest = jnp.max(scores, axis=2, keepdims=True)
        weights = jnp.exp(scores - largest)
        totals = jnp.sum(weights, axis=2, keepdims=True)
        mixture = jnp.einsum(
            "uqk,ukd->uqd",
            weights.astype(jnp.bfloat16),
            value_heads,
            preferred_element_type=jnp.float32,
        )
        return (mixture / totals).astype(jnp.bfloat16)

    attended = lax.map(attend, query_heads)
    attended = attended.transpose(1, 0, 2, 3).reshape(
        unit_count, devices, shard_rows, half_width, HD
    )
    arranged = attended.reshape(unit_count, F, devices, HT, half_width, HD).transpose(
        2, 0, 1, 3, 4, 5
    )
    arrived = lax.all_to_all(arranged, "seq", split_axis=0, concat_axis=0, tiled=True)
    arrived = arrived.reshape(HEADS, halves, F, HT, half_width, HD).transpose(2, 3, 1, 4, 0, 5)
    latents = normed_latents(arrived.reshape(F * HT * W, D), proj_weight).reshape(F, HT, W, C_LAT)
    unfolded_in = unfold(extend(latents), F, HT, W)
    first = (
        jnp.dot(unfolded_in, in_weight.reshape(27 * C_LAT, CH), preferred_element_type=jnp.float32)
        + in_bias
    ).astype(jnp.bfloat16)
    active = jax.nn.silu(first.astype(jnp.float32)).astype(jnp.bfloat16)
    unfolded_mid = unfold(extend(active.reshape(F, HT, W, CH)), F, HT, W)
    piece = lax.all_gather(mid_weight, "seq", axis=4, tiled=True)
    column_span = piece.shape[4]
    middle = (
        jnp.dot(
            unfolded_mid, piece.reshape(27 * CH, column_span), preferred_element_type=jnp.float32
        )
        + mid_bias
    ).astype(jnp.bfloat16)
    summed = first.astype(jnp.float32) + middle.astype(jnp.float32)
    return shuffle_tile(summed, F, HT, W).astype(jnp.bfloat16)[None]


def dot_f32(left, right, left_dim=1, right_dim=0):
    return lax.dot_general(
        left, right, (((left_dim,), (right_dim,)), ((), ())), preferred_element_type=jnp.float32
    )


def pack_body(query_ref, key_ref, value_ref, *rest, steps, span):
    blocks, sems = rest[:-1], rest[-1]
    rank = lax.axis_index("seq")
    copies = []
    for place, step in enumerate(steps):
        start = pl.multiple_of((rank ^ step) * span, span)
        for which, ref in enumerate((query_ref, key_ref, value_ref)):
            copies.append(
                pltpu.make_async_copy(
                    ref.at[:, pl.ds(start, span)], blocks[place].at[which], sems.at[place, which]
                )
            )
    for copy in copies:
        copy.start()
    for copy in copies:
        copy.wait()


def fetch_body(proj_ref, mid_weight_ref, rows_ref, mid_ref, sems):
    span = rows_ref.shape[0]
    start = pl.multiple_of(lax.axis_index("seq") * span, span)
    copies = (
        pltpu.make_async_copy(proj_ref.at[pl.ds(start, span), :], rows_ref, sems.at[0]),
        pltpu.make_async_copy(mid_weight_ref, mid_ref, sems.at[1]),
    )
    for copy in copies:
        copy.start()
    for copy in copies:
        copy.wait()


def read_sums(ref, count):
    cells = ref.shape[0] - (2 if ref.dtype == jnp.bfloat16 else 1) * count
    parts = ref[:cells].astype(jnp.float32).reshape(count, cells // count, C_LAT)
    tail = ref[cells:].astype(jnp.float32)
    squares = tail[:count] + tail[count:] if ref.dtype == jnp.bfloat16 else tail
    return [parts[i] for i in range(count)], [squares[i : i + 1] for i in range(count)]


def write_sums(ref, parts, squares):
    cells = len(parts) * parts[0].shape[0]
    across = jnp.concatenate(squares, axis=0)
    if ref.dtype == jnp.bfloat16:
        coarse = across.astype(jnp.bfloat16).astype(jnp.float32)
        across = jnp.concatenate([coarse, across - coarse], axis=0)
    ref[:cells] = jnp.concatenate(parts, axis=0).astype(ref.dtype)
    ref[cells:] = across.astype(ref.dtype)


def attend_body(proj_ref, *rest, order):
    blocks, (keep_ref, send_ref) = rest[:-2], rest[-2:]
    devices = len(blocks)
    _, local, span = blocks[0].shape
    tokens = devices * local
    query, key, value = (
        jnp.concatenate([block[which] for block in blocks], axis=0) for which in range(3)
    )
    sharpness = math.log2(math.e) / math.sqrt(HD)
    units = [slice(first, first + HD) for first in range(0, span, HD)]
    scores = [dot_f32(query[:, lanes], key[:, lanes], 1, 1) for lanes in units]
    heads = []
    for lanes, score in zip(units, scores):
        weights = jnp.exp2((score - jnp.max(score, axis=1, keepdims=True)) * sharpness)
        totals = jnp.sum(weights, axis=1, keepdims=True)
        mixture = dot_f32(weights.astype(jnp.bfloat16), value[:, lanes])
        heads.append((mixture / totals).astype(jnp.bfloat16))
    attended = jnp.concatenate(heads, axis=1)
    widened = attended.astype(jnp.float32)
    squares = jnp.sum(widened * widened, axis=1, keepdims=True)
    partial = dot_f32(attended, proj_ref[...]).reshape(devices, local, C_LAT)
    lane = lax.broadcasted_iota(jnp.int32, (devices, local, C_LAT), 2)
    row = lax.broadcasted_iota(jnp.int32, (devices, local, C_LAT), 1)
    spread = jnp.broadcast_to(squares, (tokens, C_LAT)).reshape(devices, local, C_LAT)
    across = jnp.sum(jnp.where(lane == row, spread, 0.0), axis=1)
    for ref, first in ((keep_ref, 0), (send_ref, 1)):
        chosen = [order.index(step) for step in range(first, devices, 2)]
        write_sums(ref, [partial[i] for i in chosen], [across[i : i + 1] for i in chosen])


def fold_body(keep_ref, got_ref, next_ref, send_ref, count, split):
    parts, squares = read_sums(keep_ref, count)
    more_parts, more_squares = read_sums(got_ref, count)
    parts = [x + y for x, y in zip(parts, more_parts)]
    squares = [x + y for x, y in zip(squares, more_squares)]
    for ref, first in ((next_ref, 0), (send_ref, 1)):
        chosen = range(first, count, 2) if split else range(count)
        write_sums(ref, [parts[i] for i in chosen], [squares[i] for i in chosen])


def latents_body(keep_ref, *rest):
    gots, out_ref = rest[:-1], rest[-1]
    count = len(rest)
    local = out_ref.shape[0] // count
    parts, squares = read_sums(keep_ref, count)
    for step, got in enumerate(gots, 1):
        more_parts, more_squares = read_sums(got, count)
        parts = [parts[i] + more_parts[i ^ step] for i in range(count)]
        squares = [squares[i] + more_squares[i ^ step] for i in range(count)]
    lane = lax.broadcasted_iota(jnp.int32, (local, C_LAT), 1)
    row = lax.broadcasted_iota(jnp.int32, (local, C_LAT), 0)
    done = []
    for part, square in zip(parts, squares):
        column = jnp.sum(jnp.where(lane == row, square, 0.0), axis=1, keepdims=True)
        done.append(part * lax.rsqrt(column / D + 1e-06))
    out_ref[...] = jnp.concatenate(done, axis=0).astype(jnp.bfloat16)


def convolve_body(
    in_weight_ref, in_bias_ref, mid_weight_ref, mid_bias_ref, *rest
):
    quarters, (out_ref, latents_ref, cols) = rest[:-3], rest[-3:]
    rank = lax.axis_index("seq")
    frame = latents_ref.shape[0] // F
    count = out_ref.shape[0] // len(quarters)
    local = quarters[0].shape[0] // count
    for low, quarter in enumerate(quarters):
        for high in range(count):
            block = rank ^ (high * len(quarters) + low)
            latents_ref[pl.ds(pl.multiple_of(block * local, 16), local), :] = quarter[
                high * local : (high + 1) * local, :
            ]
    own = mid_weight_ref.shape[1] // 9
    column = lax.broadcasted_iota(jnp.int32, (frame, C_LAT), 0) % W
    for index in range(F):
        cells = latents_ref[index * frame : (index + 1) * frame, :].astype(jnp.float32)
        shifted = (
            jnp.where(column == 0, 0.0, pltpu.roll(cells, 1, 0)),
            cells,
            jnp.where(column == W - 1, 0.0, pltpu.roll(cells, frame - 1, 0)),
        )
        blank = jnp.zeros((W, C_LAT), jnp.float32)
        for col_off, moved in enumerate(shifted):
            above = jnp.concatenate([blank, moved[:-W]], axis=0)
            below = jnp.concatenate([moved[W:], blank], axis=0)
            for row_off, piece in enumerate((above, moved, below)):
                at = ((index * 3 + row_off) * 3 + col_off) * C_LAT
                cols[:, at : at + C_LAT] = piece.astype(jnp.bfloat16)
    deep = 9 * C_LAT
    firsts = []
    actives = []
    for index in range(F):
        low = (F - 1 - index) * deep
        first = (
            dot_f32(cols[...], in_weight_ref[low : low + F * deep, :]) + in_bias_ref[...]
        ).astype(jnp.bfloat16)
        wide = first.astype(jnp.float32)
        firsts.append(first)
        actives.append((wide * lax.logistic(wide)).astype(jnp.bfloat16))
    channel = lax.broadcasted_iota(jnp.int32, (own, CH), 1)
    mine = channel == lax.broadcasted_iota(jnp.int32, (own, CH), 0) + rank * own
    bias = jnp.sum(jnp.where(mine, mid_bias_ref[...], 0.0), axis=1, keepdims=True)
    chosen = jnp.where(mine, 1.0, 0.0).astype(jnp.bfloat16)
    spot = lax.broadcasted_iota(jnp.int32, (own, frame), 1)
    spot_column = spot % W
    outs = []
    for index in range(F):
        taps = sum(
            dot_f32(mid_weight_ref[source - index + 1], actives[source], 1, 1)
            for source in range(F)
        )
        total = None
        for col_off in range(3):
            merged = None
            for row_off in range(3):
                at = (row_off * 3 + col_off) * own
                piece = taps[at : at + own, :]
                if row_off == 0:
                    piece = jnp.where(spot < W, 0.0, pltpu.roll(piece, W, 1))
                elif row_off == 2:
                    piece = jnp.where(spot >= frame - W, 0.0, pltpu.roll(piece, frame - W, 1))
                merged = piece if merged is None else merged + piece
            if col_off == 0:
                merged = jnp.where(spot_column == 0, 0.0, pltpu.roll(merged, 1, 1))
            elif col_off == 2:
                merged = jnp.where(spot_column == W - 1, 0.0, pltpu.roll(merged, frame - 1, 1))
            total = merged if total is None else total + merged
        middle = (total + bias).astype(jnp.bfloat16).astype(jnp.float32)
        outs.append((dot_f32(chosen, firsts[index], 1, 1) + middle).astype(jnp.bfloat16))
    stacked = jnp.concatenate(outs, axis=0)
    source = lax.broadcasted_iota(jnp.int32, (F * own, 128), 0)
    target = lax.broadcasted_iota(jnp.int32, (F * own, 128), 1)
    inner = source % own
    place = (source // own) * own + (inner % 4) * (own // 4) + inner // 4
    moves = jnp.where(place == target % 64, 1.0, 0.0).astype(jnp.bfloat16)
    moved = dot_f32(stacked, moves, 0, 0).reshape(frame // W, W, 128)
    tail = jnp.concatenate([moved[:, 16:], jnp.zeros((frame // W, 32 - W, 128), jnp.float32)], axis=1)
    lane = lax.broadcasted_iota(jnp.int32, (frame // W, 16, 128), 2)
    out_ref[...] = jnp.where(lane < 64, moved[:, :16], tail).astype(jnp.bfloat16)


def shuffle_body(rows_ref, out_ref, wide):
    devices = rows_ref.shape[0]
    share = C_LAT // devices
    rows = rows_ref[...].astype(jnp.float32)
    lane = lax.broadcasted_iota(jnp.int32, (W, 128), 1) // share
    for index in range(F):
        for part in range(4):
            origin = (index * 4 + part) * share
            total = None
            for source in range(devices):
                shift = source * share - origin
                moved = jnp.concatenate(
                    [
                        pltpu.roll(rows[source], shift % 128, 1),
                        pltpu.roll(rows[source, : W - 16], (shift + 64) % 128, 1),
                    ],
                    axis=0,
                )
                total = moved if total is None else jnp.where(lane == source, moved, total)
            wide[index, part // 2, pl.ds(part % 2, W, stride=2), :] = total
    out_ref[0] = wide[...].astype(jnp.bfloat16)


def near(array):
    return pltpu.with_memory_space_constraint(array, pltpu.VMEM)


def far(array):
    return pltpu.with_memory_space_constraint(array, pltpu.HBM)


LOCAL = pl.BlockSpec(memory_space=pltpu.VMEM)
REMOTE = pl.BlockSpec(memory_space=pltpu.HBM)


def launch(body, outs, in_specs, operands, scratch=(), mib=8):
    return pl.pallas_call(
        body,
        out_shape=outs,
        in_specs=in_specs,
        out_specs=jax.tree.map(lambda _: LOCAL, outs),
        scratch_shapes=scratch,
        compiler_params=pltpu.CompilerParams(vmem_limit_bytes=mib << 20),
    )(*operands)


def exchange_order(devices):
    half, quarter = devices // 2, devices // 4
    order = [0]
    for far_step, near_step in zip(
        range(half, devices - 1), [*range(quarter, half), *range(1, quarter)]
    ):
        order += [far_step, near_step]
    return order + [devices - 1]


def swap(array, step):
    devices = lax.axis_size("seq")
    return near(lax.ppermute(array, "seq", [(i, i ^ step) for i in range(devices)]))


def sums_shape(count, local, dtype):
    tail = 2 * count if dtype == jnp.bfloat16 else count
    return pltpu.VMEM((count * local + tail, C_LAT), dtype)


def whole_heads(
    query_rows, key_rows, value_rows, proj_weight, in_weight, in_bias, mid_weight, mid_bias
):
    devices = lax.axis_size("seq")
    local = query_rows.shape[0]
    span = D // devices
    frame = devices * local // F
    own = mid_weight.shape[4]
    order = exchange_order(devices)
    order = order[1:] + [0]
    landed = []
    for steps in (order[:2], order[2:]):
        blocks = launch(
            functools.partial(pack_body, steps=steps, span=span),
            [pltpu.VMEM((3, local, span), jnp.bfloat16)] * len(steps),
            [REMOTE] * 3,
            (far(query_rows), far(key_rows), far(value_rows)),
            [pltpu.SemaphoreType.DMA((len(steps), 3))],
        )
        landed += [swap(block, step) if step else near(block) for block, step in zip(blocks, steps)]
    proj_rows, mid_near = launch(
        fetch_body,
        [
            pltpu.VMEM((span, C_LAT), jnp.bfloat16),
            pltpu.VMEM((3, 9 * own, CH), jnp.bfloat16),
        ],
        [REMOTE] * 2,
        (
            far(proj_weight),
            far(mid_weight.transpose(0, 1, 2, 4, 3).reshape(3, 9 * own, CH)),
        ),
        [pltpu.SemaphoreType.DMA((2,))],
    )
    half = devices // 2
    quarter = devices // 4
    keep, send = launch(
        functools.partial(attend_body, order=order),
        [sums_shape(half, local, jnp.float32), sums_shape(half, local, jnp.bfloat16)],
        [LOCAL] * (1 + devices),
        (near(proj_rows), *landed),
        mib=32,
    )
    keep, send = launch(
        functools.partial(fold_body, count=half, split=True),
        [sums_shape(quarter, local, jnp.float32), sums_shape(quarter, local, jnp.bfloat16)],
        [LOCAL] * 2,
        (near(keep), swap(send, 1)),
    )
    keep, send = launch(
        functools.partial(fold_body, count=quarter, split=False),
        [sums_shape(quarter, local, jnp.float32), sums_shape(quarter, local, jnp.bfloat16)],
        [LOCAL] * 2,
        (near(keep), swap(send, 2)),
    )
    gots = []
    for step in range(1, quarter):
        gots.append(swap(send, 4 * step))
    ready = launch(
        latents_body,
        pltpu.VMEM((quarter * local, C_LAT), jnp.bfloat16),
        [LOCAL] * (1 + len(gots)),
        (near(keep), *gots),
    )
    quarters = [near(ready)]
    for step in range(1, 4):
        quarters.append(swap(ready, step))
    columns = launch(
        convolve_body,
        pltpu.VMEM((devices, 16, 128), jnp.bfloat16),
        [LOCAL] * 8,
        (
            near(in_weight.reshape(27 * C_LAT, CH)),
            near(in_bias.reshape(1, CH)),
            near(mid_near),
            near(mid_bias.reshape(1, CH)),
            *quarters,
        ),
        [
            pltpu.VMEM((devices * local, C_LAT), jnp.bfloat16),
            pltpu.VMEM((frame, F * 9 * C_LAT), jnp.bfloat16),
        ],
        32,
    )
    arrived = lax.all_to_all(columns, "seq", split_axis=0, concat_axis=0, tiled=True)
    return pl.pallas_call(
        shuffle_body,
        out_shape=jax.ShapeDtypeStruct((1, F, 2, 2 * W, C_LAT), jnp.bfloat16),
        in_specs=[LOCAL],
        out_specs=LOCAL,
        scratch_shapes=[pltpu.VMEM((F, 2, 2 * W, C_LAT), jnp.float32)],
        compiler_params=pltpu.CompilerParams(vmem_limit_bytes=8 << 20),
        name="shuffle",
    )(near(arrived))


def local_heads(devices):
    return 16 <= devices <= HEADS and devices & (devices - 1) == 0


def on_device(*operands):
    if not local_heads(lax.axis_size("seq")):
        return shared_heads(*operands)
    return whole_heads(*operands)


def solution(mesh):
    whole = jax.shard_map(
        on_device,
        mesh=mesh,
        in_specs=(
            P(("groups", "seq"), None),
            P(("groups", "seq"), None),
            P(("groups", "seq"), None),
            P(),
            P(),
            P(),
            P(None, None, None, None, "seq"),
            P(),
        ),
        out_specs=P(("groups", "seq"), None, None, None, None),
        check_vma=False,
    )
    devices = mesh.shape["seq"]
    if not local_heads(devices):
        return whole
    return whole
```

```python
import functools
import math

import jax
import jax.numpy as jnp
from jax import lax
from jax.experimental import pallas as pl
from jax.experimental.pallas import tpu as pltpu
from jax.sharding import PartitionSpec as P


D = 4096
HEADS = 32
HD = 128
C_LAT = 128
CH = 512
W = 24
F = 2
HT = 1


def padded_2(block, sides, width):
    for axis, dim in sides:
        count = lax.axis_size(axis)
        forward = [(i, i + 1) for i in range(count - 1)]
        backward = [(target, source) for source, target in forward]
        low = lax.ppermute(
            lax.slice_in_dim(block, block.shape[dim] - width, None, axis=dim), axis, forward
        )
        high = lax.ppermute(lax.slice_in_dim(block, 0, width, axis=dim), axis, backward)
        block = jnp.concatenate([low, block, high], axis=dim)
    return block


def unfold(padded, frames, height, columns):
    pieces = [
        padded[
            frame_off : frame_off + frames, row_off : row_off + height, col_off : col_off + columns
        ]
        for frame_off in range(3)
        for row_off in range(3)
        for col_off in range(3)
    ]
    return jnp.concatenate(pieces, axis=-1).reshape(frames * height * columns, -1)


def normed_latents(token_rows, proj_weight):
    widened = token_rows.astype(jnp.float32)
    normed = (
        widened * lax.rsqrt(jnp.mean(widened * widened, axis=1, keepdims=True) + 1e-06)
    ).astype(jnp.bfloat16)
    return jnp.dot(normed, proj_weight, preferred_element_type=jnp.float32).astype(jnp.bfloat16)


def extend(tile_cells):
    bordered = padded_2(tile_cells, (("seq", 1),), 1)
    return jnp.pad(bordered, ((1, 1), (0, 0), (1, 1), (0, 0)))


def shuffle_tile(summed, frames, height, columns):
    channels = summed.shape[-1] // 4
    return (
        summed.reshape(frames, height, columns, channels, 2, 2)
        .transpose(0, 1, 4, 2, 5, 3)
        .reshape(frames, 2 * height, 2 * columns, channels)
    )


def shared_heads(
    query_rows, key_rows, value_rows, proj_weight, in_weight, in_bias, mid_weight, mid_bias
):
    devices = lax.axis_size("seq")
    halves = max(1, devices // HEADS)
    unit_count = HEADS * halves // devices
    local_tokens = query_rows.shape[0]
    shard_rows = local_tokens // W
    half_width = W // halves
    score_scale = 1.0 / math.sqrt(HD)

    def by_head(rows):
        shaped = rows.reshape(local_tokens, HEADS, HD).transpose(1, 0, 2)
        shaped = jnp.broadcast_to(shaped[:, None], (HEADS, halves, local_tokens, HD))
        return shaped.reshape(devices, unit_count, local_tokens, HD)

    shaped = query_rows.reshape(shard_rows, halves, half_width, HEADS, HD).transpose(3, 1, 0, 2, 4)
    query_units = lax.all_to_all(
        shaped.reshape(devices, unit_count, shard_rows, half_width, HD),
        "seq",
        split_axis=0,
        concat_axis=0,
        tiled=True,
    )
    key_units = lax.all_to_all(by_head(key_rows), "seq", split_axis=0, concat_axis=0, tiled=True)
    value_units = lax.all_to_all(
        by_head(value_rows), "seq", split_axis=0, concat_axis=0, tiled=True
    )
    key_heads = key_units.transpose(1, 0, 2, 3).reshape(unit_count, -1, HD)
    value_heads = value_units.transpose(1, 0, 2, 3).reshape(unit_count, -1, HD)
    query_total = devices * shard_rows * half_width
    block_rows = 512 if query_total % 512 == 0 else query_total
    query_heads = (
        query_units.transpose(1, 0, 2, 3, 4)
        .reshape(unit_count, query_total // block_rows, block_rows, HD)
        .transpose(1, 0, 2, 3)
    )

    def attend(query_block):
        scores = (
            jnp.einsum("uqd,ukd->uqk", query_block, key_heads, preferred_element_type=jnp.float32)
            * score_scale
        )
        largest = jnp.max(scores, axis=2, keepdims=True)
        weights = jnp.exp(scores - largest)
        totals = jnp.sum(weights, axis=2, keepdims=True)
        mixture = jnp.einsum(
            "uqk,ukd->uqd",
            weights.astype(jnp.bfloat16),
            value_heads,
            preferred_element_type=jnp.float32,
        )
        return (mixture / totals).astype(jnp.bfloat16)

    attended = lax.map(attend, query_heads)
    attended = attended.transpose(1, 0, 2, 3).reshape(
        unit_count, devices, shard_rows, half_width, HD
    )
    arranged = attended.reshape(unit_count, F, devices, HT, half_width, HD).transpose(
        2, 0, 1, 3, 4, 5
    )
    arrived = lax.all_to_all(arranged, "seq", split_axis=0, concat_axis=0, tiled=True)
    arrived = arrived.reshape(HEADS, halves, F, HT, half_width, HD).transpose(2, 3, 1, 4, 0, 5)
    latents = normed_latents(arrived.reshape(F * HT * W, D), proj_weight).reshape(F, HT, W, C_LAT)
    unfolded_in = unfold(extend(latents), F, HT, W)
    first = (
        jnp.dot(unfolded_in, in_weight.reshape(27 * C_LAT, CH), preferred_element_type=jnp.float32)
        + in_bias
    ).astype(jnp.bfloat16)
    active = jax.nn.silu(first.astype(jnp.float32)).astype(jnp.bfloat16)
    unfolded_mid = unfold(extend(active.reshape(F, HT, W, CH)), F, HT, W)
    piece = lax.all_gather(mid_weight, "seq", axis=4, tiled=True)
    column_span = piece.shape[4]
    middle = (
        jnp.dot(
            unfolded_mid, piece.reshape(27 * CH, column_span), preferred_element_type=jnp.float32
        )
        + mid_bias
    ).astype(jnp.bfloat16)
    summed = first.astype(jnp.float32) + middle.astype(jnp.float32)
    return shuffle_tile(summed, F, HT, W).astype(jnp.bfloat16)[None]


def dot_f32(left, right, left_dim=1, right_dim=0):
    return lax.dot_general(
        left, right, (((left_dim,), (right_dim,)), ((), ())), preferred_element_type=jnp.float32
    )


def pack_body(query_ref, key_ref, value_ref, *rest, steps, span):
    blocks, sems = rest[:-1], rest[-1]
    rank = lax.axis_index("seq")
    copies = []
    for place, step in enumerate(steps):
        start = pl.multiple_of((rank ^ step) * span, span)
        for which, ref in enumerate((query_ref, key_ref, value_ref)):
            copies.append(
                pltpu.make_async_copy(
                    ref.at[:, pl.ds(start, span)], blocks[place].at[which], sems.at[place, which]
                )
            )
    for copy in copies:
        copy.start()
    for copy in copies:
        copy.wait()


def fetch_body(proj_ref, mid_weight_ref, rows_ref, mid_ref, sems):
    span = rows_ref.shape[0]
    start = pl.multiple_of(lax.axis_index("seq") * span, span)
    copies = (
        pltpu.make_async_copy(proj_ref.at[pl.ds(start, span), :], rows_ref, sems.at[0]),
        pltpu.make_async_copy(mid_weight_ref, mid_ref, sems.at[1]),
    )
    for copy in copies:
        copy.start()
    for copy in copies:
        copy.wait()


def read_sums(ref, count):
    cells = ref.shape[0] - (2 if ref.dtype == jnp.bfloat16 else 1) * count
    parts = ref[:cells].astype(jnp.float32).reshape(count, cells // count, C_LAT)
    tail = ref[cells:].astype(jnp.float32)
    squares = tail[:count] + tail[count:] if ref.dtype == jnp.bfloat16 else tail
    return [parts[i] for i in range(count)], [squares[i : i + 1] for i in range(count)]


def write_sums(ref, parts, squares):
    cells = len(parts) * parts[0].shape[0]
    across = jnp.concatenate(squares, axis=0)
    if ref.dtype == jnp.bfloat16:
        coarse = across.astype(jnp.bfloat16).astype(jnp.float32)
        across = jnp.concatenate([coarse, across - coarse], axis=0)
    ref[:cells] = jnp.concatenate(parts, axis=0).astype(ref.dtype)
    ref[cells:] = across.astype(ref.dtype)


def attend_body(proj_ref, *rest, order):
    blocks, (keep_ref, send_ref) = rest[:-2], rest[-2:]
    devices = len(blocks)
    _, local, span = blocks[0].shape
    tokens = devices * local
    query, key, value = (
        jnp.concatenate([block[which] for block in blocks], axis=0) for which in range(3)
    )
    sharpness = math.log2(math.e) / math.sqrt(HD)
    units = [slice(first, first + HD) for first in range(0, span, HD)]
    scores = [dot_f32(query[:, lanes], key[:, lanes], 1, 1) for lanes in units]
    heads = []
    for lanes, score in zip(units, scores):
        weights = jnp.exp2((score - jnp.max(score, axis=1, keepdims=True)) * sharpness)
        totals = jnp.sum(weights, axis=1, keepdims=True)
        mixture = dot_f32(weights.astype(jnp.bfloat16), value[:, lanes])
        heads.append((mixture / totals).astype(jnp.bfloat16))
    attended = jnp.concatenate(heads, axis=1)
    widened = attended.astype(jnp.float32)
    squares = jnp.sum(widened * widened, axis=1, keepdims=True)
    partial = dot_f32(attended, proj_ref[...]).reshape(devices, local, C_LAT)
    lane = lax.broadcasted_iota(jnp.int32, (devices, local, C_LAT), 2)
    row = lax.broadcasted_iota(jnp.int32, (devices, local, C_LAT), 1)
    spread = jnp.broadcast_to(squares, (tokens, C_LAT)).reshape(devices, local, C_LAT)
    across = jnp.sum(jnp.where(lane == row, spread, 0.0), axis=1)
    for ref, first in ((keep_ref, 0), (send_ref, 1)):
        chosen = [order.index(step) for step in range(first, devices, 2)]
        write_sums(ref, [partial[i] for i in chosen], [across[i : i + 1] for i in chosen])


def fold_body(keep_ref, got_ref, next_ref, send_ref, count, split):
    parts, squares = read_sums(keep_ref, count)
    more_parts, more_squares = read_sums(got_ref, count)
    parts = [x + y for x, y in zip(parts, more_parts)]
    squares = [x + y for x, y in zip(squares, more_squares)]
    for ref, first in ((next_ref, 0), (send_ref, 1)):
        chosen = range(first, count, 2) if split else range(count)
        write_sums(ref, [parts[i] for i in chosen], [squares[i] for i in chosen])


def latents_body(keep_ref, *rest):
    gots, out_ref = rest[:-1], rest[-1]
    count = len(rest)
    local = out_ref.shape[0] // count
    parts, squares = read_sums(keep_ref, count)
    for step, got in enumerate(gots, 1):
        more_parts, more_squares = read_sums(got, count)
        parts = [parts[i] + more_parts[i ^ step] for i in range(count)]
        squares = [squares[i] + more_squares[i ^ step] for i in range(count)]
    lane = lax.broadcasted_iota(jnp.int32, (local, C_LAT), 1)
    row = lax.broadcasted_iota(jnp.int32, (local, C_LAT), 0)
    done = []
    for part, square in zip(parts, squares):
        column = jnp.sum(jnp.where(lane == row, square, 0.0), axis=1, keepdims=True)
        done.append(part * lax.rsqrt(column / D + 1e-06))
    out_ref[...] = jnp.concatenate(done, axis=0).astype(jnp.bfloat16)


def convolve_body(
    in_weight_ref, in_bias_ref, mid_weight_ref, mid_bias_ref, *rest
):
    quarters, (out_ref, latents_ref, cols) = rest[:-3], rest[-3:]
    rank = lax.axis_index("seq")
    frame = latents_ref.shape[0] // F
    count = out_ref.shape[0] // len(quarters)
    local = quarters[0].shape[0] // count
    for low, quarter in enumerate(quarters):
        for high in range(count):
            block = rank ^ (high * len(quarters) + low)
            latents_ref[pl.ds(pl.multiple_of(block * local, 16), local), :] = quarter[
                high * local : (high + 1) * local, :
            ]
    own = mid_weight_ref.shape[1] // 9
    column = lax.broadcasted_iota(jnp.int32, (frame, C_LAT), 0) % W
    for index in range(F):
        cells = latents_ref[index * frame : (index + 1) * frame, :].astype(jnp.float32)
        shifted = (
            jnp.where(column == 0, 0.0, pltpu.roll(cells, 1, 0)),
            cells,
            jnp.where(column == W - 1, 0.0, pltpu.roll(cells, frame - 1, 0)),
        )
        blank = jnp.zeros((W, C_LAT), jnp.float32)
        for col_off, moved in enumerate(shifted):
            above = jnp.concatenate([blank, moved[:-W]], axis=0)
            below = jnp.concatenate([moved[W:], blank], axis=0)
            for row_off, piece in enumerate((above, moved, below)):
                at = ((index * 3 + row_off) * 3 + col_off) * C_LAT
                cols[:, at : at + C_LAT] = piece.astype(jnp.bfloat16)
    deep = 9 * C_LAT
    products = []
    for index in range(F):
        low = (F - 1 - index) * deep
        products.append(dot_f32(cols[...], in_weight_ref[low : low + F * deep, :]))
    firsts = [(product + in_bias_ref[...]).astype(jnp.bfloat16) for product in products]
    actives = []
    for first in firsts:
        wide = first.astype(jnp.float32)
        actives.append((wide * lax.logistic(wide)).astype(jnp.bfloat16))
    channel = lax.broadcasted_iota(jnp.int32, (own, CH), 1)
    mine = channel == lax.broadcasted_iota(jnp.int32, (own, CH), 0) + rank * own
    bias = jnp.sum(jnp.where(mine, mid_bias_ref[...], 0.0), axis=1, keepdims=True)
    chosen = jnp.where(mine, 1.0, 0.0).astype(jnp.bfloat16)
    spot = lax.broadcasted_iota(jnp.int32, (own, frame), 1)
    spot_column = spot % W
    outs = []
    for index in range(F):
        taps = sum(
            dot_f32(mid_weight_ref[source - index + 1], actives[source], 1, 1)
            for source in range(F)
        )
        total = None
        for col_off in range(3):
            merged = None
            for row_off in range(3):
                at = (row_off * 3 + col_off) * own
                piece = taps[at : at + own, :]
                if row_off == 0:
                    piece = jnp.where(spot < W, 0.0, pltpu.roll(piece, W, 1))
                elif row_off == 2:
                    piece = jnp.where(spot >= frame - W, 0.0, pltpu.roll(piece, frame - W, 1))
                merged = piece if merged is None else merged + piece
            if col_off == 0:
                merged = jnp.where(spot_column == 0, 0.0, pltpu.roll(merged, 1, 1))
            elif col_off == 2:
                merged = jnp.where(spot_column == W - 1, 0.0, pltpu.roll(merged, frame - 1, 1))
            total = merged if total is None else total + merged
        middle = (total + bias).astype(jnp.bfloat16).astype(jnp.float32)
        outs.append((dot_f32(chosen, firsts[index], 1, 1) + middle).astype(jnp.bfloat16))
    stacked = jnp.concatenate(outs, axis=0)
    source = lax.broadcasted_iota(jnp.int32, (F * own, 128), 0)
    target = lax.broadcasted_iota(jnp.int32, (F * own, 128), 1)
    inner = source % own
    place = (source // own) * own + (inner % 4) * (own // 4) + inner // 4
    moves = jnp.where(place == target % 64, 1.0, 0.0).astype(jnp.bfloat16)
    moved = dot_f32(stacked, moves, 0, 0).reshape(frame // W, W, 128)
    tail = jnp.concatenate([moved[:, 16:], jnp.zeros((frame // W, 32 - W, 128), jnp.float32)], axis=1)
    lane = lax.broadcasted_iota(jnp.int32, (frame // W, 16, 128), 2)
    out_ref[...] = jnp.where(lane < 64, moved[:, :16], tail).astype(jnp.bfloat16)


def shuffle_body(rows_ref, out_ref, wide):
    devices = rows_ref.shape[0]
    share = C_LAT // devices
    rows = rows_ref[...].astype(jnp.float32)
    lane = lax.broadcasted_iota(jnp.int32, (W, 128), 1) // share
    for index in range(F):
        for part in range(4):
            origin = (index * 4 + part) * share
            total = None
            for source in range(devices):
                shift = source * share - origin
                moved = jnp.concatenate(
                    [
                        pltpu.roll(rows[source], shift % 128, 1),
                        pltpu.roll(rows[source, : W - 16], (shift + 64) % 128, 1),
                    ],
                    axis=0,
                )
                total = moved if total is None else jnp.where(lane == source, moved, total)
            wide[index, part // 2, pl.ds(part % 2, W, stride=2), :] = total
    out_ref[0] = wide[...].astype(jnp.bfloat16)


def near(array):
    return pltpu.with_memory_space_constraint(array, pltpu.VMEM)


def far(array):
    return pltpu.with_memory_space_constraint(array, pltpu.HBM)


LOCAL = pl.BlockSpec(memory_space=pltpu.VMEM)
REMOTE = pl.BlockSpec(memory_space=pltpu.HBM)


def launch(body, outs, in_specs, operands, scratch=(), mib=8):
    return pl.pallas_call(
        body,
        out_shape=outs,
        in_specs=in_specs,
        out_specs=jax.tree.map(lambda _: LOCAL, outs),
        scratch_shapes=scratch,
        compiler_params=pltpu.CompilerParams(vmem_limit_bytes=mib << 20),
    )(*operands)


def exchange_order(devices):
    half = devices // 2
    order = [0, half]
    for step in range(1, half):
        order += [step, half + step]
    return order


def swap(array, step):
    devices = lax.axis_size("seq")
    return near(lax.ppermute(array, "seq", [(i, i ^ step) for i in range(devices)]))


def sums_shape(count, local, dtype):
    tail = 2 * count if dtype == jnp.bfloat16 else count
    return pltpu.VMEM((count * local + tail, C_LAT), dtype)


def whole_heads(
    query_rows, key_rows, value_rows, proj_weight, in_weight, in_bias, mid_weight, mid_bias
):
    devices = lax.axis_size("seq")
    local = query_rows.shape[0]
    span = D // devices
    frame = devices * local // F
    own = mid_weight.shape[4]
    order = exchange_order(devices)
    order = order[1:] + [0]
    landed = []
    for steps in (order[:2], order[2:]):
        blocks = launch(
            functools.partial(pack_body, steps=steps, span=span),
            [pltpu.VMEM((3, local, span), jnp.bfloat16)] * len(steps),
            [REMOTE] * 3,
            (far(query_rows), far(key_rows), far(value_rows)),
            [pltpu.SemaphoreType.DMA((len(steps), 3))],
        )
        landed += [swap(block, step) if step else near(block) for block, step in zip(blocks, steps)]
    proj_rows, mid_near = launch(
        fetch_body,
        [
            pltpu.VMEM((span, C_LAT), jnp.bfloat16),
            pltpu.VMEM((3, 9 * own, CH), jnp.bfloat16),
        ],
        [REMOTE] * 2,
        (
            far(proj_weight),
            far(mid_weight.transpose(0, 1, 2, 4, 3).reshape(3, 9 * own, CH)),
        ),
        [pltpu.SemaphoreType.DMA((2,))],
    )
    half = devices // 2
    quarter = devices // 4
    keep, send = launch(
        functools.partial(attend_body, order=order),
        [sums_shape(half, local, jnp.float32), sums_shape(half, local, jnp.bfloat16)],
        [LOCAL] * (1 + devices),
        (near(proj_rows), *landed),
        mib=32,
    )
    keep, send = launch(
        functools.partial(fold_body, count=half, split=True),
        [sums_shape(quarter, local, jnp.float32), sums_shape(quarter, local, jnp.bfloat16)],
        [LOCAL] * 2,
        (near(keep), swap(send, 1)),
    )
    keep, send = launch(
        functools.partial(fold_body, count=quarter, split=False),
        [sums_shape(quarter, local, jnp.float32), sums_shape(quarter, local, jnp.bfloat16)],
        [LOCAL] * 2,
        (near(keep), swap(send, 2)),
    )
    gots = []
    for step in range(1, quarter):
        gots.append(swap(send, 4 * step))
    ready = launch(
        latents_body,
        pltpu.VMEM((quarter * local, C_LAT), jnp.bfloat16),
        [LOCAL] * (1 + len(gots)),
        (near(keep), *gots),
    )
    quarters = [near(ready)]
    for step in range(1, 4):
        quarters.append(swap(ready, step))
    columns = launch(
        convolve_body,
        pltpu.VMEM((devices, 16, 128), jnp.bfloat16),
        [LOCAL] * 8,
        (
            near(in_weight.reshape(27 * C_LAT, CH)),
            near(in_bias.reshape(1, CH)),
            near(mid_near),
            near(mid_bias.reshape(1, CH)),
            *quarters,
        ),
        [
            pltpu.VMEM((devices * local, C_LAT), jnp.bfloat16),
            pltpu.VMEM((frame, F * 9 * C_LAT), jnp.bfloat16),
        ],
        32,
    )
    arrived = lax.all_to_all(columns, "seq", split_axis=0, concat_axis=0, tiled=True)
    return pl.pallas_call(
        shuffle_body,
        out_shape=jax.ShapeDtypeStruct((1, F, 2, 2 * W, C_LAT), jnp.bfloat16),
        in_specs=[LOCAL],
        out_specs=LOCAL,
        scratch_shapes=[pltpu.VMEM((F, 2, 2 * W, C_LAT), jnp.float32)],
        compiler_params=pltpu.CompilerParams(vmem_limit_bytes=8 << 20),
        name="shuffle",
    )(near(arrived))


def local_heads(devices):
    return 16 <= devices <= HEADS and devices & (devices - 1) == 0


def on_device(*operands):
    if not local_heads(lax.axis_size("seq")):
        return shared_heads(*operands)
    return whole_heads(*operands)


def solution(mesh):
    whole = jax.shard_map(
        on_device,
        mesh=mesh,
        in_specs=(
            P(("groups", "seq"), None),
            P(("groups", "seq"), None),
            P(("groups", "seq"), None),
            P(),
            P(),
            P(),
            P(None, None, None, None, "seq"),
            P(),
        ),
        out_specs=P(("groups", "seq"), None, None, None, None),
        check_vma=False,
    )
    devices = mesh.shape["seq"]
    if not local_heads(devices):
        return whole
    return whole
```
